32 devices in a mesh: section: 2 (over core), dp: 4 (over y, x), tensor: 4 (over z).
Axes of the slice: x: 2, y: 2, z: 4, core: 2. Of those that a mesh axis runs over, the one named last changes fastest.
Arguments:
- inputs: bfloat16 [4, 4, 1024, 1024], P('dp', None, 'tensor'), may hold values from -6 to 6
- segments: int32 [4, 4, 1024], P('dp'), may hold values from 0 to 3, never falling along the last dimension, each value on 1 to 512 neighbouring positions
- projection_in: bfloat16 [2, 1024, 3, 1024], P('section', None, None, 'tensor'), may hold values from -0.1875 to 0.1875
- projection_out: bfloat16 [2, 1024, 1024], P('section', 'tensor'), may hold values from -0.1875 to 0.1875
- up_weight: bfloat16 [2, 1024, 4096], P('section', None, 'tensor'), may hold values from -0.1875 to 0.1875
- down_weight: bfloat16 [2, 4096, 1024], P('section', 'tensor'), may hold values from -0.09375 to 0.09375
- norm_gains: float32 [2, 4, 1024], P('section'), may hold values from 0.25 to 1.75
- cotangent: bfloat16 [4, 4, 1024, 1024], P('dp', None, 'tensor'), may hold values from -6 to 6
Outputs:
- layer_outputs: bfloat16 [2, 4, 4, 1024, 1024], P('section', 'dp', None, 'tensor')
- input_grads: bfloat16 [2, 4, 4, 1024, 1024], P('section', 'dp', None, 'tensor')
- projection_in_grad: float32 [2, 1024, 3, 1024], P('section', None, None, 'tensor')
- projection_out_grad: float32 [2, 1024, 1024], P('section', 'tensor')
- up_grad: float32 [2, 1024, 4096], P('section', None, 'tensor')
- down_grad: float32 [2, 4096, 1024], P('section', 'tensor')
- gains_grad: float32 [2, 4, 1024], P('section')
The draws below stay inside these ranges and needn't reach their ends.
Inputs may be any that keep to these rules, and one draw needn't show every extreme that they name: `segments`: in each pack of 1024 positions the segment numbers never fall; a number covers one document of at most 512 positions, and one document has exactly that many.
All inputs are finite; a program needn't handle non-finite values.
Results may differ from the reference program's by a relative error of at most 0.025.
Values may be sent and summed in bfloat16 or wider, within the bound.
No kernel may reach another device: no remote copies, remote signals or barrier semaphores. Data moves between devices by JAX's collectives and lax.ppermute only.
A program may use at most 320 MiB of HBM per device.

```python
import math
import jax
import jax.numpy as jnp
import numpy as np
from jax import lax

D = 1024
HEADS = 16
HEAD_DIM = 64
FF = 4096
MB_TOK = 1024
MICRO = 4
QBLOCK = 512
N_DP = 4


def block_levels(stream_key, extent, cuts, least, top_value):
    level = 1.0
    for axis_at, shards_of in cuts:
        draws = jax.random.uniform(jax.random.fold_in(jax.random.fold_in(stream_key, 6), axis_at), (shards_of,), jnp.float32, least / len(cuts), top_value / len(cuts))
        level = level * jnp.repeat(jnp.exp(draws), extent[axis_at] // shards_of).reshape((-1,) + (1,) * (len(extent) - 1 - axis_at))
    return level


def profile(number_of, total, limit, lean):
    portions = [(1 << 20) // math.isqrt(standing ** lean) + 1 for standing in range(2, number_of + 1)]
    surplus, given = total - limit - (number_of - 1), [1] * (number_of - 1)
    while surplus > 0:
        candidates = [i for i in range(number_of - 1) if given[i] < limit]
        mass, left = sum([portions[i] for i in candidates]), surplus
        for i in candidates:
            extra = min(limit - given[i], max(1, left * portions[i] // mass), surplus)
            given[i] = given[i] + extra
            surplus = surplus - extra
    return np.array([limit] + given)


def uneven(rng, amount, total, limit, lean):
    if amount == 2:
        one = jax.random.randint(rng, (), max(1, total - limit), min(limit, total - 1) + 1)
        return jnp.stack([one, total - one])
    tallies = jnp.asarray(profile(amount, total, limit, lean), jnp.int32)
    pairs = (amount - 1) // 2
    source_of, receiver = tallies[1:1 + 2 * pairs:2], tallies[2:2 + 2 * pairs:2]
    margin = jnp.minimum(source_of - 1, limit - receiver)
    shifted = jax.random.randint(jax.random.fold_in(rng, 1), (pairs,), 0, 1 << 20) % (margin + 1)
    tallies = tallies.at[1:1 + 2 * pairs:2].set(source_of - shifted).at[2:2 + 2 * pairs:2].set(receiver + shifted)
    return tallies[jax.random.permutation(jax.random.fold_in(rng, 2), amount)]


def centred(stream_key, shape, scale, limit, shards=(), held_as=jnp.bfloat16):
    values = jax.random.normal(stream_key, shape, jnp.float32) * scale
    if len(shards) > 0:
        values = block_levels(stream_key, shape, shards, -0.22, 0.18) * values
    return jnp.clip(values, min=-limit, max=limit).astype(held_as)


def setup_inputs(seed: int = 0) -> dict:
    splits = jax.random.split(jax.random.key(seed), 9)
    return {
        "inputs": centred(splits[0], (N_DP, MICRO, MB_TOK, D), 1.0, 6.0, ((0, 4), (2, 4))),
        "segments": jax.vmap(lambda own: jnp.searchsorted(jnp.cumsum(uneven(own, 4, MB_TOK, MB_TOK // 2, 2)), jnp.arange(MB_TOK), side="right"))(jax.random.split(splits[1], N_DP * MICRO)).reshape((N_DP, MICRO, MB_TOK)).astype(jnp.int32),
        "projection_in": centred(splits[2], (2, D, 3, HEADS * HEAD_DIM), D ** -0.5, 0.1875, ((0, 2), (3, 4))),
        "projection_out": centred(splits[3], (2, HEADS * HEAD_DIM, D), (HEADS * HEAD_DIM) ** -0.5, 0.1875, ((0, 2), (1, 4))),
        "up_weight": centred(splits[4], (2, D, FF), D ** -0.5, 0.1875, ((0, 2), (2, 4))),
        "down_weight": centred(splits[5], (2, FF, D), FF ** -0.5, 0.09375, ((0, 2), (1, 4))),
        "norm_gains": jnp.clip(1.0 + 0.15 * jax.random.normal(splits[6], (2, 4, D), jnp.float32), 0.25, 1.75),
        "cotangent": centred(splits[7], (N_DP, MICRO, MB_TOK, D), 1.0, 6.0, ((0, 4), (2, 4))),
    }


@jax.custom_vjp
def low(v):
    return lax.optimization_barrier(v.astype(jnp.bfloat16)).astype(jnp.float32)

@jax.custom_vjp
def low_back(v):
    return v

def low_keep(v):
    return (low(v), None)

def low_pass(kept, grad):
    return (grad,)

def back_keep(v):
    return (v, None)

def back_low(kept, grad):
    return (low(grad),)
low.defvjp(low_keep, low_pass)
low_back.defvjp(back_keep, back_low)
EPSILON = 1e-05
ROTARY_BASE = 10000.0
NEGATIVE = -1e+30
HIGHEST = lax.Precision.HIGHEST

def rms_norm(values, gain):
    return values * lax.rsqrt(lax.optimization_barrier(jnp.mean(values * values, axis=-1, keepdims=True)) + EPSILON) * gain

def rotary_tables(length):
    half = HEAD_DIM // 2
    freqs = ROTARY_BASE ** (-2.0 * jnp.arange(half, dtype=jnp.float32) / HEAD_DIM)
    angles = jnp.arange(length, dtype=jnp.float32)[:, None] * freqs[None, :]
    return (jnp.cos(angles)[:, None, :], jnp.sin(angles)[:, None, :])

def rotate(values, cosine, sine):
    half = values.shape[-1] // 2
    first = values[..., :half]
    second = values[..., half:]
    return jnp.concatenate([first * cosine - second * sine, second * cosine + first * sine], axis=-1)

def attention(queries, keys, values, segment):
    length, heads, width = queries.shape
    blocks = length // QBLOCK
    scale = 1.0 / math.sqrt(width)
    position = jnp.arange(length).astype(jnp.int32)

    def one_block(pieces):
        query_block, segment_block, position_block = pieces
        scores = low_back(jnp.einsum('qhd,khd->hqk', query_block, keys, precision=HIGHEST) * scale)
        allowed = (segment_block[:, None] == segment[None, :]) & (position_block[:, None] >= position[None, :])
        scores = jnp.where(allowed[None], scores, NEGATIVE)
        largest = lax.optimization_barrier(jnp.max(scores, axis=-1, keepdims=True))
        exponent = jnp.exp(scores - largest)
        probs = exponent / lax.optimization_barrier(jnp.sum(exponent, axis=-1, keepdims=True))
        mixed = jnp.einsum('hqk,khd->qhd', low(probs), values, precision=HIGHEST)
        return mixed.reshape(QBLOCK, heads * width)
    result = lax.map(jax.checkpoint(one_block), (queries.reshape(blocks, QBLOCK, heads, width), segment.reshape(blocks, QBLOCK), position.reshape(blocks, QBLOCK)))
    return result.reshape(length, heads * width)

def pack_layer(layer_in, segment, projection_in, projection_out, up_weight, down_weight, gain_table):
    length, width = layer_in.shape
    inner = projection_out.shape[0]
    heads = inner // HEAD_DIM
    normed = low(rms_norm(layer_in, gain_table[0]))
    projected = low_back(jnp.dot(normed, projection_in.reshape(width, 3 * inner), precision=HIGHEST))
    cosine, sine = rotary_tables(length)
    queries = low(rotate(projected[:, :inner].reshape(length, heads, HEAD_DIM), cosine, sine))
    keys = low(rotate(projected[:, inner:2 * inner].reshape(length, heads, HEAD_DIM), cosine, sine))
    values = low(projected[:, 2 * inner:].reshape(length, heads, HEAD_DIM))
    attended = low(low_back(attention(queries, keys, values, segment)))
    branch = low_back(jnp.dot(attended, projection_out, precision=HIGHEST))
    middle = layer_in + rms_norm(branch, gain_table[1])
    normed_mid = low(rms_norm(middle, gain_table[2]))
    preact = low_back(jnp.dot(normed_mid, up_weight, precision=HIGHEST))
    hidden = low(jax.nn.gelu(preact, approximate=False))
    mixed = low_back(jnp.dot(hidden, down_weight, precision=HIGHEST))
    return middle + rms_norm(mixed, gain_table[3])

def layer(layer_in, segment_rows, projection_in, projection_out, up_weight, down_weight, gain_table):

    def one_pack(pieces):
        return pack_layer(pieces[0], pieces[1], projection_in, projection_out, up_weight, down_weight, gain_table)
    return lax.map(jax.checkpoint(one_pack), (layer_in, segment_rows))

def reference(inputs, segments, projection_in, projection_out, up_weight, down_weight, norm_gains, cotangent):
    shape = inputs.shape
    packs = shape[0] * shape[1]
    first_in = inputs.astype(jnp.float32).reshape(packs, shape[2], shape[3])
    segment_rows = segments.reshape(packs, shape[2])
    upstream = cotangent.astype(jnp.float32).reshape(packs, shape[2], shape[3])
    proj_in = projection_in.astype(jnp.float32)
    proj_out = projection_out.astype(jnp.float32)
    up_full = up_weight.astype(jnp.float32)
    down_full = down_weight.astype(jnp.float32)
    gain_full = norm_gains.astype(jnp.float32)

    def first_layer(layer_in, weight_in, weight_out, weight_up, weight_down, gain_table):
        return low(layer(layer_in, segment_rows, weight_in, weight_out, weight_up, weight_down, gain_table))

    def second_layer(layer_in, weight_in, weight_out, weight_up, weight_down, gain_table):
        return layer(layer_in, segment_rows, weight_in, weight_out, weight_up, weight_down, gain_table)
    hidden_state, first_back = jax.vjp(first_layer, first_in, proj_in[0], proj_out[0], up_full[0], down_full[0], gain_full[0])
    top_state, second_back = jax.vjp(second_layer, hidden_state, proj_in[1], proj_out[1], up_full[1], down_full[1], gain_full[1])
    second_grads = second_back(upstream)
    hidden_grad = low(second_grads[0])
    first_grads = first_back(hidden_grad)
    full_shape = (2,) + tuple(shape)
    layer_outputs = jnp.stack([hidden_state, top_state]).reshape(full_shape).astype(jnp.bfloat16)
    input_grads = jnp.stack([first_grads[0], hidden_grad]).reshape(full_shape).astype(jnp.bfloat16)
    projection_in_grad = jnp.stack([first_grads[1], second_grads[1]])
    projection_out_grad = jnp.stack([first_grads[2], second_grads[2]])
    up_grad = jnp.stack([first_grads[3], second_grads[3]])
    down_grad = jnp.stack([first_grads[4], second_grads[4]])
    gains_grad = jnp.stack([first_grads[5], second_grads[5]])
    return (layer_outputs, input_grads, projection_in_grad, projection_out_grad, up_grad, down_grad, gains_grad)
```

```python
from functools import partial
import math

import jax
import jax.numpy as jnp
from jax import lax
from jax.experimental import pallas as pl
from jax.experimental.pallas import tpu as pltpu
from jax.sharding import PartitionSpec as P

HEAD_DIM = 64
QBLOCK = 512


EPSILON = 1e-05
ROTARY_BASE = 10000.0
NEGATIVE = -1e30


def from_behind(shard, axis, by):
    length = lax.axis_size(axis)
    pairs = [(i, i + by) for i in range(length) if 0 <= i + by < length]
    return lax.ppermute(shard, axis, pairs)


def rms_parts(values, gain):
    inverse = lax.rsqrt(jnp.mean(values * values, axis=-1, keepdims=True) + EPSILON)
    return (values * inverse * gain, inverse)


def rms_back(values, inverse, gain, upstream):
    normed = values * inverse
    scaled = upstream * gain
    back = inverse * (scaled - normed * jnp.mean(scaled * normed, axis=-1, keepdims=True))
    return (back, jnp.sum(upstream * normed, axis=0))


def rotary_tables(length):
    half = HEAD_DIM // 2
    freqs = ROTARY_BASE ** (-2.0 * jnp.arange(half, dtype=jnp.float32) / HEAD_DIM)
    angles = jnp.arange(length, dtype=jnp.float32)[:, None] * freqs[None, :]
    return (jnp.cos(angles)[:, None, :], jnp.sin(angles)[:, None, :])


def rotate(values, cosine, sine):
    half = values.shape[-1] // 2
    first = values[..., :half]
    second = values[..., half:]
    return jnp.concatenate(
        [first * cosine - second * sine, second * cosine + first * sine], axis=-1
    )


def unrotate(upstream, cosine, sine):
    half = upstream.shape[-1] // 2
    first = upstream[..., :half]
    second = upstream[..., half:]
    return jnp.concatenate(
        [first * cosine + second * sine, second * cosine - first * sine], axis=-1
    )


def times_transposed(left, right):
    return lax.dot_general(
        left, right, (((1,), (1,)), ((), ())), preferred_element_type=jnp.float32
    )


def transposed_times(left, right):
    return lax.dot_general(
        left, right, (((0,), (0,)), ((), ())), preferred_element_type=jnp.float32
    )


def split_heads(projected, inner, cosine, sine):
    length = projected.shape[0]
    heads = inner // HEAD_DIM
    queries = rotate(projected[:, :inner].reshape(length, heads, HEAD_DIM), cosine, sine).astype(
        jnp.bfloat16
    )
    keys = rotate(
        projected[:, inner : 2 * inner].reshape(length, heads, HEAD_DIM), cosine, sine
    ).astype(jnp.bfloat16)
    values = projected[:, 2 * inner :].reshape(length, heads, HEAD_DIM).astype(jnp.bfloat16)
    return (queries, keys, values)


def block_scores(query_block, keys, segment_block, position_block, segment, position):
    scale = 1.0 / math.sqrt(HEAD_DIM)
    scores = (
        jnp.einsum("qhd,khd->hqk", query_block, keys, preferred_element_type=jnp.float32) * scale
    )
    allowed = (segment_block[:, None] == segment[None, :]) & (
        position_block[:, None] >= position[None, :]
    )
    return jnp.where(allowed[None], scores, NEGATIVE)


def attend(queries, keys, values, segment):
    length, heads, width = queries.shape
    blocks = length // QBLOCK
    position = jnp.arange(length, dtype=jnp.int32)

    def one_block(pieces):
        query_block, segment_block, position_block = pieces
        scores = block_scores(query_block, keys, segment_block, position_block, segment, position)
        largest = jnp.max(scores, axis=-1, keepdims=True)
        exponent = jnp.exp(scores - largest)
        totals = jnp.sum(exponent, axis=-1, keepdims=True)
        probs = (exponent / totals).astype(jnp.bfloat16)
        mixed = jnp.einsum("hqk,khd->qhd", probs, values, preferred_element_type=jnp.float32)
        return (
            mixed.reshape(QBLOCK, heads * width).astype(jnp.bfloat16),
            (largest + jnp.log(totals))[..., 0],
        )

    attended, logsum = lax.map(
        one_block,
        (
            queries.reshape(blocks, QBLOCK, heads, width),
            segment.reshape(blocks, QBLOCK),
            position.reshape(blocks, QBLOCK),
        ),
    )
    return (attended.reshape(length, heads * width), logsum)


def attend_back(queries, keys, values, segment, logsum, upstream):
    length, heads, width = queries.shape
    blocks = length // QBLOCK
    scale = 1.0 / math.sqrt(width)
    position = jnp.arange(length, dtype=jnp.int32)

    def one_block(carry, pieces):
        key_grad, value_grad = carry
        query_block, segment_block, position_block, logsum_block, upstream_block = pieces
        scores = block_scores(query_block, keys, segment_block, position_block, segment, position)
        probs = jnp.exp(scores - logsum_block[:, :, None])
        upstream_heads = upstream_block.reshape(QBLOCK, heads, width)
        prob_grad = jnp.einsum(
            "qhd,khd->hqk", upstream_heads, values, preferred_element_type=jnp.float32
        )
        score_grad = (
            probs * (prob_grad - jnp.sum(probs * prob_grad, axis=-1, keepdims=True))
        ).astype(jnp.bfloat16)
        query_grad = (
            jnp.einsum("hqk,khd->qhd", score_grad, keys, preferred_element_type=jnp.float32) * scale
        )
        key_grad = (
            key_grad
            + jnp.einsum(
                "hqk,qhd->khd", score_grad, query_block, preferred_element_type=jnp.float32
            )
            * scale
        )
        value_grad = value_grad + jnp.einsum(
            "hqk,qhd->khd",
            probs.astype(jnp.bfloat16),
            upstream_heads,
            preferred_element_type=jnp.float32,
        )
        return ((key_grad, value_grad), query_grad)

    zeros = jnp.zeros((length, heads, width), jnp.float32)
    carried, query_grad = lax.scan(
        one_block,
        (zeros, zeros),
        (
            queries.reshape(blocks, QBLOCK, heads, width),
            segment.reshape(blocks, QBLOCK),
            position.reshape(blocks, QBLOCK),
            logsum,
            upstream.reshape(blocks, QBLOCK, heads * width),
        ),
    )
    return (query_grad.reshape(length, heads, width), carried[0], carried[1])


def layer_forward(layer_in, segment, params):
    weight_in, weight_out, weight_up, weight_down, gain_table = params
    inner = weight_out.shape[0]
    inputs_float = layer_in.astype(jnp.float32)
    normed, _ = rms_parts(inputs_float, gain_table[0])
    normed_full = lax.all_gather(normed.astype(jnp.bfloat16), "tensor", axis=0, tiled=True)
    cosine, sine = rotary_tables(normed_full.shape[0])
    projected = jnp.dot(normed_full, weight_in, preferred_element_type=jnp.float32)
    queries, keys, values = split_heads(projected, inner, cosine, sine)
    attended, logsum = attend(queries, keys, values, segment)
    branch = lax.psum_scatter(
        jnp.dot(attended, weight_out, preferred_element_type=jnp.float32).astype(jnp.bfloat16),
        "tensor",
        scatter_dimension=0,
        tiled=True,
    ).astype(jnp.float32)
    branch_normed, _ = rms_parts(branch, gain_table[1])
    middle = inputs_float + branch_normed
    normed_mid, _ = rms_parts(middle, gain_table[2])
    mid_rows = lax.all_gather(normed_mid.astype(jnp.bfloat16), "tensor", axis=0, tiled=True)
    hidden = jax.nn.gelu(
        jnp.dot(mid_rows, weight_up, preferred_element_type=jnp.float32), approximate=False
    ).astype(jnp.bfloat16)
    mixed = lax.psum_scatter(
        jnp.dot(hidden, weight_down, preferred_element_type=jnp.float32).astype(jnp.bfloat16),
        "tensor",
        scatter_dimension=0,
        tiled=True,
    ).astype(jnp.float32)
    mixed_normed, _ = rms_parts(mixed, gain_table[3])
    return (middle + mixed_normed, (branch, mixed, attended, logsum, normed_full, mid_rows))


def layer_backward(layer_in, segment, params, kept, upstream):
    weight_in, weight_out, weight_up, weight_down, gain_table = params
    inner = weight_out.shape[0]
    branch, mixed, attended, logsum, normed_full, mid_rows = kept
    inputs_float = layer_in.astype(jnp.float32)
    _, in_inverse = rms_parts(inputs_float, gain_table[0])
    branch_normed, branch_inverse = rms_parts(branch, gain_table[1])
    middle = inputs_float + branch_normed
    _, mid_inverse = rms_parts(middle, gain_table[2])
    _, mixed_inverse = rms_parts(mixed, gain_table[3])
    mixed_grad, gain_three = rms_back(mixed, mixed_inverse, gain_table[3], upstream)
    mixed_rows = lax.all_gather(mixed_grad.astype(jnp.bfloat16), "tensor", axis=0, tiled=True)
    preact = jnp.dot(mid_rows, weight_up, preferred_element_type=jnp.float32)
    hidden, gelu_back = jax.vjp(partial(jax.nn.gelu, approximate=False), preact)
    hidden = hidden.astype(jnp.bfloat16)
    down_part = transposed_times(hidden, mixed_rows)
    preact_grad = gelu_back(times_transposed(mixed_rows, weight_down))[0].astype(jnp.bfloat16)
    up_part = transposed_times(mid_rows, preact_grad)
    mid_grad = lax.psum_scatter(
        times_transposed(preact_grad, weight_up).astype(jnp.bfloat16),
        "tensor",
        scatter_dimension=0,
        tiled=True,
    ).astype(jnp.float32)
    middle_back, gain_two = rms_back(middle, mid_inverse, gain_table[2], mid_grad)
    middle_grad = upstream + middle_back
    branch_grad, gain_one = rms_back(branch, branch_inverse, gain_table[1], middle_grad)
    branch_full = lax.all_gather(branch_grad.astype(jnp.bfloat16), "tensor", axis=0, tiled=True)
    out_part = transposed_times(attended, branch_full)
    attended_grad = times_transposed(branch_full, weight_out).astype(jnp.bfloat16)
    length = normed_full.shape[0]
    cosine, sine = rotary_tables(length)
    projected = jnp.dot(normed_full, weight_in, preferred_element_type=jnp.float32)
    queries, keys, values = split_heads(projected, inner, cosine, sine)
    query_grad, key_grad, value_grad = attend_back(
        queries, keys, values, segment, logsum, attended_grad
    )
    projected_grad = jnp.concatenate(
        [
            unrotate(query_grad, cosine, sine).reshape(length, inner),
            unrotate(key_grad, cosine, sine).reshape(length, inner),
            value_grad.reshape(length, inner),
        ],
        axis=1,
    ).astype(jnp.bfloat16)
    in_part = transposed_times(normed_full, projected_grad)
    normed_grad = lax.psum_scatter(
        times_transposed(projected_grad, weight_in).astype(jnp.bfloat16),
        "tensor",
        scatter_dimension=0,
        tiled=True,
    ).astype(jnp.float32)
    input_back, gain_zero = rms_back(inputs_float, in_inverse, gain_table[0], normed_grad)
    gain_parts = jnp.stack([gain_zero, gain_one, gain_two, gain_three])
    return (middle_grad + input_back, (in_part, out_part, up_part, down_part), gain_parts)


def take_slot(buffer, slot):
    return lax.dynamic_index_in_dim(buffer, slot, 0, keepdims=False)


def put_slot(buffer, slot, value, valid):
    merged = jnp.where(valid, value, take_slot(buffer, slot))
    return lax.dynamic_update_index_in_dim(buffer, merged, slot, 0)


def per_device(
    inputs, segments, projection_in, projection_out, up_weight, down_weight, norm_gains, cotangent
):
    section = lax.axis_index("section")
    micro = inputs.shape[1]
    rows = inputs.shape[2]
    width = inputs.shape[3]
    inner = projection_out.shape[1]
    up_use, down_use = (up_weight[0], down_weight[0])
    params = (
        projection_in[0].reshape(width, 3 * inner),
        projection_out[0],
        up_use,
        down_use,
        norm_gains[0],
    )
    received = jnp.zeros((rows, width), jnp.bfloat16)
    stored_inputs = jnp.zeros((micro, rows, width), jnp.bfloat16)
    layer_store = jnp.zeros((micro, rows, width), jnp.bfloat16)
    saved = None
    for period in range(micro + 1):
        index = period - section
        valid = (index >= 0) & (index < micro)
        slot = jnp.clip(index, 0, micro - 1)
        own_rows = take_slot(inputs[0], slot)
        layer_in = jnp.where(section == 0, own_rows, received)
        segment = take_slot(segments[0], slot)
        result, kept = layer_forward(layer_in, segment, params)
        result_low = result.astype(jnp.bfloat16)
        if saved is None:
            saved = jax.tree.map(lambda item: jnp.zeros((micro,) + item.shape, item.dtype), kept)
        saved = jax.tree.map(lambda buffer, item: put_slot(buffer, slot, item, valid), saved, kept)
        stored_inputs = put_slot(stored_inputs, slot, layer_in, valid)
        layer_store = put_slot(layer_store, slot, result_low, valid)
        if period < micro:
            received = from_behind(result_low, "section", 1)
    grad_back = jnp.zeros((rows, width), jnp.bfloat16)
    grad_store = jnp.zeros((micro, rows, width), jnp.bfloat16)
    total_in = jnp.zeros((width, 3 * inner), jnp.float32)
    total_out = jnp.zeros((inner, width), jnp.float32)
    total_up = jnp.zeros(up_use.shape, jnp.float32)
    total_down = jnp.zeros(down_use.shape, jnp.float32)
    total_gain = jnp.zeros((4, width), jnp.float32)
    for period in range(micro + 1):
        index = period - (1 - section)
        valid = (index >= 0) & (index < micro)
        slot = jnp.clip(index, 0, micro - 1)
        own_grad = take_slot(cotangent[0], slot)
        upstream = jnp.where(section == 1, own_grad, grad_back).astype(jnp.float32)
        kept = jax.tree.map(lambda buffer: take_slot(buffer, slot), saved)
        layer_in = take_slot(stored_inputs, slot)
        segment = take_slot(segments[0], slot)
        input_grad, weight_parts, gain_parts = layer_backward(
            layer_in, segment, params, kept, upstream
        )
        total_in = total_in + jnp.where(valid, weight_parts[0], 0.0)
        total_out = total_out + jnp.where(valid, weight_parts[1], 0.0)
        total_up = total_up + jnp.where(valid, weight_parts[2], 0.0)
        total_down = total_down + jnp.where(valid, weight_parts[3], 0.0)
        total_gain = total_gain + jnp.where(valid, gain_parts, 0.0)
        grad_low = input_grad.astype(jnp.bfloat16)
        grad_store = put_slot(grad_store, slot, grad_low, valid)
        if period < micro:
            grad_back = from_behind(grad_low, "section", -1)
    total_in, total_out, total_up, total_down = (
        lax.psum(total_in.astype(jnp.bfloat16), "dp").astype(jnp.float32),
        lax.psum(total_out.astype(jnp.bfloat16), "dp").astype(jnp.float32),
        lax.psum(total_up.astype(jnp.bfloat16), "dp").astype(jnp.float32),
        lax.psum(total_down.astype(jnp.bfloat16), "dp").astype(jnp.float32),
    )
    total_gain = lax.psum(total_gain, ("dp", "tensor"))
    return (
        layer_store[None, None],
        grad_store[None, None],
        total_in.reshape(1, width, 3, inner),
        total_out[None],
        total_up[None],
        total_down[None],
        total_gain[None],
    )


BF16 = jnp.bfloat16
F32 = jnp.float32
QROWS = 256
WINDOW = 512


def rope_lanes(length, lanes):
    half = HEAD_DIM // 2
    lane = jnp.arange(lanes, dtype=jnp.int32)
    freqs = ROTARY_BASE ** (-2.0 * jnp.arange(half, dtype=F32) / HEAD_DIM)
    angles = jnp.arange(length, dtype=F32)[:, None] * freqs[None, :]
    repeat = lanes // half
    cosine = jnp.tile(jnp.cos(angles), (1, repeat))
    sine = jnp.tile(jnp.sin(angles), (1, repeat))
    first = (lane % HEAD_DIM) < half
    return (cosine, jnp.where(first[None, :], -sine, sine))


def partner(values):
    lanes = values.shape[-1]
    half = HEAD_DIM // 2
    lane = lax.broadcasted_iota(jnp.int32, values.shape, 1)
    return jnp.where(
        (lane % HEAD_DIM) < half,
        pltpu.roll(values, lanes - half, 1),
        pltpu.roll(values, half, 1),
    )


def head_lanes(shape, head):
    lane = lax.broadcasted_iota(jnp.int32, shape, 1)
    return (lane // HEAD_DIM) == head


def nt(left, right):
    return lax.dot_general(left, right, (((1,), (1,)), ((), ())), preferred_element_type=F32)


def nn(left, right):
    return lax.dot_general(left, right, (((1,), (0,)), ((), ())), preferred_element_type=F32)


def allowed_keys(row0, rows, key0, keys, seg_col, seg_row):
    query_at = row0 + lax.broadcasted_iota(jnp.int32, (rows, keys), 0)
    key_at = key0 + lax.broadcasted_iota(jnp.int32, (rows, keys), 1)
    same = seg_col[row0 : row0 + rows, :] == seg_row[:, key0 : key0 + keys]
    return same & (query_at >= key_at)


def windows(length):
    rows = min(QROWS, length)
    for row0 in range(0, length, rows):
        key0 = max(0, row0 - WINDOW)
        yield row0, rows, key0, row0 + rows - key0


def attend_kernel(normed, weight, cosine, sine, seg_col, seg_row, qkv, mixed):
    length = normed.shape[0]
    lanes = mixed.shape[1]
    projected = nn(normed[...], weight[...])
    for part in range(2):
        raw = projected[:, part * lanes : (part + 1) * lanes]
        turned = raw * cosine[...] + partner(raw) * sine[...]
        qkv[:, part * lanes : (part + 1) * lanes] = turned.astype(BF16)
    qkv[:, 2 * lanes :] = projected[:, 2 * lanes :].astype(BF16)
    scale = 1.0 / math.sqrt(HEAD_DIM)
    for row0, rows, key0, keys in windows(length):
        keep = allowed_keys(row0, rows, key0, keys, seg_col, seg_row)
        query = qkv[row0 : row0 + rows, :lanes].astype(F32) * scale
        key = qkv[key0 : key0 + keys, lanes : 2 * lanes]
        value = qkv[key0 : key0 + keys, 2 * lanes :]
        total = jnp.zeros((rows, lanes), F32)
        for head in range(lanes // HEAD_DIM):
            mine = head_lanes((rows, lanes), head)
            scores = nt(jnp.where(mine, query, 0.0).astype(BF16), key)
            scores = jnp.where(keep, scores, NEGATIVE)
            largest = jnp.max(scores, axis=-1, keepdims=True)
            exponent = jnp.exp(scores - largest)
            inverse = 1.0 / jnp.sum(exponent, axis=-1, keepdims=True)
            probs = (exponent * inverse).astype(BF16)
            total = jnp.where(mine, nn(probs, value), total)
        mixed[row0 : row0 + rows, :] = total.astype(BF16)


def attend_forward(normed, weight, cosine, sine, seg_col, seg_row, lanes):
    length, width = normed.shape
    pieces = weight.shape[1] // (3 * lanes)
    whole = lambda shape: pl.BlockSpec(shape, lambda j: (0, 0))
    return pl.pallas_call(
        attend_kernel,
        grid=(pieces,),
        in_specs=[
            whole((length, width)),
            pl.BlockSpec((width, 3 * lanes), lambda j: (0, j)),
            whole((length, lanes)),
            whole((length, lanes)),
            whole((length, 1)),
            whole((1, length)),
        ],
        out_specs=[
            pl.BlockSpec((length, 3 * lanes), lambda j: (0, j)),
            pl.BlockSpec((length, lanes), lambda j: (0, j)),
        ],
        out_shape=[
            jax.ShapeDtypeStruct((length, pieces * 3 * lanes), BF16),
            jax.ShapeDtypeStruct((length, pieces * lanes), BF16),
        ],
        compiler_params=pltpu.CompilerParams(vmem_limit_bytes=48 * 1024 * 1024),
        cost_estimate=pl.CostEstimate(
            flops=pieces * length * 12 * lanes * width,
            bytes_accessed=2 * length * (width + pieces * 7 * lanes),
            transcendentals=pieces * 2 * length * length // 2,
        ),
    )(normed, weight, cosine, sine, seg_col, seg_row)


def attend_back_kernel(qkv, upstream, cosine, sine, seg_col, seg_row, grads, key_acc, value_acc):
    length = qkv.shape[0]
    lanes = upstream.shape[1]
    scale = 1.0 / math.sqrt(HEAD_DIM)
    key_acc[...] = jnp.zeros_like(key_acc)
    value_acc[...] = jnp.zeros_like(value_acc)
    for row0, rows, key0, keys in windows(length):
        keep = allowed_keys(row0, rows, key0, keys, seg_col, seg_row)
        query = qkv[row0 : row0 + rows, :lanes].astype(F32) * scale
        above = upstream[row0 : row0 + rows, :].astype(F32)
        key = qkv[key0 : key0 + keys, lanes : 2 * lanes]
        value = qkv[key0 : key0 + keys, 2 * lanes :]
        query_grad = jnp.zeros((rows, lanes), F32)
        key_sum = jnp.zeros((lanes, keys), F32)
        value_sum = jnp.zeros((lanes, keys), F32)
        for head in range(lanes // HEAD_DIM):
            mine = head_lanes((rows, lanes), head)
            query_low = jnp.where(mine, query, 0.0).astype(BF16)
            above_low = jnp.where(mine, above, 0.0).astype(BF16)
            scores = jnp.where(keep, nt(query_low, key), NEGATIVE)
            largest = jnp.max(scores, axis=-1, keepdims=True)
            exponent = jnp.exp(scores - largest)
            probs = exponent * (1.0 / jnp.sum(exponent, axis=-1, keepdims=True))
            prob_grad = nt(above_low, value)
            centre = jnp.sum(probs * prob_grad, axis=-1, keepdims=True)
            score_grad = (probs * (prob_grad - centre)).astype(BF16)
            query_grad = jnp.where(mine, nn(score_grad, key), query_grad)
            key_sum = key_sum + nn(jnp.where(mine, query, 0.0).T.astype(BF16), score_grad)
            value_sum = value_sum + nn(
                jnp.where(mine, above, 0.0).T.astype(BF16), probs.astype(BF16)
            )
        key_acc[:, key0 : key0 + keys] += key_sum
        value_acc[:, key0 : key0 + keys] += value_sum
        query_grad = query_grad * scale
        near, far = (cosine[row0 : row0 + rows, :], sine[row0 : row0 + rows, :])
        grads[row0 : row0 + rows, :lanes] = (query_grad * near - partner(query_grad) * far).astype(
            BF16
        )
    key_grad = key_acc[...].T
    grads[:, lanes : 2 * lanes] = (key_grad * cosine[...] - partner(key_grad) * sine[...]).astype(
        BF16
    )
    grads[:, 2 * lanes :] = value_acc[...].T.astype(BF16)


def attend_backward(qkv, upstream, cosine, sine, seg_col, seg_row, lanes):
    length = qkv.shape[0]
    pieces = upstream.shape[1] // lanes
    whole = lambda shape: pl.BlockSpec(shape, lambda j: (0, 0))
    return pl.pallas_call(
        attend_back_kernel,
        grid=(pieces,),
        in_specs=[
            pl.BlockSpec((length, 3 * lanes), lambda j: (0, j)),
            pl.BlockSpec((length, lanes), lambda j: (0, j)),
            whole((length, lanes)),
            whole((length, lanes)),
            whole((length, 1)),
            whole((1, length)),
        ],
        out_specs=pl.BlockSpec((length, 3 * lanes), lambda j: (0, j)),
        out_shape=jax.ShapeDtypeStruct((length, pieces * 3 * lanes), BF16),
        scratch_shapes=[pltpu.VMEM((lanes, length), F32), pltpu.VMEM((lanes, length), F32)],
        compiler_params=pltpu.CompilerParams(vmem_limit_bytes=48 * 1024 * 1024),
        cost_estimate=pl.CostEstimate(
            flops=pieces * 10 * length * length * lanes,
            bytes_accessed=2 * length * pieces * 7 * lanes,
            transcendentals=pieces * 2 * length * length // 2,
        ),
    )(qkv, upstream, cosine, sine, seg_col, seg_row)


def gelu_kernel(rows_ref, weight, hidden, slope):
    length = rows_ref.shape[0]
    step = min(QROWS, length)
    for row0 in range(0, length, step):
        preact = nn(rows_ref[row0 : row0 + step, :], weight[...])
        cumulative = 0.5 + 0.5 * lax.erf(preact * (1.0 / math.sqrt(2.0)))
        density = jnp.exp(preact * preact * -0.5) * (1.0 / math.sqrt(2.0 * math.pi))
        hidden[row0 : row0 + step, :] = (preact * cumulative).astype(BF16)
        slope[row0 : row0 + step, :] = (cumulative + preact * density).astype(BF16)


def gelu_forward(rows, weight, first, count, block):
    length, width = rows.shape
    return pl.pallas_call(
        gelu_kernel,
        grid=(count,),
        in_specs=[
            pl.BlockSpec((length, width), lambda j: (0, 0)),
            pl.BlockSpec((width, block), lambda j: (0, first + j)),
        ],
        out_specs=[pl.BlockSpec((length, block), lambda j: (0, j))] * 2,
        out_shape=[jax.ShapeDtypeStruct((length, count * block), BF16)] * 2,
        compiler_params=pltpu.CompilerParams(vmem_limit_bytes=48 * 1024 * 1024),
        cost_estimate=pl.CostEstimate(
            flops=2 * length * width * count * block,
            bytes_accessed=2 * (length * width + width * count * block + 2 * length * count * block),
            transcendentals=2 * length * count * block,
        ),
    )(rows, weight)


def ring(length, by):
    return [(i, (i + by) % length) for i in range(length)]


def other_core(values):
    return lax.ppermute(values, "section", [(0, 1), (1, 0)])


def both_cores(partial_sum):
    low = partial_sum.astype(BF16)
    return low.astype(F32) + other_core(low).astype(F32)


def pack_rows(blocks, section, tensor, count):
    _, rows, width = blocks.shape
    half = rows // 2
    mine = lambda pack: lax.dynamic_slice(blocks, (pack, section * half, 0), (1, half, width))[0]
    got = [(tensor, mine(tensor))]
    for by in range(1, count):
        sent = mine((tensor + by) % count)
        got.append(((tensor + count - by) % count, lax.ppermute(sent, "tensor", ring(count, by))))
    out = jnp.zeros((count, 2, half, width), blocks.dtype)
    for source, block in got:
        out = lax.dynamic_update_slice(out, block[None, None], (source, section, 0, 0))
    owned = jnp.concatenate([block[None] for _, block in got])
    theirs = other_core(owned)
    for step in range(count):
        source = (tensor + count - step) % count
        out = lax.dynamic_update_slice(
            out, theirs[step][None, None], (source, 1 - section, 0, 0)
        )
    return out.reshape(count * rows, width)


def unpack_rows(values, tensor, count):
    length, width = values.shape
    rows = length // count
    out = jnp.zeros((count, rows, width), values.dtype)
    for by in range(count):
        target = (tensor + by) % count
        block = lax.dynamic_slice(values, (target * rows, 0), (rows, width))
        if by:
            block = lax.ppermute(block, "tensor", ring(count, by))
        source = (tensor + count - by) % count
        out = lax.dynamic_update_slice(out, block[None], (source, 0, 0))
    return out


def gather_weights(own, column, group, count, dp):
    rows = own.shape[0] // dp
    piece = lax.dynamic_slice(own, (column * rows, 0), (rows, own.shape[1]))
    pieces = []
    for _ in range(count - 1):
        piece = lax.ppermute(piece, "tensor", ring(count, 1))
        pieces.append(piece)
    ordered = []
    start = 0
    for size in group:
        ordered += [item[:, start : start + size] for item in pieces]
        start += size
    rest = lax.all_gather(jnp.concatenate(ordered, axis=1), "dp", axis=0, tiled=True)
    return rest


def split_group(own, rest, group, count):
    out = []
    start = 0
    for size in group:
        out.append(
            (
                own[:, start : start + size],
                rest[:, start * (count - 1) : (start + size) * (count - 1)],
            )
        )
        start += size
    return out


def reduce_weights(parts, group, count):
    own = jnp.concatenate([part[0] for part in parts], axis=1)
    rest = jnp.concatenate([part[1] for part in parts], axis=1)
    whole = jnp.concatenate([own, rest], axis=1)
    summed = lax.psum_scatter(whole, "dp", scatter_dimension=0, tiled=True)
    total_size = sum(group)

    def slot(index):
        if index == 0:
            return summed[:, :total_size]
        pieces = []
        start = 0
        for size in group:
            at = total_size + start * (count - 1) + (index - 1) * size
            pieces.append(summed[:, at : at + size])
            start += size
        return jnp.concatenate(pieces, axis=1)

    running = slot(1)
    for index in range(2, count + 1):
        arrived = lax.ppermute(running, "tensor", ring(count, 1))
        running = (arrived.astype(F32) + slot(index % count).astype(F32)).astype(BF16)
    return lax.all_gather(running, "dp", axis=0, tiled=True)


def packed_forward(layer_in, weights, gain_table, tables, lanes, hidden_block):
    attn, mlp = weights
    (in_own, in_rest), (out_own, out_rest) = attn
    (up_own, up_rest), (down_own, down_rest) = mlp
    inputs_float = layer_in.astype(F32)
    normed = rms_parts(inputs_float, gain_table[0])[0].astype(BF16)
    qkv_own, mixed_own = attend_forward(normed, in_own, *tables, lanes)
    qkv_rest, mixed_rest = attend_forward(normed, in_rest, *tables, lanes)
    branch = both_cores(nt(mixed_own, out_own) + nt(mixed_rest, out_rest))
    middle = inputs_float + rms_parts(branch, gain_table[1])[0]
    normed_mid = rms_parts(middle, gain_table[2])[0].astype(BF16)
    hid_own, slope_own = gelu_forward(
        normed_mid, up_own, 0, up_own.shape[1] // hidden_block, hidden_block
    )
    hid_rest, slope_rest = gelu_forward(
        normed_mid, up_rest, 0, up_rest.shape[1] // hidden_block, hidden_block
    )
    mixed = both_cores(nt(hid_own, down_own) + nt(hid_rest, down_rest))
    result = (middle + rms_parts(mixed, gain_table[3])[0]).astype(BF16)
    kept = (
        branch,
        mixed,
        normed,
        normed_mid,
        (qkv_own, qkv_rest),
        (mixed_own, mixed_rest),
        (hid_own, hid_rest),
        (slope_own, slope_rest),
    )
    return result, kept


def packed_backward(layer_in, weights, gain_table, tables, lanes, kept, upstream, reduce):
    attn, mlp = weights
    in_parts, out_parts = attn
    up_parts, down_parts = mlp
    branch, mixed, normed, normed_mid, qkv, attended, hidden, slope = kept
    inputs_float = layer_in.astype(F32)
    _, in_inverse = rms_parts(inputs_float, gain_table[0])
    branch_normed, branch_inverse = rms_parts(branch, gain_table[1])
    middle = inputs_float + branch_normed
    _, mid_inverse = rms_parts(middle, gain_table[2])
    _, mixed_inverse = rms_parts(mixed, gain_table[3])
    mixed_grad, gain_three = rms_back(mixed, mixed_inverse, gain_table[3], upstream)
    mixed_grad = mixed_grad.astype(BF16)
    down_grads = [transposed_times(mixed_grad, part).astype(BF16) for part in hidden]
    preact_grads = [
        (nn(mixed_grad, weight) * factor.astype(F32)).astype(BF16)
        for weight, factor in zip(down_parts, slope)
    ]
    up_grads = [transposed_times(normed_mid, part).astype(BF16) for part in preact_grads]
    mlp_sum = reduce((tuple(up_grads), tuple(down_grads)), 1)
    mid_grad = both_cores(nt(preact_grads[0], up_parts[0]) + nt(preact_grads[1], up_parts[1]))
    middle_back, gain_two = rms_back(middle, mid_inverse, gain_table[2], mid_grad)
    middle_grad = upstream + middle_back
    branch_grad, gain_one = rms_back(branch, branch_inverse, gain_table[1], middle_grad)
    branch_grad = branch_grad.astype(BF16)
    out_grads = [transposed_times(branch_grad, part).astype(BF16) for part in attended]
    attended_grads = [nn(branch_grad, weight).astype(BF16) for weight in out_parts]
    projected_grads = [
        attend_backward(part, above, *tables, lanes) for part, above in zip(qkv, attended_grads)
    ]
    in_grads = [transposed_times(normed, part).astype(BF16) for part in projected_grads]
    attn_sum = reduce((tuple(in_grads), tuple(out_grads)), 0)
    normed_grad = both_cores(
        nt(projected_grads[0], in_parts[0]) + nt(projected_grads[1], in_parts[1])
    )
    input_back, gain_zero = rms_back(inputs_float, in_inverse, gain_table[0], normed_grad)
    gain_parts = jnp.stack([gain_zero, gain_one, gain_two, gain_three])
    return middle_grad + input_back, (attn_sum, mlp_sum), gain_parts


def per_chip(
    inputs, segments, projection_in, projection_out, up_weight, down_weight, norm_gains, cotangent
):
    section = lax.axis_index("section")
    column = lax.axis_index("dp")
    tensor = lax.axis_index("tensor")
    dp = lax.axis_size("dp")
    count = lax.axis_size("tensor")
    width = inputs.shape[3]
    length = inputs.shape[2] * count
    lanes = projection_out.shape[1] // 2
    hidden = up_weight.shape[2] // 2
    groups = ((3 * lanes, lanes), (hidden, hidden))
    up_down = down_weight[0].T
    out_turned = projection_out[0].T

    def half(core):
        cut = lambda table, size: lax.dynamic_slice(table, (0, core * size), (width, size))
        attn = [cut(projection_in[0][:, part, :], lanes) for part in range(3)]
        attn.append(cut(out_turned, lanes))
        mlp = [cut(up_weight[0], hidden), cut(up_down, hidden)]
        return [jnp.concatenate(attn, axis=1), jnp.concatenate(mlp, axis=1)]

    keep = half(section)
    swapped = [other_core(part) for part in half(1 - section)]
    own = [
        [jnp.where(section == layer, a, b) for a, b in zip(keep, swapped)] for layer in range(2)
    ]
    gains_other = other_core(norm_gains[0])
    gains = [jnp.where(section == layer, norm_gains[0], gains_other) for layer in range(2)]
    weights = []
    for layer in range(2):
        pair = []
        for kind in range(2):
            rest = gather_weights(own[layer][kind], column, groups[kind], count, dp)
            pair.append(split_group(own[layer][kind], rest, groups[kind], count))
        weights.append(pair)
    segment = lax.dynamic_index_in_dim(segments[0], tensor, 0, keepdims=False)
    cosine, sine = rope_lanes(length, lanes)
    tables = (cosine, sine, segment[:, None], segment[None, :])
    layer_in = pack_rows(inputs[0], section, tensor, count)
    upstream = pack_rows(cotangent[0], section, tensor, count)
    entering = []
    saved = []
    for layer in range(2):
        entering.append(layer_in)
        layer_in, kept = packed_forward(
            layer_in, weights[layer], gains[layer], tables, lanes, min(512, hidden)
        )
        saved.append(kept)
    outputs = jnp.where(section == 0, entering[1], layer_in)
    layer_store = unpack_rows(outputs, tensor, count)

    def reduce(parts, kind):
        return reduce_weights(parts, groups[kind], count)

    sums = [None, None]
    gain_sums = [None, None]
    input_grads = [None, None]
    for layer in (1, 0):
        grad, sums[layer], gain_sums[layer] = packed_backward(
            entering[layer],
            weights[layer],
            gains[layer],
            tables,
            lanes,
            saved[layer],
            upstream.astype(F32),
            reduce,
        )
        upstream = grad.astype(BF16)
        input_grads[layer] = upstream
    grad_store = unpack_rows(
        jnp.where(section == 0, input_grads[0], input_grads[1]), tensor, count
    )
    gain_total = lax.psum(jnp.stack(gain_sums), ("dp", "tensor"))
    gain_total = jnp.where(section == 0, gain_total[0], gain_total[1])
    finished = []
    for kind in range(2):
        mine = jnp.where(section == 0, sums[0][kind], sums[1][kind])
        sent = jnp.where(section == 0, sums[1][kind], sums[0][kind])
        theirs = other_core(sent)
        finished.append(
            (jnp.where(section == 0, mine, theirs), jnp.where(section == 0, theirs, mine))
        )
    (attn_low, attn_high), (mlp_low, mlp_high) = finished
    in_grad = jnp.stack(
        [
            jnp.concatenate(
                [item[:, part * lanes : (part + 1) * lanes] for item in (attn_low, attn_high)],
                axis=1,
            )
            for part in range(3)
        ],
        axis=1,
    ).astype(F32)
    out_grad = jnp.concatenate([attn_low[:, 3 * lanes :], attn_high[:, 3 * lanes :]], axis=1)
    up_grad = jnp.concatenate([mlp_low[:, :hidden], mlp_high[:, :hidden]], axis=1).astype(F32)
    down_grad = jnp.concatenate([mlp_low[:, hidden:], mlp_high[:, hidden:]], axis=1)
    return (
        layer_store[None, None],
        grad_store[None, None],
        in_grad[None],
        out_grad.T.astype(F32)[None],
        up_grad[None],
        down_grad.T.astype(F32)[None],
        gain_total[None],
    )


def one_pack_per_chip(mesh):
    return mesh.shape["section"] == 2 and mesh.shape["tensor"] == 4 and mesh.shape["dp"] == 4


def solution(mesh):
    placed = (
        P("dp", None, "tensor", None),
        P("dp", None, None),
        P("section", None, None, "tensor"),
        P("section", "tensor", None),
        P("section", None, "tensor"),
        P("section", "tensor", None),
        P("section", None, None),
        P("dp", None, "tensor", None),
    )
    body = per_chip if one_pack_per_chip(mesh) else per_device
    return jax.shard_map(
        body,
        mesh=mesh,
        in_specs=placed,
        out_specs=(
            P("section", "dp", None, "tensor", None),
            P("section", "dp", None, "tensor", None),
            P("section", None, None, "tensor"),
            P("section", "tensor", None),
            P("section", None, "tensor"),
            P("section", "tensor", None),
            P("section", None, None),
        ),
        check_vma=False,
    )
```

```python
from functools import partial
import math

import jax
import jax.numpy as jnp
from jax import lax
from jax.experimental import pallas as pl
from jax.experimental.pallas import tpu as pltpu
from jax.sharding import PartitionSpec as P

HEAD_DIM = 64
QBLOCK = 512


EPSILON = 1e-05
ROTARY_BASE = 10000.0
NEGATIVE = -1e30


def from_behind(shard, axis, by):
    length = lax.axis_size(axis)
    pairs = [(i, i + by) for i in range(length) if 0 <= i + by < length]
    return lax.ppermute(shard, axis, pairs)


def rms_parts(values, gain):
    inverse = lax.rsqrt(jnp.mean(values * values, axis=-1, keepdims=True) + EPSILON)
    return (values * inverse * gain, inverse)


def rms_back(values, inverse, gain, upstream):
    normed = values * inverse
    scaled = upstream * gain
    back = inverse * (scaled - normed * jnp.mean(scaled * normed, axis=-1, keepdims=True))
    return (back, jnp.sum(upstream * normed, axis=0))


def rotary_tables(length):
    half = HEAD_DIM // 2
    freqs = ROTARY_BASE ** (-2.0 * jnp.arange(half, dtype=jnp.float32) / HEAD_DIM)
    angles = jnp.arange(length, dtype=jnp.float32)[:, None] * freqs[None, :]
    return (jnp.cos(angles)[:, None, :], jnp.sin(angles)[:, None, :])


def rotate(values, cosine, sine):
    half = values.shape[-1] // 2
    first = values[..., :half]
    second = values[..., half:]
    return jnp.concatenate(
        [first * cosine - second * sine, second * cosine + first * sine], axis=-1
    )


def unrotate(upstream, cosine, sine):
    half = upstream.shape[-1] // 2
    first = upstream[..., :half]
    second = upstream[..., half:]
    return jnp.concatenate(
        [first * cosine + second * sine, second * cosine - first * sine], axis=-1
    )


def times_transposed(left, right):
    return lax.dot_general(
        left, right, (((1,), (1,)), ((), ())), preferred_element_type=jnp.float32
    )


def transposed_times(left, right):
    return lax.dot_general(
        left, right, (((0,), (0,)), ((), ())), preferred_element_type=jnp.float32
    )


def split_heads(projected, inner, cosine, sine):
    length = projected.shape[0]
    heads = inner // HEAD_DIM
    queries = rotate(projected[:, :inner].reshape(length, heads, HEAD_DIM), cosine, sine).astype(
        jnp.bfloat16
    )
    keys = rotate(
        projected[:, inner : 2 * inner].reshape(length, heads, HEAD_DIM), cosine, sine
    ).astype(jnp.bfloat16)
    values = projected[:, 2 * inner :].reshape(length, heads, HEAD_DIM).astype(jnp.bfloat16)
    return (queries, keys, values)


def block_scores(query_block, keys, segment_block, position_block, segment, position):
    scale = 1.0 / math.sqrt(HEAD_DIM)
    scores = (
        jnp.einsum("qhd,khd->hqk", query_block, keys, preferred_element_type=jnp.float32) * scale
    )
    allowed = (segment_block[:, None] == segment[None, :]) & (
        position_block[:, None] >= position[None, :]
    )
    return jnp.where(allowed[None], scores, NEGATIVE)


def attend(queries, keys, values, segment):
    length, heads, width = queries.shape
    blocks = length // QBLOCK
    position = jnp.arange(length, dtype=jnp.int32)

    def one_block(pieces):
        query_block, segment_block, position_block = pieces
        scores = block_scores(query_block, keys, segment_block, position_block, segment, position)
        largest = jnp.max(scores, axis=-1, keepdims=True)
        exponent = jnp.exp(scores - largest)
        totals = jnp.sum(exponent, axis=-1, keepdims=True)
        probs = (exponent / totals).astype(jnp.bfloat16)
        mixed = jnp.einsum("hqk,khd->qhd", probs, values, preferred_element_type=jnp.float32)
        return (
            mixed.reshape(QBLOCK, heads * width).astype(jnp.bfloat16),
            (largest + jnp.log(totals))[..., 0],
        )

    attended, logsum = lax.map(
        one_block,
        (
            queries.reshape(blocks, QBLOCK, heads, width),
            segment.reshape(blocks, QBLOCK),
            position.reshape(blocks, QBLOCK),
        ),
    )
    return (attended.reshape(length, heads * width), logsum)


def attend_back(queries, keys, values, segment, logsum, upstream):
    length, heads, width = queries.shape
    blocks = length // QBLOCK
    scale = 1.0 / math.sqrt(width)
    position = jnp.arange(length, dtype=jnp.int32)

    def one_block(carry, pieces):
        key_grad, value_grad = carry
        query_block, segment_block, position_block, logsum_block, upstream_block = pieces
        scores = block_scores(query_block, keys, segment_block, position_block, segment, position)
        probs = jnp.exp(scores - logsum_block[:, :, None])
        upstream_heads = upstream_block.reshape(QBLOCK, heads, width)
        prob_grad = jnp.einsum(
            "qhd,khd->hqk", upstream_heads, values, preferred_element_type=jnp.float32
        )
        score_grad = (
            probs * (prob_grad - jnp.sum(probs * prob_grad, axis=-1, keepdims=True))
        ).astype(jnp.bfloat16)
        query_grad = (
            jnp.einsum("hqk,khd->qhd", score_grad, keys, preferred_element_type=jnp.float32) * scale
        )
        key_grad = (
            key_grad
            + jnp.einsum(
                "hqk,qhd->khd", score_grad, query_block, preferred_element_type=jnp.float32
            )
            * scale
        )
        value_grad = value_grad + jnp.einsum(
            "hqk,qhd->khd",
            probs.astype(jnp.bfloat16),
            upstream_heads,
            preferred_element_type=jnp.float32,
        )
        return ((key_grad, value_grad), query_grad)

    zeros = jnp.zeros((length, heads, width), jnp.float32)
    carried, query_grad = lax.scan(
        one_block,
        (zeros, zeros),
        (
            queries.reshape(blocks, QBLOCK, heads, width),
            segment.reshape(blocks, QBLOCK),
            position.reshape(blocks, QBLOCK),
            logsum,
            upstream.reshape(blocks, QBLOCK, heads * width),
        ),
    )
    return (query_grad.reshape(length, heads, width), carried[0], carried[1])


def layer_forward(layer_in, segment, params):
    weight_in, weight_out, weight_up, weight_down, gain_table = params
    inner = weight_out.shape[0]
    inputs_float = layer_in.astype(jnp.float32)
    normed, _ = rms_parts(inputs_float, gain_table[0])
    normed_full = lax.all_gather(normed.astype(jnp.bfloat16), "tensor", axis=0, tiled=True)
    cosine, sine = rotary_tables(normed_full.shape[0])
    projected = jnp.dot(normed_full, weight_in, preferred_element_type=jnp.float32)
    queries, keys, values = split_heads(projected, inner, cosine, sine)
    attended, logsum = attend(queries, keys, values, segment)
    branch = lax.psum_scatter(
        jnp.dot(attended, weight_out, preferred_element_type=jnp.float32).astype(jnp.bfloat16),
        "tensor",
        scatter_dimension=0,
        tiled=True,
    ).astype(jnp.float32)
    branch_normed, _ = rms_parts(branch, gain_table[1])
    middle = inputs_float + branch_normed
    normed_mid, _ = rms_parts(middle, gain_table[2])
    mid_rows = lax.all_gather(normed_mid.astype(jnp.bfloat16), "tensor", axis=0, tiled=True)
    hidden = jax.nn.gelu(
        jnp.dot(mid_rows, weight_up, preferred_element_type=jnp.float32), approximate=False
    ).astype(jnp.bfloat16)
    mixed = lax.psum_scatter(
        jnp.dot(hidden, weight_down, preferred_element_type=jnp.float32).astype(jnp.bfloat16),
        "tensor",
        scatter_dimension=0,
        tiled=True,
    ).astype(jnp.float32)
    mixed_normed, _ = rms_parts(mixed, gain_table[3])
    return (middle + mixed_normed, (branch, mixed, attended, logsum, normed_full, mid_rows))


def layer_backward(layer_in, segment, params, kept, upstream):
    weight_in, weight_out, weight_up, weight_down, gain_table = params
    inner = weight_out.shape[0]
    branch, mixed, attended, logsum, normed_full, mid_rows = kept
    inputs_float = layer_in.astype(jnp.float32)
    _, in_inverse = rms_parts(inputs_float, gain_table[0])
    branch_normed, branch_inverse = rms_parts(branch, gain_table[1])
    middle = inputs_float + branch_normed
    _, mid_inverse = rms_parts(middle, gain_table[2])
    _, mixed_inverse = rms_parts(mixed, gain_table[3])
    mixed_grad, gain_three = rms_back(mixed, mixed_inverse, gain_table[3], upstream)
    mixed_rows = lax.all_gather(mixed_grad.astype(jnp.bfloat16), "tensor", axis=0, tiled=True)
    preact = jnp.dot(mid_rows, weight_up, preferred_element_type=jnp.float32)
    hidden, gelu_back = jax.vjp(partial(jax.nn.gelu, approximate=False), preact)
    hidden = hidden.astype(jnp.bfloat16)
    down_part = transposed_times(hidden, mixed_rows)
    preact_grad = gelu_back(times_transposed(mixed_rows, weight_down))[0].astype(jnp.bfloat16)
    up_part = transposed_times(mid_rows, preact_grad)
    mid_grad = lax.psum_scatter(
        times_transposed(preact_grad, weight_up).astype(jnp.bfloat16),
        "tensor",
        scatter_dimension=0,
        tiled=True,
    ).astype(jnp.float32)
    middle_back, gain_two = rms_back(middle, mid_inverse, gain_table[2], mid_grad)
    middle_grad = upstream + middle_back
    branch_grad, gain_one = rms_back(branch, branch_inverse, gain_table[1], middle_grad)
    branch_full = lax.all_gather(branch_grad.astype(jnp.bfloat16), "tensor", axis=0, tiled=True)
    out_part = transposed_times(attended, branch_full)
    attended_grad = times_transposed(branch_full, weight_out).astype(jnp.bfloat16)
    length = normed_full.shape[0]
    cosine, sine = rotary_tables(length)
    projected = jnp.dot(normed_full, weight_in, preferred_element_type=jnp.float32)
    queries, keys, values = split_heads(projected, inner, cosine, sine)
    query_grad, key_grad, value_grad = attend_back(
        queries, keys, values, segment, logsum, attended_grad
    )
    projected_grad = jnp.concatenate(
        [
            unrotate(query_grad, cosine, sine).reshape(length, inner),
            unrotate(key_grad, cosine, sine).reshape(length, inner),
            value_grad.reshape(length, inner),
        ],
        axis=1,
    ).astype(jnp.bfloat16)
    in_part = transposed_times(normed_full, projected_grad)
    normed_grad = lax.psum_scatter(
        times_transposed(projected_grad, weight_in).astype(jnp.bfloat16),
        "tensor",
        scatter_dimension=0,
        tiled=True,
    ).astype(jnp.float32)
    input_back, gain_zero = rms_back(inputs_float, in_inverse, gain_table[0], normed_grad)
    gain_parts = jnp.stack([gain_zero, gain_one, gain_two, gain_three])
    return (middle_grad + input_back, (in_part, out_part, up_part, down_part), gain_parts)


def take_slot(buffer, slot):
    return lax.dynamic_index_in_dim(buffer, slot, 0, keepdims=False)


def put_slot(buffer, slot, value, valid):
    merged = jnp.where(valid, value, take_slot(buffer, slot))
    return lax.dynamic_update_index_in_dim(buffer, merged, slot, 0)


def per_device(
    inputs, segments, projection_in, projection_out, up_weight, down_weight, norm_gains, cotangent
):
    section = lax.axis_index("section")
    micro = inputs.shape[1]
    rows = inputs.shape[2]
    width = inputs.shape[3]
    inner = projection_out.shape[1]
    up_use, down_use = (up_weight[0], down_weight[0])
    params = (
        projection_in[0].reshape(width, 3 * inner),
        projection_out[0],
        up_use,
        down_use,
        norm_gains[0],
    )
    received = jnp.zeros((rows, width), jnp.bfloat16)
    stored_inputs = jnp.zeros((micro, rows, width), jnp.bfloat16)
    layer_store = jnp.zeros((micro, rows, width), jnp.bfloat16)
    saved = None
    for period in range(micro + 1):
        index = period - section
        valid = (index >= 0) & (index < micro)
        slot = jnp.clip(index, 0, micro - 1)
        own_rows = take_slot(inputs[0], slot)
        layer_in = jnp.where(section == 0, own_rows, received)
        segment = take_slot(segments[0], slot)
        result, kept = layer_forward(layer_in, segment, params)
        result_low = result.astype(jnp.bfloat16)
        if saved is None:
            saved = jax.tree.map(lambda item: jnp.zeros((micro,) + item.shape, item.dtype), kept)
        saved = jax.tree.map(lambda buffer, item: put_slot(buffer, slot, item, valid), saved, kept)
        stored_inputs = put_slot(stored_inputs, slot, layer_in, valid)
        layer_store = put_slot(layer_store, slot, result_low, valid)
        if period < micro:
            received = from_behind(result_low, "section", 1)
    grad_back = jnp.zeros((rows, width), jnp.bfloat16)
    grad_store = jnp.zeros((micro, rows, width), jnp.bfloat16)
    total_in = jnp.zeros((width, 3 * inner), jnp.float32)
    total_out = jnp.zeros((inner, width), jnp.float32)
    total_up = jnp.zeros(up_use.shape, jnp.float32)
    total_down = jnp.zeros(down_use.shape, jnp.float32)
    total_gain = jnp.zeros((4, width), jnp.float32)
    for period in range(micro + 1):
        index = period - (1 - section)
        valid = (index >= 0) & (index < micro)
        slot = jnp.clip(index, 0, micro - 1)
        own_grad = take_slot(cotangent[0], slot)
        upstream = jnp.where(section == 1, own_grad, grad_back).astype(jnp.float32)
        kept = jax.tree.map(lambda buffer: take_slot(buffer, slot), saved)
        layer_in = take_slot(stored_inputs, slot)
        segment = take_slot(segments[0], slot)
        input_grad, weight_parts, gain_parts = layer_backward(
            layer_in, segment, params, kept, upstream
        )
        total_in = total_in + jnp.where(valid, weight_parts[0], 0.0)
        total_out = total_out + jnp.where(valid, weight_parts[1], 0.0)
        total_up = total_up + jnp.where(valid, weight_parts[2], 0.0)
        total_down = total_down + jnp.where(valid, weight_parts[3], 0.0)
        total_gain = total_gain + jnp.where(valid, gain_parts, 0.0)
        grad_low = input_grad.astype(jnp.bfloat16)
        grad_store = put_slot(grad_store, slot, grad_low, valid)
        if period < micro:
            grad_back = from_behind(grad_low, "section", -1)
    total_in, total_out, total_up, total_down = (
        lax.psum(total_in.astype(jnp.bfloat16), "dp").astype(jnp.float32),
        lax.psum(total_out.astype(jnp.bfloat16), "dp").astype(jnp.float32),
        lax.psum(total_up.astype(jnp.bfloat16), "dp").astype(jnp.float32),
        lax.psum(total_down.astype(jnp.bfloat16), "dp").astype(jnp.float32),
    )
    total_gain = lax.psum(total_gain, ("dp", "tensor"))
    return (
        layer_store[None, None],
        grad_store[None, None],
        total_in.reshape(1, width, 3, inner),
        total_out[None],
        total_up[None],
        total_down[None],
        total_gain[None],
    )


BF16 = jnp.bfloat16
F32 = jnp.float32
QROWS = 256
COLUMNS = 4
ROOMY = pltpu.CompilerParams(vmem_limit_bytes=56 * 1024 * 1024)
WINDOW = 512
BYTES_PER_MICRO = 3400000
COLUMN_DEPTH = 2
TENSOR_DEPTH = 2


def cost(micros):
    return pl.CostEstimate(
        flops=int(micros * 3e8), bytes_accessed=int(micros * BYTES_PER_MICRO), transcendentals=0
    )


def rope_lanes(length, lanes):
    half = HEAD_DIM // 2
    lane = jnp.arange(lanes, dtype=jnp.int32)
    freqs = ROTARY_BASE ** (-2.0 * jnp.arange(half, dtype=F32) / HEAD_DIM)
    angles = jnp.arange(length, dtype=F32)[:, None] * freqs[None, :]
    repeat = lanes // half
    cosine = jnp.tile(jnp.cos(angles), (1, repeat))
    sine = jnp.tile(jnp.sin(angles), (1, repeat))
    first = (lane % HEAD_DIM) < half
    return (cosine, jnp.where(first[None, :], -sine, sine))


def partner(values):
    lanes = values.shape[-1]
    half = HEAD_DIM // 2
    lane = lax.broadcasted_iota(jnp.int32, values.shape, 1)
    return jnp.where(
        (lane % HEAD_DIM) < half,
        pltpu.roll(values, lanes - half, 1),
        pltpu.roll(values, half, 1),
    )


def head_lanes(shape, head):
    lane = lax.broadcasted_iota(jnp.int32, shape, 1)
    return (lane // HEAD_DIM) == head


def nt(left, right):
    return lax.dot_general(left, right, (((1,), (1,)), ((), ())), preferred_element_type=F32)


def nn(left, right):
    return lax.dot_general(left, right, (((1,), (0,)), ((), ())), preferred_element_type=F32)


def allowed_keys(row0, rows, key0, keys, seg_col, seg_row):
    query_at = row0 + lax.broadcasted_iota(jnp.int32, (rows, keys), 0)
    key_at = key0 + lax.broadcasted_iota(jnp.int32, (rows, keys), 1)
    same = seg_col[row0 : row0 + rows, :] == seg_row[:, key0 : key0 + keys]
    return same & (query_at >= key_at)


def windows(length):
    rows = min(QROWS, length)
    for row0 in range(0, length, rows):
        key0 = max(0, row0 - WINDOW)
        yield row0, rows, key0, row0 + rows - key0


def attend_kernel(normed, weight, cosine, sine, seg_col, seg_row, qkv, mixed):
    length = normed.shape[0]
    lanes = mixed.shape[1]
    projected = nn(normed[...], weight[...])
    for part in range(2):
        raw = projected[:, part * lanes : (part + 1) * lanes]
        turned = raw * cosine[...] + partner(raw) * sine[...]
        qkv[:, part * lanes : (part + 1) * lanes] = turned.astype(BF16)
    qkv[:, 2 * lanes :] = projected[:, 2 * lanes :].astype(BF16)
    scale = 1.0 / math.sqrt(HEAD_DIM)
    for row0, rows, key0, keys in windows(length):
        keep = allowed_keys(row0, rows, key0, keys, seg_col, seg_row)
        query = qkv[row0 : row0 + rows, :lanes].astype(F32) * scale
        key = qkv[key0 : key0 + keys, lanes : 2 * lanes]
        value = qkv[key0 : key0 + keys, 2 * lanes :]
        total = jnp.zeros((rows, lanes), F32)
        for head in range(lanes // HEAD_DIM):
            mine = head_lanes((rows, lanes), head)
            scores = nt(jnp.where(mine, query, 0.0).astype(BF16), key)
            scores = jnp.where(keep, scores, NEGATIVE)
            largest = jnp.max(scores, axis=-1, keepdims=True)
            exponent = jnp.exp(scores - largest)
            inverse = 1.0 / jnp.sum(exponent, axis=-1, keepdims=True)
            probs = (exponent * inverse).astype(BF16)
            total = jnp.where(mine, nn(probs, value), total)
        mixed[row0 : row0 + rows, :] = total.astype(BF16)


def attend_forward(normed, weight, tables, lanes, first, count, kept=()):
    length, width = normed.shape
    pieces = weight.shape[1] // (3 * lanes)
    whole = lambda shape: pl.BlockSpec(shape, lambda j: (0, 0))

    def kernel(*refs):
        attend_kernel(*refs[:6], *refs[6 + len(kept) :])

    return pl.pallas_call(
        kernel,
        grid=(count,),
        in_specs=[
            whole((length, width)),
            pl.BlockSpec((width, 3 * lanes), lambda j: (0, first + j)),
            whole((length, lanes)),
            whole((length, lanes)),
            whole((length, 1)),
            whole((1, length)),
        ]
        + [pl.BlockSpec(memory_space=pl.ANY)] * len(kept),
        out_specs=[
            pl.BlockSpec((length, 3 * lanes), lambda j: (0, first + j)),
            pl.BlockSpec((length, lanes), lambda j: (0, first + j)),
        ],
        out_shape=[
            jax.ShapeDtypeStruct((length, pieces * 3 * lanes), BF16),
            jax.ShapeDtypeStruct((length, pieces * lanes), BF16),
        ],
        input_output_aliases={6 + at: at for at in range(len(kept))},
        compiler_params=ROOMY,
        cost_estimate=cost(13),
    )(normed, weight, *tables, *kept)


def tn(left, right):
    return lax.dot_general(left, right, (((0,), (0,)), ((), ())), preferred_element_type=F32)


def attend_back_kernel(
    carried,
    place,
    branch_grad,
    normed,
    qkv,
    attended,
    w_in,
    w_out,
    cosine,
    sine,
    seg_col,
    seg_row,
    *refs,
):
    before, refs = refs[:carried], refs[carried:]
    outs, (normed_grad, grads, key_acc, value_acc, total) = refs[:-5], refs[-5:]
    step = pl.program_id(0)
    length = qkv.shape[0]
    lanes = attended.shape[1]
    scale = 1.0 / math.sqrt(HEAD_DIM)

    @pl.when(step == 0)
    def _():
        total[...] = before[-1][...] if carried else jnp.zeros_like(total)

    key_acc[...] = jnp.zeros_like(key_acc)
    value_acc[...] = jnp.zeros_like(value_acc)
    for row0, rows, key0, keys in windows(length):
        keep = allowed_keys(row0, rows, key0, keys, seg_col, seg_row)
        query = qkv[row0 : row0 + rows, :lanes].astype(F32) * scale
        above = nn(branch_grad[row0 : row0 + rows, :], w_out[...]).astype(BF16).astype(F32)
        key = qkv[key0 : key0 + keys, lanes : 2 * lanes]
        value = qkv[key0 : key0 + keys, 2 * lanes :]
        query_grad = jnp.zeros((rows, lanes), F32)
        key_sum = jnp.zeros((lanes, keys), F32)
        value_sum = jnp.zeros((lanes, keys), F32)
        for head in range(lanes // HEAD_DIM):
            mine = head_lanes((rows, lanes), head)
            query_mine = jnp.where(mine, query, 0.0)
            above_mine = jnp.where(mine, above, 0.0)
            scores = jnp.where(keep, nt(query_mine.astype(BF16), key), NEGATIVE)
            largest = jnp.max(scores, axis=-1, keepdims=True)
            exponent = jnp.exp(scores - largest)
            probs = exponent * (1.0 / jnp.sum(exponent, axis=-1, keepdims=True))
            prob_grad = nt(above_mine.astype(BF16), value)
            centre = jnp.sum(probs * prob_grad, axis=-1, keepdims=True)
            score_grad = (probs * (prob_grad - centre)).astype(BF16)
            query_grad = jnp.where(mine, nn(score_grad, key), query_grad)
            key_sum = key_sum + nn(query_mine.T.astype(BF16), score_grad)
            value_sum = value_sum + nn(above_mine.T.astype(BF16), probs.astype(BF16))
        key_acc[:, key0 : key0 + keys] += key_sum
        value_acc[:, key0 : key0 + keys] += value_sum
        query_grad = query_grad * scale
        near, far = (cosine[row0 : row0 + rows, :], sine[row0 : row0 + rows, :])
        grads[row0 : row0 + rows, :lanes] = (query_grad * near - partner(query_grad) * far).astype(
            BF16
        )
    key_grad = key_acc[...].T
    grads[:, lanes : 2 * lanes] = (key_grad * cosine[...] - partner(key_grad) * sine[...]).astype(
        BF16
    )
    grads[:, 2 * lanes :] = value_acc[...].T.astype(BF16)
    width = normed.shape[1]
    block = width // COLUMNS
    targets = [(out, slice(0, out.shape[0])) for out in outs]
    if len(outs) == 1:
        owners = [place[1] ^ block_mask(at, place[0]) for at in range(COLUMNS)]
        targets = [(outs[0], spot(owner, block)) for owner in owners]
    low = 0
    for out, rows in targets:
        high = low + (block if len(outs) == 1 else out.shape[0])
        out[rows, : 3 * lanes] = tn(normed[:, low:high], grads[...]).astype(BF16)
        out[rows, 3 * lanes :] = tn(branch_grad[:, low:high], attended[...]).astype(BF16)
        low = high
    for row0 in range(0, length, QROWS):
        total[row0 : row0 + QROWS, :] += nt(grads[row0 : row0 + QROWS, :], w_in[...])

    @pl.when(step == pl.num_programs(0) - 1)
    def _():
        normed_grad[...] = total[...].astype(normed_grad.dtype)


def attend_backward(
    place,
    branch_grad,
    normed,
    qkv,
    attended,
    w_in,
    w_out,
    tables,
    lanes,
    heights,
    first,
    count,
    kept=(),
):
    length, width = normed.shape
    pieces = attended.shape[1] // lanes
    last = first + count == pieces
    whole = lambda shape: pl.BlockSpec(shape, lambda j, place: (0, 0))
    by_piece = lambda rows, size: pl.BlockSpec((rows, size), lambda j, place: (0, first + j))
    aliases = {11 + at: at for at in range(len(heights))} if kept else {}
    specs = [pl.BlockSpec(memory_space=pl.ANY)] * len(heights) + [whole((length, width))]
    return placed_call(
        partial(attend_back_kernel, len(kept)),
        place,
        (branch_grad, normed, qkv, attended, w_in, w_out, *tables, *kept),
        [
            whole((length, width)),
            whole((length, width)),
            by_piece(length, 3 * lanes),
            by_piece(length, lanes),
            by_piece(width, 3 * lanes),
            by_piece(width, lanes),
            whole((length, lanes)),
            whole((length, lanes)),
            whole((length, 1)),
            whole((1, length)),
        ]
        + (specs if kept else []),
        [by_piece(rows, 4 * lanes) for rows in heights] + [whole((length, width))],
        [((rows, 4 * lanes * pieces), BF16) for rows in heights]
        + [((length, width), BF16 if last else F32)],
        (count,),
        [
            pltpu.VMEM((length, 3 * lanes), BF16),
            pltpu.VMEM((lanes, length), F32),
            pltpu.VMEM((lanes, length), F32),
            pltpu.VMEM((length, width), F32),
        ],
        aliases,
    )


def outward_kernel(values, weight, out):
    out[...] = nt(values[...], weight[...]).astype(BF16)


def outward(values, weight):
    length, inner = values.shape
    width = weight.shape[0]
    return pl.pallas_call(
        outward_kernel,
        grid=(length // QROWS,),
        in_specs=[
            pl.BlockSpec((QROWS, inner), lambda j: (j, 0)),
            pl.BlockSpec((width, inner), lambda j: (0, 0)),
        ],
        out_specs=pl.BlockSpec((QROWS, width), lambda j: (j, 0)),
        out_shape=jax.ShapeDtypeStruct((length, width), BF16),
        compiler_params=ROOMY,
        cost_estimate=cost(5),
    )(values, weight)


def hidden_kernel(rows_ref, w_up, w_down, hidden, slope, mixed, total):
    step = pl.program_id(0)

    @pl.when(step == 0)
    def _():
        total[...] = jnp.zeros_like(total)

    for row0 in range(0, rows_ref.shape[0], QROWS):
        rows = slice(row0, row0 + QROWS)
        preact = nn(rows_ref[rows, :], w_up[...])
        cumulative = 0.5 + 0.5 * lax.erf(preact * (1.0 / math.sqrt(2.0)))
        density = jnp.exp(preact * preact * -0.5) * (1.0 / math.sqrt(2.0 * math.pi))
        hidden[rows, :] = (preact * cumulative).astype(BF16)
        slope[rows, :] = (cumulative + preact * density).astype(BF16)
        total[rows, :] += nt(hidden[rows, :], w_down[...])

    @pl.when(step == pl.num_programs(0) - 1)
    def _():
        mixed[...] = total[...].astype(BF16)


def hidden_forward(rows, w_up, w_down, block):
    length, width = rows.shape
    size = w_up.shape[1]
    whole = pl.BlockSpec((length, width), lambda j: (0, 0))
    return pl.pallas_call(
        hidden_kernel,
        grid=(size // block,),
        in_specs=[whole] + [pl.BlockSpec((width, block), lambda j: (0, j))] * 2,
        out_specs=[pl.BlockSpec((length, block), lambda j: (0, j))] * 2 + [whole],
        out_shape=[jax.ShapeDtypeStruct((length, size), BF16)] * 2
        + [jax.ShapeDtypeStruct((length, width), BF16)],
        scratch_shapes=[pltpu.VMEM((length, width), F32)],
        compiler_params=ROOMY,
        cost_estimate=cost(19),
    )(rows, w_up, w_down)


def hidden_back_kernel(
    place,
    mixed_grad,
    normed_mid,
    w_up,
    w_down,
    hidden,
    slope,
    *refs,
):
    outs, (mid_grad, preact_grad, total) = refs[:-3], refs[-3:]
    step = pl.program_id(0)

    @pl.when(step == 0)
    def _():
        total[...] = jnp.zeros_like(total)

    for row0 in range(0, mixed_grad.shape[0], QROWS):
        rows = slice(row0, row0 + QROWS)
        back = nn(mixed_grad[rows, :], w_down[...]) * slope[rows, :].astype(F32)
        preact_grad[rows, :] = back.astype(BF16)
        total[rows, :] += nt(preact_grad[rows, :], w_up[...])
    block = mixed_grad.shape[1] // COLUMNS
    for at in range(COLUMNS):
        features = slice(block * at, block * (at + 1))
        if len(outs) == 1:
            owner = place[1] ^ block_mask(at, place[0])
            up, down = outs[0].at[spot(2 * owner, block)], outs[0].at[spot(2 * owner + 1, block)]
        elif at < 3:
            up, down = outs[at].at[:block], outs[at].at[block:]
        else:
            up, down = outs[3:]
        up[...] = tn(normed_mid[:, features], preact_grad[...]).astype(BF16)
        down[...] = tn(mixed_grad[:, features], hidden[...]).astype(BF16)

    @pl.when(step == pl.num_programs(0) - 1)
    def _():
        mid_grad[...] = total[...].astype(BF16)


def hidden_backward(place, mixed_grad, normed_mid, w_up, w_down, hidden, slope, size, heights):
    length, width = mixed_grad.shape
    total = hidden.shape[1]
    whole = pl.BlockSpec((length, width), lambda j, place: (0, 0))
    column = lambda rows: pl.BlockSpec((rows, size), lambda j, place: (0, j))
    return placed_call(
        hidden_back_kernel,
        place,
        (mixed_grad, normed_mid, w_up, w_down, hidden, slope),
        [whole, whole, column(width), column(width), column(length), column(length)],
        [column(rows) for rows in heights] + [whole],
        [((rows, total), BF16) for rows in heights] + [((length, width), BF16)],
        (total // size,),
        [pltpu.VMEM((length, size), BF16), pltpu.VMEM((length, width), F32)],
    )


def rms_row(values):
    return lax.rsqrt(jnp.mean(values * values, axis=-1, keepdims=True) + EPSILON)


def both(left, right):
    block = left.shape[1] // COLUMNS
    turned = [right[:, block * at : block * (at + 1)].astype(F32) for at in (0, 2, 1, 3)]
    return left[...].astype(F32) + jnp.concatenate(turned, axis=1)


def back_row(values, gain, upstream):
    inverse = rms_row(values)
    normed = values * inverse
    scaled = upstream * gain
    back = inverse * (scaled - normed * jnp.mean(scaled * normed, axis=-1, keepdims=True))
    product = upstream * normed
    return back, jnp.sum(product.reshape(-1, 8, product.shape[1]), axis=0)


def gather_gain(out, parts):
    @pl.when(pl.program_id(0) == 0)
    def _():
        out[...] = jnp.zeros_like(out)

    for at, part in enumerate(parts):
        out[at] += part


def row_call(kernel, arrays, tables, outs, gains=0):
    length, width = arrays[0].shape
    by_row = pl.BlockSpec((QROWS, width), lambda i: (i, 0))
    out_specs = [by_row] * len(outs)
    out_shape = [jax.ShapeDtypeStruct((length, width), kind) for kind in outs]
    if gains:
        out_specs.append(pl.BlockSpec((gains, 8, width), lambda i: (0, 0, 0)))
        out_shape.append(jax.ShapeDtypeStruct((gains, 8, width), F32))
    return pl.pallas_call(
        kernel,
        grid=(length // QROWS,),
        in_specs=[by_row] * len(arrays)
        + [pl.BlockSpec(table.shape, lambda i: (0, 0)) for table in tables],
        out_specs=out_specs,
        out_shape=out_shape,
        compiler_params=ROOMY,
        cost_estimate=cost(6),
    )(*arrays, *tables)


def norm_kernel(values, gain, normed):
    rows = values[...].astype(F32)
    normed[...] = (rows * rms_row(rows) * gain[0:1, :]).astype(BF16)


def middle_row(layer_in, low, other, gain):
    branch = both(low, other)
    return layer_in[...].astype(F32) + branch * rms_row(branch) * gain[1:2, :], branch


def middle_kernel(layer_in, low, other, gain, normed_mid):
    middle, _ = middle_row(layer_in, low, other, gain)
    normed_mid[...] = (middle * rms_row(middle) * gain[2:3, :]).astype(BF16)


def result_kernel(layer_in, low, other, mixed_low, mixed_other, gain, follow, result, normed):
    middle, _ = middle_row(layer_in, low, other, gain)
    mixed = both(mixed_low, mixed_other)
    result[...] = (middle + mixed * rms_row(mixed) * gain[3:4, :]).astype(BF16)
    rows = result[...].astype(F32)
    normed[...] = (rows * rms_row(rows) * follow[0:1, :]).astype(BF16)


def mixed_back_kernel(mixed_low, mixed_other, upstream, gain, mixed_grad, gains):
    back, part = back_row(
        both(mixed_low, mixed_other), gain[3:4, :], upstream[...].astype(F32)
    )
    mixed_grad[...] = back.astype(BF16)
    gather_gain(gains, [part])


def middle_back_kernel(
    layer_in, low, other, upstream, mid_low, mid_other, gain, branch_grad, middle_grad, gains
):
    middle, branch = middle_row(layer_in, low, other, gain)
    back, part_two = back_row(middle, gain[2:3, :], both(mid_low, mid_other))
    total = upstream[...].astype(F32) + back
    middle_grad[...] = total
    back, part_one = back_row(branch, gain[1:2, :], total)
    branch_grad[...] = back.astype(BF16)
    gather_gain(gains, [part_one, part_two])


def input_back_kernel(layer_in, middle_grad, low, other, gain, grad, gains):
    back, part = back_row(layer_in[...].astype(F32), gain[0:1, :], both(low, other))
    grad[...] = (middle_grad[...] + back).astype(BF16)
    gather_gain(gains, [part])


def join_kernel(near, arrived, out):
    out[...] = (near[...].astype(F32) + arrived[...].astype(F32)).astype(BF16)


def join_half(near, arrived, half):
    rows, size = arrived.shape
    return pl.pallas_call(
        join_kernel,
        grid=(4,),
        in_specs=[
            pl.BlockSpec((rows, size // 4), lambda j: (half, j)),
            pl.BlockSpec((rows, size // 4), lambda j: (0, j)),
        ],
        out_specs=pl.BlockSpec((rows, size // 4), lambda j: (half, j)),
        out_shape=jax.ShapeDtypeStruct(near.shape, BF16),
        input_output_aliases={0: 0},
        compiler_params=ROOMY,
        cost_estimate=cost(3.7),
    )(near, arrived)


def total_kernel(count, *refs):
    sources, slots = refs[:-count], refs[-count:]
    low = 0
    for own, from_x, from_y in zip(sources[0::3], sources[1::3], sources[2::3]):
        high = low + own.shape[0]
        size = own.shape[1] // count
        for at, slot in enumerate(slots):
            part = slice(size * at, size * (at + 1))
            slot[low:high, :] = (
                own[:, part].astype(F32) + from_x[:, part].astype(F32) + from_y[:, part].astype(F32)
            ).astype(BF16)
        low = high


def total_slots(triples, count):
    sources = [item for triple in triples for item in triple]
    rows = sum(triple[0].shape[0] for triple in triples)
    shape = (rows, sources[0].shape[1] // count)
    return pl.pallas_call(
        partial(total_kernel, count),
        out_shape=[jax.ShapeDtypeStruct(shape, BF16)] * count,
        compiler_params=ROOMY,
        cost_estimate=cost(5),
    )(*sources)


def ring(length, by):
    return [(i, (i + by) % length) for i in range(length)]


def other_core(values):
    return lax.ppermute(values, "section", [(0, 1), (1, 0)])


def block_mask(at, section):
    return at ^ (3 * section * ((at ^ (at >> 1)) & 1))


def turn_blocks(values, section, column, axis):
    size = values.shape[axis] // COLUMNS
    blocks = [
        lax.dynamic_slice_in_dim(
            values, (column ^ block_mask(block, section)) * size, size, axis
        )
        for block in range(COLUMNS)
    ]
    return jnp.concatenate(blocks, axis=axis)


def unturn(values, section, column):
    size = values.shape[1] // COLUMNS
    blocks = []
    for block in range(COLUMNS):
        at = block_mask(column ^ block, section)
        blocks.append(lax.dynamic_slice_in_dim(values, at * size, size, 1))
    return jnp.concatenate(blocks, axis=1)


class Channel:
    def __init__(self, depth):
        self.depth = depth
        self.sent = []

    def send(self, values, axes, pairs):
        if len(self.sent) >= self.depth:
            (values,) = hold([values], self.sent[-self.depth])
        got = lax.ppermute(values, axes, pairs)
        self.sent.append(got)
        return got


class Links:
    def __init__(self, count):
        self.count = count
        self.columns = Channel(COLUMN_DEPTH)
        self.tensor = Channel(TENSOR_DEPTH)

    def across(self, values, masks):
        pairs = [
            (core * COLUMNS + at, core * COLUMNS + (at ^ masks[core]))
            for core in range(2)
            for at in range(COLUMNS)
        ]
        return self.columns.send(values, ("section", "dp"), pairs)

    def near(self, values):
        return self.across(values, (1, 2))

    def other(self, values):
        return self.across(values, (2, 1))

    def along(self, values, by):
        return self.tensor.send(values, "tensor", ring(self.count, by % self.count))

    def relay(self, first, second):
        half = first.shape[0] // 2
        return self.other(first[:half]), self.near(second[half:])


def spot(index, size):
    return pl.ds(pl.multiple_of(index * size, size), size)


def placed_call(
    kernel, place, operands, in_specs, out_specs, shapes, grid, scratch=(), aliases=None
):
    return pl.pallas_call(
        kernel,
        grid_spec=pltpu.PrefetchScalarGridSpec(
            num_scalar_prefetch=1,
            grid=grid,
            in_specs=in_specs,
            out_specs=out_specs,
            scratch_shapes=scratch,
        ),
        out_shape=[jax.ShapeDtypeStruct(shape, kind) for shape, kind in shapes],
        input_output_aliases=aliases or {},
        compiler_params=ROOMY,
        cost_estimate=cost(6),
    )(place, *operands)


def whole_spec(shape):
    return pl.BlockSpec(shape, lambda *_: (0,) * len(shape))


def slab_kernel(place, *refs):
    (keep_attn, keep_mlp, send_attn, send_mlp) = refs[8:]
    lanes = refs[1].shape[0] // 2
    hidden = refs[3].shape[0] // 2
    for sources, attn, mlp, core in (
        (refs[:4], keep_attn, keep_mlp, place[0]),
        (refs[4:8], send_attn, send_mlp, 1 - place[0]),
    ):
        w_in, w_out, w_up, w_down = sources
        for part in range(3):
            attn[:, lanes * part : lanes * (part + 1)] = w_in[:, spot(2 * part + core, lanes)]
        attn[:, 3 * lanes :] = w_out[spot(core, lanes), :].T
        mlp[:, :hidden] = w_up[:, spot(core, hidden)]
        mlp[:, hidden:] = w_down[spot(core, hidden), :].T


def make_slabs(place, w_in, w_out, w_up, w_down):
    width = w_in.shape[0]
    rows = width // COLUMNS
    lanes, hidden = (w_out.shape[0] // 2, w_down.shape[0] // 2)
    at = lambda r, place: place[1] ^ block_mask(r, place[0])
    other = lambda r, place: place[1] ^ block_mask(r, 1 - place[0])
    by_row = lambda size, which: pl.BlockSpec((rows, size), lambda r, p: (which(r, p), 0))
    by_column = lambda size, which: pl.BlockSpec((size, rows), lambda r, p: (0, which(r, p)))
    result = lambda size: pl.BlockSpec((rows, size), lambda r, place: (r, 0))
    sizes = (4 * lanes, 2 * hidden, 4 * lanes, 2 * hidden)
    return placed_call(
        slab_kernel,
        place,
        (w_in, w_out, w_up, w_down) * 2,
        [
            make(size, which)
            for which in (at, other)
            for make, size in (
                (by_row, 6 * lanes),
                (by_column, 2 * lanes),
                (by_row, 2 * hidden),
                (by_column, 2 * hidden),
            )
        ],
        [result(size) for size in sizes],
        [((width, size), BF16) for size in sizes],
        (COLUMNS,),
    )


def enter_kernel(place, owned, theirs, out):
    count = 4
    half = owned.shape[0] // count
    block = out.shape[1] // COLUMNS
    for by in range(count):
        source = (place[2] + count - by) % count
        for held, core in ((owned, place[0]), (theirs, 1 - place[0])):
            for at in range(COLUMNS):
                out[spot(2 * source + core, half), block * at : block * (at + 1)] = held[
                    half * by : half * (by + 1), spot(place[1] ^ block_mask(at, place[0]), block)
                ]


def hold(values, *others):
    return lax.optimization_barrier((*values, *others))[: len(values)]


def send_rows(links, blocks, section, tensor, count, *others):
    _, rows, width = blocks.shape
    half = rows // 2
    mine = lambda pack: lax.dynamic_slice(blocks, (pack, section * half, 0), (1, half, width))[0]
    sent = hold([mine((tensor + by) % count) for by in range(count)], *others)
    return [sent[0]] + [links.along(sent[by], by) for by in range(1, count)]


def enter_rows(place, got):
    owned = jnp.concatenate(got)
    theirs = other_core(owned)
    shape = (2 * owned.shape[0], owned.shape[1])
    return placed_call(
        enter_kernel,
        place,
        (owned, theirs),
        [whole_spec(owned.shape)] * 2,
        [whole_spec(shape)],
        [(shape, BF16)],
        (1,),
    )[0]


def leave_kernel(place, *refs):
    out = refs[-1]
    rows = refs[0].shape[0]
    count = out.shape[0] // rows
    block = out.shape[1] // COLUMNS
    for layer in range(2):

        @pl.when(place[0] == layer)
        def _():
            start = count * layer if len(refs) > count + 1 else 0
            for by, held in enumerate(refs[start : start + count]):
                source = (place[2] + count - by) % count
                for at in range(COLUMNS):
                    target = spot(place[1] ^ block_mask(at, layer), block)
                    out[spot(source, rows), target] = held[:, block * at : block * (at + 1)]


def rows_out(values, core, tensor, count, *others):
    length, width = values.shape
    rows = length // count
    blocks = hold(
        [
            lax.dynamic_slice(values, (((tensor + by) % count) * rows, 0), (rows, width))
            for by in range(count)
        ],
        *others,
    )
    pairs = lambda by: [(core * count + i, core * count + (i + by) % count) for i in range(count)]
    return [blocks[0]] + [
        lax.ppermute(blocks[by], ("section", "tensor"), pairs(by)) for by in range(1, count)
    ]


def leave_rows(place, first, second=()):
    rows, width = first[0].shape
    count = len(first)
    shape = (rows * count, width)
    out = placed_call(
        leave_kernel,
        place,
        (*first, *second),
        [whole_spec((rows, width))] * (count + len(second)),
        [whole_spec(shape)],
        [(shape, BF16)],
        (1,),
    )[0]
    return out.reshape(count, rows, width)


def assemble_kernel(layer, pieces, place, keep, theirs, *refs):
    blocks, outs = refs[:pieces], refs[pieces:]
    rows = keep.shape[0] // COLUMNS

    def put(target, size, read):
        start = 0
        for out in outs:
            part = out.shape[1] // 4
            out[target : target + size, read[0] * part : (read[0] + 1) * part] = read[1](
                start, start + part
            )
            start += part

    for mine, held in ((True, keep), (False, theirs)):

        @pl.when((place[0] == layer) == mine)
        def _():
            put(0, keep.shape[0], (0, lambda low, high: held[:, low:high]))

    if pieces == 1:
        for at in range(COLUMNS):
            owner = place[1] ^ block_mask(at, place[0])
            for slot in range(3):
                source = spot(3 * owner + slot, rows)
                put(rows * at, rows, (slot + 1, lambda low, high: blocks[0][source, low:high]))
        return
    own, from_x, from_y, far_low, far_high = blocks
    half = far_low.shape[0]
    for at, held in enumerate((own, from_x, from_y)):
        for slot in range(3):
            put(
                rows * at,
                rows,
                (slot + 1, lambda low, high: held[rows * slot : rows * (slot + 1), low:high]),
            )
    step = rows // 2
    for chunk in range(6):
        held, start = (far_low, chunk * step) if chunk < 3 else (far_high, chunk * step - half)
        put(
            3 * rows + (chunk % 2) * step,
            step,
            (chunk // 2 + 1, lambda low, high: held[start : start + step, low:high]),
        )


def assemble(layer, place, keep, theirs, blocks, parts):
    operands = (keep, theirs, *blocks)
    return placed_call(
        partial(assemble_kernel, layer, len(blocks)),
        place,
        operands,
        [whole_spec(item.shape) for item in operands],
        [whole_spec((keep.shape[0], 4 * part)) for part in parts],
        [((keep.shape[0], 4 * part), BF16) for part in parts],
        (1,),
    )


def add_low(*terms):
    total = terms[0].astype(F32)
    for term in terms[1:]:
        total = total + term.astype(F32)
    return total.astype(BF16)


def finish_kernel(place, *refs):
    sources, (g_in, g_out, g_up, g_down, attn, mlp, sems) = refs[:8], refs[8:]
    step = pl.program_id(0)
    rows = g_in.shape[0]
    lanes = g_out.shape[0] // 2
    hidden = g_down.shape[0] // 2
    core = place[0]

    @pl.when(step == 0)
    def _():
        for layer in range(2):

            @pl.when(core == layer)
            def _():
                own_attn, own_mlp, got_attn, got_mlp = sources[4 * layer : 4 * layer + 4]
                copies = [
                    pltpu.make_async_copy(own_attn, attn.at[layer], sems.at[0]),
                    pltpu.make_async_copy(got_attn, attn.at[1 - layer], sems.at[1]),
                    pltpu.make_async_copy(own_mlp, mlp.at[layer], sems.at[2]),
                    pltpu.make_async_copy(got_mlp, mlp.at[1 - layer], sems.at[3]),
                ]
                for copy in copies:
                    copy.start()
                for copy in copies:
                    copy.wait()

    for half in range(2):
        at = block_mask(place[1] ^ step, half)
        attn_rows = spot(at, rows)
        up_rows = spot(2 * at, rows)
        down_rows = spot(2 * at + 1, rows)
        for part in range(3):
            start = (2 * part + half) * lanes
            g_in[:, start : start + lanes] = attn[
                half, attn_rows, lanes * part : lanes * (part + 1)
            ].astype(F32)
        g_out[lanes * half : lanes * (half + 1), :] = (
            attn[half, attn_rows, 3 * lanes :].astype(F32).T
        )
        g_up[:, hidden * half : hidden * (half + 1)] = mlp[half, up_rows, :].astype(F32)
        g_down[hidden * half : hidden * (half + 1), :] = mlp[half, down_rows, :].astype(F32).T


def finish(place, sources, lanes, hidden):
    width = sources[0].shape[0]
    rows = width // COLUMNS
    return placed_call(
        finish_kernel,
        place,
        sources,
        [pl.BlockSpec(memory_space=pl.ANY)] * 8,
        [
            pl.BlockSpec((rows, 6 * lanes), lambda b, place: (b, 0)),
            pl.BlockSpec((2 * lanes, rows), lambda b, place: (0, b)),
            pl.BlockSpec((rows, 2 * hidden), lambda b, place: (b, 0)),
            pl.BlockSpec((2 * hidden, rows), lambda b, place: (0, b)),
        ],
        [
            ((width, 6 * lanes), F32),
            ((2 * lanes, width), F32),
            ((width, 2 * hidden), F32),
            ((2 * hidden, width), F32),
        ],
        (COLUMNS,),
        [
            pltpu.VMEM((2, *sources[0].shape), BF16),
            pltpu.VMEM((2, *sources[1].shape), BF16),
            pltpu.SemaphoreType.DMA((4,)),
        ],
    )


class Flow:
    def __init__(self):
        self.table = {}
        self.at = 0

    def plan(self, at, action):
        self.table.setdefault(max(at, self.at), []).append(action)

    def point(self, token, *inputs):
        launched = []
        while self.table.get(self.at):
            launched += self.table[self.at].pop(0)(token)
        self.at += 1
        return hold(inputs, *launched) if launched else inputs

    def drain(self):
        while any(self.table.values()):
            at = min(key for key, actions in self.table.items() if actions)
            self.table[at].pop(0)(None)


def held(values, token):
    return values if token is None else hold(values, token)


def column_stage(links, state, token):
    far_low, far_high = held(state["far"], token)
    to_x = join_half(state["at_x"], far_low, 0)
    to_y = join_half(state["at_y"], far_high, 1)
    state["near"] = (links.near(to_x), links.other(to_y))
    return [to_x, to_y]


def slot_stage(links, states, total, token):
    count = links.count
    if "sum" in states[0]:
        sums = held(tuple(state["sum"] for state in states), token)
        size = sums[0].shape[1] // count
        slots = [
            jnp.concatenate([item[:, size * at : size * (at + 1)] for item in sums])
            for at in range(count)
        ]
    else:
        slots = total_slots([(state["own"], *held(state["near"], token)) for state in states], count)
    total["slots"] = slots
    total["near"] = links.along(slots[2], -1)
    total["last"] = links.along(slots[3], 1)
    return slots[2:]


def arrive(state, token):
    (state["sum"],) = held((state["sum"],), token)
    return [state["sum"]]


def relay_stage(links, total, token):
    (near,) = held((total["near"],), token)
    relayed = add_low(total["slots"][1], near)
    total["near"] = links.along(relayed, -1)
    return [relayed]


def spread_stage(links, total, token):
    came = held((total["near"], total["last"]), token)
    own = add_low(total["slots"][0], *came)
    total["blocks"] = (own, links.near(own), links.other(own))
    return [own]


def far_stage(links, total, token):
    own, from_x, from_y = total["blocks"]
    from_x, from_y = held((from_x, from_y), token)
    total["blocks"] = (own, from_x, from_y, *links.relay(from_x, from_y))
    return []


def sum_everywhere(values):
    swap = lambda axis, by: lax.ppermute(
        values, axis, [(i, i ^ by) for i in range(lax.axis_size(axis))]
    )
    for axis, by in (("dp", 1), ("dp", 2), ("tensor", 1), ("tensor", 2)):
        values = values + swap(axis, by)
    return values


def per_chip(
    inputs, segments, projection_in, projection_out, up_weight, down_weight, norm_gains, cotangent
):
    section = lax.axis_index("section")
    column = lax.axis_index("dp")
    tensor = lax.axis_index("tensor")
    count = lax.axis_size("tensor")
    width = inputs.shape[3]
    length = inputs.shape[2] * count
    lanes = projection_out.shape[1] // 2
    hidden = up_weight.shape[2] // 2

    place = jnp.stack([section, column, tensor]).astype(jnp.int32)
    keep_attn, keep_mlp, send_attn, send_mlp = make_slabs(
        place,
        projection_in[0].reshape(width, 6 * lanes),
        projection_out[0],
        up_weight[0],
        down_weight[0],
    )
    attn_slabs = (keep_attn, other_core(send_attn))
    mlp_slabs = (keep_mlp, other_core(send_mlp))
    gains_other = other_core(norm_gains[0])
    gains = [
        turn_blocks(
            jnp.where(section == layer, norm_gains[0], gains_other), section, column, 1
        )
        for layer in range(2)
    ]
    rows = width // COLUMNS
    piece = lambda slabs, layer: jnp.where(section == layer, slabs[0][:rows], slabs[1][:rows])
    attn_parts, mlp_parts = ((3 * lanes, lanes), (hidden, hidden))
    links = Links(count)
    everywhere = lambda values: lax.all_gather(values, "dp", axis=0, tiled=True)
    hop = lambda values: (links.along(values, 1), links.along(values, -1))
    segment = lax.dynamic_index_in_dim(segments[0], tensor, 0, keepdims=False)
    cosine, sine = rope_lanes(length, lanes)
    tables = (cosine, sine, segment[:, None], segment[None, :])

    block = min(512, hidden)
    a_first, a_last = hop(piece(attn_slabs, 0))
    (m_own,) = hold([piece(mlp_slabs, 0)], a_first, a_last, cosine, sine, *gains)
    a_second = links.along(a_first, 1)
    m_first, m_last = hop(m_own)
    a_z = jnp.concatenate([a_first, a_second, a_last])
    a_x, a_y = links.near(a_z), links.other(a_z)
    m_second = links.along(m_first, 1)
    got = send_rows(links, inputs[0], section, tensor, count, m_first, m_last)
    a_far = links.relay(a_x, a_y)
    (m_z,) = hold([jnp.concatenate([m_first, m_second, m_last])], *a_far)
    m_all = everywhere(m_z)
    w_in, w_out = assemble(0, place, *attn_slabs, (a_z, a_x, a_y, *a_far), attn_parts)
    got = hold(got, w_out)
    layer_in = enter_rows(place, got)
    (b_own,) = hold([piece(attn_slabs, 1)], *got)
    b_first, b_last = hop(b_own)
    (normed,) = row_call(norm_kernel, [layer_in], [gains[0]], [BF16])
    b_second = links.along(b_first, 1)
    (n_own,) = hold([piece(mlp_slabs, 1)], b_first, b_last)
    qkv, attended = attend_forward(normed, w_in, tables, lanes, 0, 2)
    b_second, b_last = hold((b_second, b_last), attended)
    n_first, n_last = hop(n_own)
    b_z = jnp.concatenate([b_first, b_second, b_last])
    b_all = everywhere(b_z)
    (normed_b,) = hold([normed], b_z, n_own)
    qkv, attended = attend_forward(normed_b, w_in, tables, lanes, 2, 2, (qkv, attended))
    n_first, n_last = hold((n_first, n_last), attended)
    n_second = links.along(n_first, 1)
    (attended_b,) = hold([attended], n_first)
    branch = outward(attended_b, w_out)
    branch = (branch, other_core(branch))
    (normed_mid,) = row_call(middle_kernel, [layer_in, *branch], [gains[0]], [BF16])
    m_all, n_second, n_last = hold((m_all, n_second, n_last), normed_mid)
    w_up, w_down = assemble(0, place, *mlp_slabs, (m_all,), mlp_parts)
    n_z = jnp.concatenate([n_first, n_second, n_last])
    n_all = everywhere(n_z)
    got = send_rows(links, cotangent[0], section, tensor, count, n_z)
    (normed_b,) = hold([normed_mid], n_z)
    hid, slope, mixed = hidden_forward(normed_b, w_up, w_down, block)
    mixed_b, *got = hold([mixed, *got])
    upstream = enter_rows(place, got)
    mixed = (mixed_b, other_core(mixed_b))
    result, normed_next = row_call(
        result_kernel, [layer_in, *branch, *mixed], [gains[0], gains[1]], [BF16, BF16]
    )
    entering = [layer_in, result]
    weights = [(w_in, w_out, w_up, w_down)]
    saved = [(branch, mixed, normed, normed_mid, qkv, attended, hid, slope)]
    b_all, upstream = hold((b_all, upstream), result)
    w_in, w_out = assemble(1, place, *attn_slabs, (b_all,), attn_parts)
    layer_in = result
    normed = normed_next
    left = [rows_out(entering[1], 0, tensor, count, w_in)]
    (normed_b,) = hold([normed], left[0][0])
    qkv, attended = attend_forward(normed_b, w_in, tables, lanes, 0, 4)
    attended_b, *left[0] = hold([attended, *left[0]])
    branch = outward(attended_b, w_out)
    branch = (branch, other_core(branch))
    (normed_mid,) = row_call(middle_kernel, [layer_in, *branch], [gains[1]], [BF16])
    (n_all,) = hold([n_all], normed_mid)
    w_up, w_down = assemble(1, place, *mlp_slabs, (n_all,), mlp_parts)
    hid, slope, mixed = hidden_forward(normed_mid, w_up, w_down, block)
    mixed = (mixed, other_core(mixed))
    result, _ = row_call(
        result_kernel, [layer_in, *branch, *mixed], [gains[1], gains[1]], [BF16, BF16]
    )
    weights.append((w_in, w_out, w_up, w_down))
    saved.append((branch, mixed, normed, normed_mid, qkv, attended, hid, slope))
    flow = Flow()

    def plan_totals(layer, states, steps):
        total = {}
        totals[layer].append(total)
        for at, stage in zip(steps, (slot_stage, relay_stage, spread_stage, far_stage)):
            item = (states, total) if stage is slot_stage else (total,)
            flow.plan(at, partial(stage, links, *item))

    totals = [[], []]
    gain_sums = [None, None]
    input_grads = [None, None]

    def send_grads(token):
        grads = jnp.where(section == 0, *input_grads)
        size = grads.shape[0] // count
        blocks = [
            lax.dynamic_slice_in_dim(grads, ((tensor + by) % count) * size, size, 0)
            for by in range(count)
        ]
        left.append([blocks[0]] + [links.along(blocks[by], by) for by in range(1, count)])
        return []

    def reduction(parts):
        if len(parts) == 1:
            return {"sum": lax.psum_scatter(parts[0], "dp", scatter_dimension=0, tiled=True)}
        own, at_x, at_y, far_low, far_high = parts
        far = (links.other(far_low), links.near(far_high))
        return {"own": own, "at_x": at_x, "at_y": at_y, "far": far}

    for layer in (1, 0):
        layer_in = entering[layer]
        gain = gains[layer]
        w_in, w_out, w_up, w_down = weights[layer]
        branch, mixed, normed, normed_mid, qkv, attended, hid, slope = saved[layer]
        mixed_grad, part_three = row_call(
            mixed_back_kernel, [*mixed, upstream], [gain], [BF16], 1
        )
        (mixed_grad,) = flow.point(mixed_grad, mixed_grad)
        heights = (2 * rows, 2 * rows, 2 * rows, rows, rows) if layer == 0 else (2 * width,)
        *parts, mid_low = hidden_backward(
            place, mixed_grad, normed_mid, w_up, w_down, hid, slope, block, heights
        )
        mlp = reduction(parts)
        (mid_low,) = flow.point(mid_low, mid_low)
        mid_other = other_core(mid_low)
        branch_grad, middle_grad, part_two = row_call(
            middle_back_kernel,
            [layer_in, *branch, upstream, mid_low, mid_other],
            [gain],
            [BF16, F32],
            2,
        )
        if layer == 0:
            flow.plan(7, partial(column_stage, links, mlp))
        (branch_grad,) = flow.point(branch_grad, branch_grad)
        heights = (rows, rows, rows, rows // 2, rows // 2) if layer == 0 else (width,)
        shared = (normed, qkv, attended, w_in, w_out, tables, lanes, heights)
        if layer:
            leaving = rows_out(result, 1, tensor, count, branch_grad)
            (branch_grad,) = hold([branch_grad], leaving[0])
            parts = attend_backward(place, branch_grad, *shared, 0, 2)
            branch_grad, *leaving = hold([branch_grad, *leaving], parts[-1])
            left.append(leaving)
            *parts, normed_low = attend_backward(place, branch_grad, *shared, 2, 2, parts)
        else:
            *parts, normed_low = attend_backward(place, branch_grad, *shared, 0, 4)
        attn = reduction(parts)
        if layer:
            flow.plan(6, partial(arrive, mlp))
            plan_totals(1, [mlp, attn], (7, 8, 10, 13))
        else:
            flow.plan(9, partial(column_stage, links, attn))
            plan_totals(0, [mlp], (8, 11, 14, 16))
            plan_totals(0, [attn], (12, 15, 17, 18))
            flow.plan(13, send_grads)
        (normed_low,) = flow.point(normed_low, normed_low)
        normed_other = other_core(normed_low)
        grad, part_zero = row_call(
            input_back_kernel, [layer_in, middle_grad, normed_low, normed_other], [gain], [BF16], 1
        )
        (grad,) = flow.point(grad, grad)
        gain_sums[layer] = jnp.sum(
            jnp.concatenate([part_zero, part_two, part_three]), axis=1
        )
        input_grads[layer] = grad
        upstream = grad
    flow.drain()
    layer_store = leave_rows(place, left[0], left[1])
    grad_store = leave_rows(place, left[2])
    gain_total = sum_everywhere(unturn(jnp.concatenate(gain_sums), section, column))
    gain_total = jnp.where(section == 0, gain_total[:4], gain_total[4:])
    (both_parts,) = totals[1]
    own, from_x, from_y, far_low, far_high = both_parts["blocks"]
    far_rows = jnp.concatenate([far_low, far_high])
    upper = (own, from_x, from_y, far_rows)
    sums = [
        tuple(jnp.concatenate(total["blocks"]) for total in reversed(totals[0])),
        (
            jnp.concatenate([item[2 * rows :] for item in upper]),
            jnp.concatenate([item[: 2 * rows] for item in upper]),
        ),
    ]
    sources = []
    for layer in range(2):
        got = [lax.ppermute(item, "section", [(1 - layer, layer)]) for item in sums[layer]]
        sources += [*sums[layer], *got]
    in_grad, out_grad, up_grad, down_grad = finish(place, sources, lanes, hidden)
    return (
        layer_store[None, None],
        grad_store[None, None],
        in_grad.reshape(1, width, 3, 2 * lanes),
        out_grad[None],
        up_grad[None],
        down_grad[None],
        gain_total[None],
    )


def one_pack_per_chip(mesh):
    return mesh.shape["section"] == 2 and mesh.shape["tensor"] == 4 and mesh.shape["dp"] == 4


def solution(mesh):
    placed = (
        P("dp", None, "tensor", None),
        P("dp", None, None),
        P("section", None, None, "tensor"),
        P("section", "tensor", None),
        P("section", None, "tensor"),
        P("section", "tensor", None),
        P("section", None, None),
        P("dp", None, "tensor", None),
    )
    body = per_chip if one_pack_per_chip(mesh) else per_device
    return jax.shard_map(
        body,
        mesh=mesh,
        in_specs=placed,
        out_specs=(
            P("section", "dp", None, "tensor", None),
            P("section", "dp", None, "tensor", None),
            P("section", None, None, "tensor"),
            P("section", "tensor", None),
            P("section", None, "tensor"),
            P("section", "tensor", None),
            P("section", None, None),
        ),
        check_vma=False,
    )
```

```python
from functools import partial
import math

import jax
import jax.numpy as jnp
from jax import lax
from jax.experimental import pallas as pl
from jax.experimental.pallas import tpu as pltpu
from jax.sharding import PartitionSpec as P

HEAD_DIM = 64
QBLOCK = 512


EPSILON = 1e-05
ROTARY_BASE = 10000.0
NEGATIVE = -1e30


def from_behind(shard, axis, by):
    length = lax.axis_size(axis)
    pairs = [(i, i + by) for i in range(length) if 0 <= i + by < length]
    return lax.ppermute(shard, axis, pairs)


def rms_parts(values, gain):
    inverse = lax.rsqrt(jnp.mean(values * values, axis=-1, keepdims=True) + EPSILON)
    return (values * inverse * gain, inverse)


def rms_back(values, inverse, gain, upstream):
    normed = values * inverse
    scaled = upstream * gain
    back = inverse * (scaled - normed * jnp.mean(scaled * normed, axis=-1, keepdims=True))
    return (back, jnp.sum(upstream * normed, axis=0))


def rotary_tables(length):
    half = HEAD_DIM // 2
    freqs = ROTARY_BASE ** (-2.0 * jnp.arange(half, dtype=jnp.float32) / HEAD_DIM)
    angles = jnp.arange(length, dtype=jnp.float32)[:, None] * freqs[None, :]
    return (jnp.cos(angles)[:, None, :], jnp.sin(angles)[:, None, :])


def rotate(values, cosine, sine):
    half = values.shape[-1] // 2
    first = values[..., :half]
    second = values[..., half:]
    return jnp.concatenate(
        [first * cosine - second * sine, second * cosine + first * sine], axis=-1
    )


def unrotate(upstream, cosine, sine):
    half = upstream.shape[-1] // 2
    first = upstream[..., :half]
    second = upstream[..., half:]
    return jnp.concatenate(
        [first * cosine + second * sine, second * cosine - first * sine], axis=-1
    )


def times_transposed(left, right):
    return lax.dot_general(
        left, right, (((1,), (1,)), ((), ())), preferred_element_type=jnp.float32
    )


def transposed_times(left, right):
    return lax.dot_general(
        left, right, (((0,), (0,)), ((), ())), preferred_element_type=jnp.float32
    )


def split_heads(projected, inner, cosine, sine):
    length = projected.shape[0]
    heads = inner // HEAD_DIM
    queries = rotate(projected[:, :inner].reshape(length, heads, HEAD_DIM), cosine, sine).astype(
        jnp.bfloat16
    )
    keys = rotate(
        projected[:, inner : 2 * inner].reshape(length, heads, HEAD_DIM), cosine, sine
    ).astype(jnp.bfloat16)
    values = projected[:, 2 * inner :].reshape(length, heads, HEAD_DIM).astype(jnp.bfloat16)
    return (queries, keys, values)


def block_scores(query_block, keys, segment_block, position_block, segment, position):
    scale = 1.0 / math.sqrt(HEAD_DIM)
    scores = (
        jnp.einsum("qhd,khd->hqk", query_block, keys, preferred_element_type=jnp.float32) * scale
    )
    allowed = (segment_block[:, None] == segment[None, :]) & (
        position_block[:, None] >= position[None, :]
    )
    return jnp.where(allowed[None], scores, NEGATIVE)


def attend(queries, keys, values, segment):
    length, heads, width = queries.shape
    blocks = length // QBLOCK
    position = jnp.arange(length, dtype=jnp.int32)

    def one_block(pieces):
        query_block, segment_block, position_block = pieces
        scores = block_scores(query_block, keys, segment_block, position_block, segment, position)
        largest = jnp.max(scores, axis=-1, keepdims=True)
        exponent = jnp.exp(scores - largest)
        totals = jnp.sum(exponent, axis=-1, keepdims=True)
        probs = (exponent / totals).astype(jnp.bfloat16)
        mixed = jnp.einsum("hqk,khd->qhd", probs, values, preferred_element_type=jnp.float32)
        return (
            mixed.reshape(QBLOCK, heads * width).astype(jnp.bfloat16),
            (largest + jnp.log(totals))[..., 0],
        )

    attended, logsum = lax.map(
        one_block,
        (
            queries.reshape(blocks, QBLOCK, heads, width),
            segment.reshape(blocks, QBLOCK),
            position.reshape(blocks, QBLOCK),
        ),
    )
    return (attended.reshape(length, heads * width), logsum)


def attend_back(queries, keys, values, segment, logsum, upstream):
    length, heads, width = queries.shape
    blocks = length // QBLOCK
    scale = 1.0 / math.sqrt(width)
    position = jnp.arange(length, dtype=jnp.int32)

    def one_block(carry, pieces):
        key_grad, value_grad = carry
        query_block, segment_block, position_block, logsum_block, upstream_block = pieces
        scores = block_scores(query_block, keys, segment_block, position_block, segment, position)
        probs = jnp.exp(scores - logsum_block[:, :, None])
        upstream_heads = upstream_block.reshape(QBLOCK, heads, width)
        prob_grad = jnp.einsum(
            "qhd,khd->hqk", upstream_heads, values, preferred_element_type=jnp.float32
        )
        score_grad = (
            probs * (prob_grad - jnp.sum(probs * prob_grad, axis=-1, keepdims=True))
        ).astype(jnp.bfloat16)
        query_grad = (
            jnp.einsum("hqk,khd->qhd", score_grad, keys, preferred_element_type=jnp.float32) * scale
        )
        key_grad = (
            key_grad
            + jnp.einsum(
                "hqk,qhd->khd", score_grad, query_block, preferred_element_type=jnp.float32
            )
            * scale
        )
        value_grad = value_grad + jnp.einsum(
            "hqk,qhd->khd",
            probs.astype(jnp.bfloat16),
            upstream_heads,
            preferred_element_type=jnp.float32,
        )
        return ((key_grad, value_grad), query_grad)

    zeros = jnp.zeros((length, heads, width), jnp.float32)
    carried, query_grad = lax.scan(
        one_block,
        (zeros, zeros),
        (
            queries.reshape(blocks, QBLOCK, heads, width),
            segment.reshape(blocks, QBLOCK),
            position.reshape(blocks, QBLOCK),
            logsum,
            upstream.reshape(blocks, QBLOCK, heads * width),
        ),
    )
    return (query_grad.reshape(length, heads, width), carried[0], carried[1])


def layer_forward(layer_in, segment, params):
    weight_in, weight_out, weight_up, weight_down, gain_table = params
    inner = weight_out.shape[0]
    inputs_float = layer_in.astype(jnp.float32)
    normed, _ = rms_parts(inputs_float, gain_table[0])
    normed_full = lax.all_gather(normed.astype(jnp.bfloat16), "tensor", axis=0, tiled=True)
    cosine, sine = rotary_tables(normed_full.shape[0])
    projected = jnp.dot(normed_full, weight_in, preferred_element_type=jnp.float32)
    queries, keys, values = split_heads(projected, inner, cosine, sine)
    attended, logsum = attend(queries, keys, values, segment)
    branch = lax.psum_scatter(
        jnp.dot(attended, weight_out, preferred_element_type=jnp.float32).astype(jnp.bfloat16),
        "tensor",
        scatter_dimension=0,
        tiled=True,
    ).astype(jnp.float32)
    branch_normed, _ = rms_parts(branch, gain_table[1])
    middle = inputs_float + branch_normed
    normed_mid, _ = rms_parts(middle, gain_table[2])
    mid_rows = lax.all_gather(normed_mid.astype(jnp.bfloat16), "tensor", axis=0, tiled=True)
    hidden = jax.nn.gelu(
        jnp.dot(mid_rows, weight_up, preferred_element_type=jnp.float32), approximate=False
    ).astype(jnp.bfloat16)
    mixed = lax.psum_scatter(
        jnp.dot(hidden, weight_down, preferred_element_type=jnp.float32).astype(jnp.bfloat16),
        "tensor",
        scatter_dimension=0,
        tiled=True,
    ).astype(jnp.float32)
    mixed_normed, _ = rms_parts(mixed, gain_table[3])
    return (middle + mixed_normed, (branch, mixed, attended, logsum, normed_full, mid_rows))


def layer_backward(layer_in, segment, params, kept, upstream):
    weight_in, weight_out, weight_up, weight_down, gain_table = params
    inner = weight_out.shape[0]
    branch, mixed, attended, logsum, normed_full, mid_rows = kept
    inputs_float = layer_in.astype(jnp.float32)
    _, in_inverse = rms_parts(inputs_float, gain_table[0])
    branch_normed, branch_inverse = rms_parts(branch, gain_table[1])
    middle = inputs_float + branch_normed
    _, mid_inverse = rms_parts(middle, gain_table[2])
    _, mixed_inverse = rms_parts(mixed, gain_table[3])
    mixed_grad, gain_three = rms_back(mixed, mixed_inverse, gain_table[3], upstream)
    mixed_rows = lax.all_gather(mixed_grad.astype(jnp.bfloat16), "tensor", axis=0, tiled=True)
    preact = jnp.dot(mid_rows, weight_up, preferred_element_type=jnp.float32)
    hidden, gelu_back = jax.vjp(partial(jax.nn.gelu, approximate=False), preact)
    hidden = hidden.astype(jnp.bfloat16)
    down_part = transposed_times(hidden, mixed_rows)
    preact_grad = gelu_back(times_transposed(mixed_rows, weight_down))[0].astype(jnp.bfloat16)
    up_part = transposed_times(mid_rows, preact_grad)
    mid_grad = lax.psum_scatter(
        times_transposed(preact_grad, weight_up).astype(jnp.bfloat16),
        "tensor",
        scatter_dimension=0,
        tiled=True,
    ).astype(jnp.float32)
    middle_back, gain_two = rms_back(middle, mid_inverse, gain_table[2], mid_grad)
    middle_grad = upstream + middle_back
    branch_grad, gain_one = rms_back(branch, branch_inverse, gain_table[1], middle_grad)
    branch_full = lax.all_gather(branch_grad.astype(jnp.bfloat16), "tensor", axis=0, tiled=True)
    out_part = transposed_times(attended, branch_full)
    attended_grad = times_transposed(branch_full, weight_out).astype(jnp.bfloat16)
    length = normed_full.shape[0]
    cosine, sine = rotary_tables(length)
    projected = jnp.dot(normed_full, weight_in, preferred_element_type=jnp.float32)
    queries, keys, values = split_heads(projected, inner, cosine, sine)
    query_grad, key_grad, value_grad = attend_back(
        queries, keys, values, segment, logsum, attended_grad
    )
    projected_grad = jnp.concatenate(
        [
            unrotate(query_grad, cosine, sine).reshape(length, inner),
            unrotate(key_grad, cosine, sine).reshape(length, inner),
            value_grad.reshape(length, inner),
        ],
        axis=1,
    ).astype(jnp.bfloat16)
    in_part = transposed_times(normed_full, projected_grad)
    normed_grad = lax.psum_scatter(
        times_transposed(projected_grad, weight_in).astype(jnp.bfloat16),
        "tensor",
        scatter_dimension=0,
        tiled=True,
    ).astype(jnp.float32)
    input_back, gain_zero = rms_back(inputs_float, in_inverse, gain_table[0], normed_grad)
    gain_parts = jnp.stack([gain_zero, gain_one, gain_two, gain_three])
    return (middle_grad + input_back, (in_part, out_part, up_part, down_part), gain_parts)


def take_slot(buffer, slot):
    return lax.dynamic_index_in_dim(buffer, slot, 0, keepdims=False)


def put_slot(buffer, slot, value, valid):
    merged = jnp.where(valid, value, take_slot(buffer, slot))
    return lax.dynamic_update_index_in_dim(buffer, merged, slot, 0)


def per_device(
    inputs, segments, projection_in, projection_out, up_weight, down_weight, norm_gains, cotangent
):
    section = lax.axis_index("section")
    micro = inputs.shape[1]
    rows = inputs.shape[2]
    width = inputs.shape[3]
    inner = projection_out.shape[1]
    up_use, down_use = (up_weight[0], down_weight[0])
    params = (
        projection_in[0].reshape(width, 3 * inner),
        projection_out[0],
        up_use,
        down_use,
        norm_gains[0],
    )
    received = jnp.zeros((rows, width), jnp.bfloat16)
    stored_inputs = jnp.zeros((micro, rows, width), jnp.bfloat16)
    layer_store = jnp.zeros((micro, rows, width), jnp.bfloat16)
    saved = None
    for period in range(micro + 1):
        index = period - section
        valid = (index >= 0) & (index < micro)
        slot = jnp.clip(index, 0, micro - 1)
        own_rows = take_slot(inputs[0], slot)
        layer_in = jnp.where(section == 0, own_rows, received)
        segment = take_slot(segments[0], slot)
        result, kept = layer_forward(layer_in, segment, params)
        result_low = result.astype(jnp.bfloat16)
        if saved is None:
            saved = jax.tree.map(lambda item: jnp.zeros((micro,) + item.shape, item.dtype), kept)
        saved = jax.tree.map(lambda buffer, item: put_slot(buffer, slot, item, valid), saved, kept)
        stored_inputs = put_slot(stored_inputs, slot, layer_in, valid)
        layer_store = put_slot(layer_store, slot, result_low, valid)
        if period < micro:
            received = from_behind(result_low, "section", 1)
    grad_back = jnp.zeros((rows, width), jnp.bfloat16)
    grad_store = jnp.zeros((micro, rows, width), jnp.bfloat16)
    total_in = jnp.zeros((width, 3 * inner), jnp.float32)
    total_out = jnp.zeros((inner, width), jnp.float32)
    total_up = jnp.zeros(up_use.shape, jnp.float32)
    total_down = jnp.zeros(down_use.shape, jnp.float32)
    total_gain = jnp.zeros((4, width), jnp.float32)
    for period in range(micro + 1):
        index = period - (1 - section)
        valid = (index >= 0) & (index < micro)
        slot = jnp.clip(index, 0, micro - 1)
        own_grad = take_slot(cotangent[0], slot)
        upstream = jnp.where(section == 1, own_grad, grad_back).astype(jnp.float32)
        kept = jax.tree.map(lambda buffer: take_slot(buffer, slot), saved)
        layer_in = take_slot(stored_inputs, slot)
        segment = take_slot(segments[0], slot)
        input_grad, weight_parts, gain_parts = layer_backward(
            layer_in, segment, params, kept, upstream
        )
        total_in = total_in + jnp.where(valid, weight_parts[0], 0.0)
        total_out = total_out + jnp.where(valid, weight_parts[1], 0.0)
        total_up = total_up + jnp.where(valid, weight_parts[2], 0.0)
        total_down = total_down + jnp.where(valid, weight_parts[3], 0.0)
        total_gain = total_gain + jnp.where(valid, gain_parts, 0.0)
        grad_low = input_grad.astype(jnp.bfloat16)
        grad_store = put_slot(grad_store, slot, grad_low, valid)
        if period < micro:
            grad_back = from_behind(grad_low, "section", -1)
    total_in, total_out, total_up, total_down = (
        lax.psum(total_in.astype(jnp.bfloat16), "dp").astype(jnp.float32),
        lax.psum(total_out.astype(jnp.bfloat16), "dp").astype(jnp.float32),
        lax.psum(total_up.astype(jnp.bfloat16), "dp").astype(jnp.float32),
        lax.psum(total_down.astype(jnp.bfloat16), "dp").astype(jnp.float32),
    )
    total_gain = lax.psum(total_gain, ("dp", "tensor"))
    return (
        layer_store[None, None],
        grad_store[None, None],
        total_in.reshape(1, width, 3, inner),
        total_out[None],
        total_up[None],
        total_down[None],
        total_gain[None],
    )


BF16 = jnp.bfloat16
F32 = jnp.float32
QROWS = 256
ROW_BLOCK = 256
COLUMNS = 4
ROOMY = pltpu.CompilerParams(vmem_limit_bytes=40 * 1024 * 1024)
WINDOW = 512
BYTES_PER_MICRO = 3400000
COLUMN_DEPTH = 2
TENSOR_DEPTH = 3


def cost(micros):
    return pl.CostEstimate(
        flops=int(micros * 1e9), bytes_accessed=int(micros * BYTES_PER_MICRO), transcendentals=0
    )


def rope_lanes(length, lanes):
    half = HEAD_DIM // 2
    lane = jnp.arange(lanes, dtype=jnp.int32)
    freqs = ROTARY_BASE ** (-2.0 * jnp.arange(half, dtype=F32) / HEAD_DIM)
    angles = jnp.arange(length, dtype=F32)[:, None] * freqs[None, :]
    repeat = lanes // half
    cosine = jnp.tile(jnp.cos(angles), (1, repeat))
    sine = jnp.tile(jnp.sin(angles), (1, repeat))
    first = (lane % HEAD_DIM) < half
    return (cosine, jnp.where(first[None, :], -sine, sine))


def partner(values):
    lanes = values.shape[-1]
    half = HEAD_DIM // 2
    lane = lax.broadcasted_iota(jnp.int32, values.shape, 1)
    return jnp.where(
        (lane % HEAD_DIM) < half,
        pltpu.roll(values, lanes - half, 1),
        pltpu.roll(values, half, 1),
    )


def head_lanes(shape, head):
    lane = lax.broadcasted_iota(jnp.int32, shape, 1)
    return (lane // HEAD_DIM) == head


def nt(left, right):
    return lax.dot_general(left, right, (((1,), (1,)), ((), ())), preferred_element_type=F32)


def nn(left, right):
    return lax.dot_general(left, right, (((1,), (0,)), ((), ())), preferred_element_type=F32)


def allowed_keys(row0, rows, key0, keys, seg_col, seg_row):
    query_at = row0 + lax.broadcasted_iota(jnp.int32, (rows, keys), 0)
    key_at = key0 + lax.broadcasted_iota(jnp.int32, (rows, keys), 1)
    same = seg_col[row0 : row0 + rows, :] == seg_row[:, key0 : key0 + keys]
    return same & (query_at >= key_at)


def windows(length):
    rows = min(QROWS, length)
    for row0 in range(0, length, rows):
        key0 = max(0, row0 - WINDOW)
        yield row0, rows, key0, row0 + rows - key0


def attend_kernel(normed, weight, cosine, sine, seg_col, seg_row, qkv, mixed):
    length = normed.shape[0]
    lanes = mixed.shape[1]
    projected = nn(normed[...], weight[...])
    for part in range(2):
        raw = projected[:, part * lanes : (part + 1) * lanes]
        turned = raw * cosine[...] + partner(raw) * sine[...]
        qkv[:, part * lanes : (part + 1) * lanes] = turned.astype(BF16)
    qkv[:, 2 * lanes :] = projected[:, 2 * lanes :].astype(BF16)
    scale = 1.0 / math.sqrt(HEAD_DIM)
    for row0, rows, key0, keys in windows(length):
        keep = allowed_keys(row0, rows, key0, keys, seg_col, seg_row)
        query = qkv[row0 : row0 + rows, :lanes].astype(F32) * scale
        key = qkv[key0 : key0 + keys, lanes : 2 * lanes]
        value = qkv[key0 : key0 + keys, 2 * lanes :]
        total = jnp.zeros((rows, lanes), F32)
        for head in range(lanes // HEAD_DIM):
            mine = head_lanes((rows, lanes), head)
            scores = nt(jnp.where(mine, query, 0.0).astype(BF16), key)
            scores = jnp.where(keep, scores, NEGATIVE)
            largest = jnp.max(scores, axis=-1, keepdims=True)
            exponent = jnp.exp(scores - largest)
            inverse = 1.0 / jnp.sum(exponent, axis=-1, keepdims=True)
            probs = (exponent * inverse).astype(BF16)
            total = jnp.where(mine, nn(probs, value), total)
        mixed[row0 : row0 + rows, :] = total.astype(BF16)


def attend_forward(normed, weight, tables, lanes, first, count, kept=()):
    length, width = normed.shape
    pieces = weight.shape[1] // (3 * lanes)
    whole = lambda shape: pl.BlockSpec(shape, lambda j: (0, 0))

    def kernel(*refs):
        attend_kernel(*refs[:6], *refs[6 + len(kept) :])

    return pl.pallas_call(
        kernel,
        grid=(count,),
        in_specs=[
            whole((length, width)),
            pl.BlockSpec((width, 3 * lanes), lambda j: (0, first + j)),
            whole((length, lanes)),
            whole((length, lanes)),
            whole((length, 1)),
            whole((1, length)),
        ]
        + [pl.BlockSpec(memory_space=pl.ANY)] * len(kept),
        out_specs=[
            pl.BlockSpec((length, 3 * lanes), lambda j: (0, first + j)),
            pl.BlockSpec((length, lanes), lambda j: (0, first + j)),
        ],
        out_shape=[
            jax.ShapeDtypeStruct((length, pieces * 3 * lanes), BF16),
            jax.ShapeDtypeStruct((length, pieces * lanes), BF16),
        ],
        input_output_aliases={6 + at: at for at in range(len(kept))},
        compiler_params=ROOMY,
        cost_estimate=cost(13),
    )(normed, weight, *tables, *kept)


def tn(left, right):
    return lax.dot_general(left, right, (((0,), (0,)), ((), ())), preferred_element_type=F32)


def attend_back_kernel(
    carried,
    place,
    branch_grad,
    normed,
    qkv,
    attended,
    w_in,
    w_out,
    cosine,
    sine,
    seg_col,
    seg_row,
    *refs,
):
    before, refs = refs[:carried], refs[carried:]
    outs, (normed_grad, grads, key_acc, value_acc, total) = refs[:-5], refs[-5:]
    step = pl.program_id(0)
    length = qkv.shape[0]
    lanes = attended.shape[1]
    scale = 1.0 / math.sqrt(HEAD_DIM)

    @pl.when(step == 0)
    def _():
        total[...] = before[-1][...] if carried else jnp.zeros_like(total)

    key_acc[...] = jnp.zeros_like(key_acc)
    value_acc[...] = jnp.zeros_like(value_acc)
    for row0, rows, key0, keys in windows(length):
        keep = allowed_keys(row0, rows, key0, keys, seg_col, seg_row)
        query = qkv[row0 : row0 + rows, :lanes].astype(F32) * scale
        above = nn(branch_grad[row0 : row0 + rows, :], w_out[...]).astype(BF16).astype(F32)
        key = qkv[key0 : key0 + keys, lanes : 2 * lanes]
        value = qkv[key0 : key0 + keys, 2 * lanes :]
        query_grad = jnp.zeros((rows, lanes), F32)
        key_sum = jnp.zeros((lanes, keys), F32)
        value_sum = jnp.zeros((lanes, keys), F32)
        for head in range(lanes // HEAD_DIM):
            mine = head_lanes((rows, lanes), head)
            query_mine = jnp.where(mine, query, 0.0)
            above_mine = jnp.where(mine, above, 0.0)
            scores = jnp.where(keep, nt(query_mine.astype(BF16), key), NEGATIVE)
            largest = jnp.max(scores, axis=-1, keepdims=True)
            exponent = jnp.exp(scores - largest)
            probs = exponent * (1.0 / jnp.sum(exponent, axis=-1, keepdims=True))
            prob_grad = nt(above_mine.astype(BF16), value)
            centre = jnp.sum(probs * prob_grad, axis=-1, keepdims=True)
            score_grad = (probs * (prob_grad - centre)).astype(BF16)
            query_grad = jnp.where(mine, nn(score_grad, key), query_grad)
            key_sum = key_sum + nn(query_mine.T.astype(BF16), score_grad)
            value_sum = value_sum + nn(above_mine.T.astype(BF16), probs.astype(BF16))
        key_acc[:, key0 : key0 + keys] += key_sum
        value_acc[:, key0 : key0 + keys] += value_sum
        query_grad = query_grad * scale
        near, far = (cosine[row0 : row0 + rows, :], sine[row0 : row0 + rows, :])
        grads[row0 : row0 + rows, :lanes] = (query_grad * near - partner(query_grad) * far).astype(
            BF16
        )
    key_grad = key_acc[...].T
    grads[:, lanes : 2 * lanes] = (key_grad * cosine[...] - partner(key_grad) * sine[...]).astype(
        BF16
    )
    grads[:, 2 * lanes :] = value_acc[...].T.astype(BF16)
    width = normed.shape[1]
    block = width // COLUMNS
    targets = [(out, slice(0, out.shape[0])) for out in outs]
    if len(outs) == 1:
        owners = [place[1] ^ block_mask(at, place[0]) for at in range(COLUMNS)]
        targets = [(outs[0], spot(owner, block)) for owner in owners]
    low = 0
    for out, rows in targets:
        high = low + (block if len(outs) == 1 else out.shape[0])
        out[rows, : 3 * lanes] = tn(normed[:, low:high], grads[...]).astype(BF16)
        out[rows, 3 * lanes :] = tn(branch_grad[:, low:high], attended[...]).astype(BF16)
        low = high
    for row0 in range(0, length, QROWS):
        total[row0 : row0 + QROWS, :] += nt(grads[row0 : row0 + QROWS, :], w_in[...])

    @pl.when(step == pl.num_programs(0) - 1)
    def _():
        normed_grad[...] = total[...].astype(normed_grad.dtype)


def attend_backward(
    place,
    branch_grad,
    normed,
    qkv,
    attended,
    w_in,
    w_out,
    tables,
    lanes,
    heights,
    first,
    count,
    kept=(),
):
    length, width = normed.shape
    pieces = attended.shape[1] // lanes
    last = first + count == pieces
    whole = lambda shape: pl.BlockSpec(shape, lambda j, place: (0, 0))
    by_piece = lambda rows, size: pl.BlockSpec((rows, size), lambda j, place: (0, first + j))
    aliases = {11 + at: at for at in range(len(heights))} if kept else {}
    specs = [pl.BlockSpec(memory_space=pl.ANY)] * len(heights) + [whole((length, width))]
    return placed_call(
        partial(attend_back_kernel, len(kept)),
        place,
        (branch_grad, normed, qkv, attended, w_in, w_out, *tables, *kept),
        [
            whole((length, width)),
            whole((length, width)),
            by_piece(length, 3 * lanes),
            by_piece(length, lanes),
            by_piece(width, 3 * lanes),
            by_piece(width, lanes),
            whole((length, lanes)),
            whole((length, lanes)),
            whole((length, 1)),
            whole((1, length)),
        ]
        + (specs if kept else []),
        [by_piece(rows, 4 * lanes) for rows in heights] + [whole((length, width))],
        [((rows, 4 * lanes * pieces), BF16) for rows in heights]
        + [((length, width), BF16 if last else F32)],
        (count,),
        [
            pltpu.VMEM((length, 3 * lanes), BF16),
            pltpu.VMEM((lanes, length), F32),
            pltpu.VMEM((lanes, length), F32),
            pltpu.VMEM((length, width), F32),
        ],
        aliases,
    )


def outward_kernel(values, weight, out):
    out[...] = nt(values[...], weight[...]).astype(BF16)


def outward(values, weight):
    length, inner = values.shape
    width = weight.shape[0]
    return pl.pallas_call(
        outward_kernel,
        grid=(length // QROWS,),
        in_specs=[
            pl.BlockSpec((QROWS, inner), lambda j: (j, 0)),
            pl.BlockSpec((width, inner), lambda j: (0, 0)),
        ],
        out_specs=pl.BlockSpec((QROWS, width), lambda j: (j, 0)),
        out_shape=jax.ShapeDtypeStruct((length, width), BF16),
        compiler_params=ROOMY,
        cost_estimate=cost(5),
    )(values, weight)


def hidden_kernel(rows_ref, w_up, w_down, hidden, slope, mixed, total):
    step = pl.program_id(0)

    @pl.when(step == 0)
    def _():
        total[...] = jnp.zeros_like(total)

    for row0 in range(0, rows_ref.shape[0], QROWS):
        rows = slice(row0, row0 + QROWS)
        preact = nn(rows_ref[rows, :], w_up[...])
        cumulative = 0.5 + 0.5 * lax.erf(preact * (1.0 / math.sqrt(2.0)))
        density = jnp.exp(preact * preact * -0.5) * (1.0 / math.sqrt(2.0 * math.pi))
        hidden[rows, :] = (preact * cumulative).astype(BF16)
        slope[rows, :] = (cumulative + preact * density).astype(BF16)
        total[rows, :] += nt(hidden[rows, :], w_down[...])

    @pl.when(step == pl.num_programs(0) - 1)
    def _():
        mixed[...] = total[...].astype(BF16)


def hidden_forward(rows, w_up, w_down, block):
    length, width = rows.shape
    size = w_up.shape[1]
    whole = pl.BlockSpec((length, width), lambda j: (0, 0))
    return pl.pallas_call(
        hidden_kernel,
        grid=(size // block,),
        in_specs=[whole] + [pl.BlockSpec((width, block), lambda j: (0, j))] * 2,
        out_specs=[pl.BlockSpec((length, block), lambda j: (0, j))] * 2 + [whole],
        out_shape=[jax.ShapeDtypeStruct((length, size), BF16)] * 2
        + [jax.ShapeDtypeStruct((length, width), BF16)],
        scratch_shapes=[pltpu.VMEM((length, width), F32)],
        compiler_params=ROOMY,
        cost_estimate=cost(19),
    )(rows, w_up, w_down)


def hidden_back_kernel(
    place,
    mixed_grad,
    normed_mid,
    w_up,
    w_down,
    hidden,
    slope,
    *refs,
):
    outs, (mid_grad, preact_grad, total) = refs[:-3], refs[-3:]
    step = pl.program_id(0)

    @pl.when(step == 0)
    def _():
        total[...] = jnp.zeros_like(total)

    for row0 in range(0, mixed_grad.shape[0], QROWS):
        rows = slice(row0, row0 + QROWS)
        back = nn(mixed_grad[rows, :], w_down[...]) * slope[rows, :].astype(F32)
        preact_grad[rows, :] = back.astype(BF16)
        total[rows, :] += nt(preact_grad[rows, :], w_up[...])
    block = mixed_grad.shape[1] // COLUMNS
    for at in range(COLUMNS):
        features = slice(block * at, block * (at + 1))
        if len(outs) == 1:
            owner = place[1] ^ block_mask(at, place[0])
            up, down = outs[0].at[spot(2 * owner, block)], outs[0].at[spot(2 * owner + 1, block)]
        elif at < 3:
            up, down = outs[at].at[:block], outs[at].at[block:]
        else:
            up, down = outs[3:]
        up[...] = tn(normed_mid[:, features], preact_grad[...]).astype(BF16)
        down[...] = tn(mixed_grad[:, features], hidden[...]).astype(BF16)

    @pl.when(step == pl.num_programs(0) - 1)
    def _():
        mid_grad[...] = total[...].astype(BF16)


def hidden_backward(place, mixed_grad, normed_mid, w_up, w_down, hidden, slope, size, heights):
    length, width = mixed_grad.shape
    total = hidden.shape[1]
    whole = pl.BlockSpec((length, width), lambda j, place: (0, 0))
    column = lambda rows: pl.BlockSpec((rows, size), lambda j, place: (0, j))
    return placed_call(
        hidden_back_kernel,
        place,
        (mixed_grad, normed_mid, w_up, w_down, hidden, slope),
        [whole, whole, column(width), column(width), column(length), column(length)],
        [column(rows) for rows in heights] + [whole],
        [((rows, total), BF16) for rows in heights] + [((length, width), BF16)],
        (total // size,),
        [pltpu.VMEM((length, size), BF16), pltpu.VMEM((length, width), F32)],
    )


def rms_row(values):
    return lax.rsqrt(jnp.mean(values * values, axis=-1, keepdims=True) + EPSILON)


def both(left, right):
    block = left.shape[1] // COLUMNS
    turned = [right[:, block * at : block * (at + 1)].astype(F32) for at in (0, 2, 1, 3)]
    return left[...].astype(F32) + jnp.concatenate(turned, axis=1)


def back_row(values, gain, upstream):
    inverse = rms_row(values)
    normed = values * inverse
    scaled = upstream * gain
    back = inverse * (scaled - normed * jnp.mean(scaled * normed, axis=-1, keepdims=True))
    product = upstream * normed
    return back, jnp.sum(product.reshape(-1, 8, product.shape[1]), axis=0)


def gather_gain(out, parts):
    @pl.when(pl.program_id(0) == 0)
    def _():
        out[...] = jnp.zeros_like(out)

    for at, part in enumerate(parts):
        out[at] += part


def row_call(kernel, arrays, tables, outs, gains=0):
    length, width = arrays[0].shape
    by_row = pl.BlockSpec((ROW_BLOCK, width), lambda i: (i, 0))
    out_specs = [by_row] * len(outs)
    out_shape = [jax.ShapeDtypeStruct((length, width), kind) for kind in outs]
    if gains:
        out_specs.append(pl.BlockSpec((gains, 8, width), lambda i: (0, 0, 0)))
        out_shape.append(jax.ShapeDtypeStruct((gains, 8, width), F32))
    return pl.pallas_call(
        kernel,
        grid=(length // ROW_BLOCK,),
        in_specs=[by_row] * len(arrays)
        + [pl.BlockSpec(table.shape, lambda i: (0, 0)) for table in tables],
        out_specs=out_specs,
        out_shape=out_shape,
        compiler_params=ROOMY,
        cost_estimate=cost(6),
    )(*arrays, *tables)


def norm_kernel(values, gain, normed):
    rows = values[...].astype(F32)
    normed[...] = (rows * rms_row(rows) * gain[0:1, :]).astype(BF16)


def middle_row(layer_in, low, other, gain):
    branch = both(low, other)
    return layer_in[...].astype(F32) + branch * rms_row(branch) * gain[1:2, :], branch


def middle_kernel(layer_in, low, other, gain, normed_mid):
    middle, _ = middle_row(layer_in, low, other, gain)
    normed_mid[...] = (middle * rms_row(middle) * gain[2:3, :]).astype(BF16)


def result_kernel(layer_in, low, other, mixed_low, mixed_other, gain, follow, result, normed):
    middle, _ = middle_row(layer_in, low, other, gain)
    mixed = both(mixed_low, mixed_other)
    result[...] = (middle + mixed * rms_row(mixed) * gain[3:4, :]).astype(BF16)
    rows = result[...].astype(F32)
    normed[...] = (rows * rms_row(rows) * follow[0:1, :]).astype(BF16)


def mixed_back_kernel(mixed_low, mixed_other, upstream, gain, mixed_grad, gains):
    back, part = back_row(
        both(mixed_low, mixed_other), gain[3:4, :], upstream[...].astype(F32)
    )
    mixed_grad[...] = back.astype(BF16)
    gather_gain(gains, [part])


def middle_back_kernel(
    layer_in, low, other, upstream, mid_low, mid_other, gain, branch_grad, middle_grad, gains
):
    middle, branch = middle_row(layer_in, low, other, gain)
    back, part_two = back_row(middle, gain[2:3, :], both(mid_low, mid_other))
    total = upstream[...].astype(F32) + back
    middle_grad[...] = total
    back, part_one = back_row(branch, gain[1:2, :], total)
    branch_grad[...] = back.astype(BF16)
    gather_gain(gains, [part_one, part_two])


def input_back_kernel(layer_in, middle_grad, low, other, gain, grad, gains):
    back, part = back_row(layer_in[...].astype(F32), gain[0:1, :], both(low, other))
    grad[...] = (middle_grad[...] + back).astype(BF16)
    gather_gain(gains, [part])


def join_kernel(near, arrived, out):
    out[...] = (near[...].astype(F32) + arrived[...].astype(F32)).astype(BF16)


def join_half(near, arrived, half):
    rows, size = arrived.shape
    return pl.pallas_call(
        join_kernel,
        grid=(4,),
        in_specs=[
            pl.BlockSpec((rows, size // 4), lambda j: (half, j)),
            pl.BlockSpec((rows, size // 4), lambda j: (0, j)),
        ],
        out_specs=pl.BlockSpec((rows, size // 4), lambda j: (half, j)),
        out_shape=jax.ShapeDtypeStruct(near.shape, BF16),
        input_output_aliases={0: 0},
        compiler_params=ROOMY,
        cost_estimate=cost(3.7),
    )(near, arrived)


def total_kernel(own, from_x, from_y, *slots):
    size = own.shape[1] // len(slots)
    for at, slot in enumerate(slots):
        part = slice(size * at, size * (at + 1))
        slot[...] = (
            own[:, part].astype(F32) + from_x[:, part].astype(F32) + from_y[:, part].astype(F32)
        ).astype(BF16)


def total_slots(own, from_x, from_y, count):
    rows, size = own.shape
    step = rows // 4
    by_row = lambda size: pl.BlockSpec((step, size), lambda i: (i, 0))
    return pl.pallas_call(
        total_kernel,
        grid=(4,),
        in_specs=[by_row(size)] * 3,
        out_specs=[by_row(size // count)] * count,
        out_shape=[jax.ShapeDtypeStruct((rows, size // count), BF16)] * count,
        compiler_params=ROOMY,
        cost_estimate=cost(3),
    )(own, from_x, from_y)


def ring(length, by):
    return [(i, (i + by) % length) for i in range(length)]


def other_core(values):
    return lax.ppermute(values, "section", [(0, 1), (1, 0)])


def block_mask(at, section):
    return at ^ (3 * section * ((at ^ (at >> 1)) & 1))


def turn_blocks(values, section, column, axis):
    size = values.shape[axis] // COLUMNS
    blocks = [
        lax.dynamic_slice_in_dim(
            values, (column ^ block_mask(block, section)) * size, size, axis
        )
        for block in range(COLUMNS)
    ]
    return jnp.concatenate(blocks, axis=axis)


def unturn(values, section, column):
    size = values.shape[1] // COLUMNS
    blocks = []
    for block in range(COLUMNS):
        at = block_mask(column ^ block, section)
        blocks.append(lax.dynamic_slice_in_dim(values, at * size, size, 1))
    return jnp.concatenate(blocks, axis=1)


class Channel:
    def __init__(self, depth):
        self.depth = depth
        self.sent = []

    def send(self, values, axes, pairs):
        if len(self.sent) >= self.depth:
            (values,) = hold([values], self.sent[-self.depth])
        got = lax.ppermute(values, axes, pairs)
        self.sent.append(got)
        return got


class Links:
    def __init__(self, count):
        self.count = count
        self.columns = Channel(COLUMN_DEPTH)
        self.tensor = Channel(TENSOR_DEPTH)

    def across(self, values, masks):
        pairs = [
            (core * COLUMNS + at, core * COLUMNS + (at ^ masks[core]))
            for core in range(2)
            for at in range(COLUMNS)
        ]
        return self.columns.send(values, ("section", "dp"), pairs)

    def near(self, values):
        return self.across(values, (1, 2))

    def other(self, values):
        return self.across(values, (2, 1))

    def along(self, values, by):
        return self.tensor.send(values, "tensor", ring(self.count, by % self.count))

    def relay(self, first, second):
        half = first.shape[0] // 2
        return self.other(first[:half]), self.near(second[half:])


def spot(index, size):
    return pl.ds(pl.multiple_of(index * size, size), size)


def placed_call(
    kernel, place, operands, in_specs, out_specs, shapes, grid, scratch=(), aliases=None
):
    return pl.pallas_call(
        kernel,
        grid_spec=pltpu.PrefetchScalarGridSpec(
            num_scalar_prefetch=1,
            grid=grid,
            in_specs=in_specs,
            out_specs=out_specs,
            scratch_shapes=scratch,
        ),
        out_shape=[jax.ShapeDtypeStruct(shape, kind) for shape, kind in shapes],
        input_output_aliases=aliases or {},
        compiler_params=ROOMY,
        cost_estimate=cost(6),
    )(place, *operands)


def whole_spec(shape):
    return pl.BlockSpec(shape, lambda *_: (0,) * len(shape))


def slab_kernel(place, *refs):
    (keep_attn, keep_mlp, send_attn, send_mlp) = refs[8:]
    lanes = refs[1].shape[0] // 2
    hidden = refs[3].shape[0] // 2
    for sources, attn, mlp, core in (
        (refs[:4], keep_attn, keep_mlp, place[0]),
        (refs[4:8], send_attn, send_mlp, 1 - place[0]),
    ):
        w_in, w_out, w_up, w_down = sources
        for part in range(3):
            attn[:, lanes * part : lanes * (part + 1)] = w_in[:, spot(2 * part + core, lanes)]
        attn[:, 3 * lanes :] = w_out[spot(core, lanes), :].T
        mlp[:, :hidden] = w_up[:, spot(core, hidden)]
        mlp[:, hidden:] = w_down[spot(core, hidden), :].T


def make_slabs(place, w_in, w_out, w_up, w_down):
    width = w_in.shape[0]
    rows = width // COLUMNS
    lanes, hidden = (w_out.shape[0] // 2, w_down.shape[0] // 2)
    at = lambda r, place: place[1] ^ block_mask(r, place[0])
    other = lambda r, place: place[1] ^ block_mask(r, 1 - place[0])
    by_row = lambda size, which: pl.BlockSpec((rows, size), lambda r, p: (which(r, p), 0))
    by_column = lambda size, which: pl.BlockSpec((size, rows), lambda r, p: (0, which(r, p)))
    result = lambda size: pl.BlockSpec((rows, size), lambda r, place: (r, 0))
    sizes = (4 * lanes, 2 * hidden, 4 * lanes, 2 * hidden)
    return placed_call(
        slab_kernel,
        place,
        (w_in, w_out, w_up, w_down) * 2,
        [
            make(size, which)
            for which in (at, other)
            for make, size in (
                (by_row, 6 * lanes),
                (by_column, 2 * lanes),
                (by_row, 2 * hidden),
                (by_column, 2 * hidden),
            )
        ],
        [result(size) for size in sizes],
        [((width, size), BF16) for size in sizes],
        (COLUMNS,),
    )


def enter_kernel(place, owned, theirs, out):
    count = 4
    half = owned.shape[0] // count
    block = out.shape[1] // COLUMNS
    for by in range(count):
        source = (place[2] + count - by) % count
        for held, core in ((owned, place[0]), (theirs, 1 - place[0])):
            for at in range(COLUMNS):
                out[spot(2 * source + core, half), block * at : block * (at + 1)] = held[
                    half * by : half * (by + 1), spot(place[1] ^ block_mask(at, place[0]), block)
                ]


def hold(values, *others):
    return lax.optimization_barrier((*values, *others))[: len(values)]


def send_rows(links, blocks, section, tensor, count, *others):
    _, rows, width = blocks.shape
    half = rows // 2
    mine = lambda pack: lax.dynamic_slice(blocks, (pack, section * half, 0), (1, half, width))[0]
    sent = hold([mine((tensor + by) % count) for by in range(count)], *others)
    return [sent[0]] + [links.along(sent[by], by) for by in range(1, count)]


def enter_rows(place, got):
    owned = jnp.concatenate(got)
    theirs = other_core(owned)
    shape = (2 * owned.shape[0], owned.shape[1])
    return placed_call(
        enter_kernel,
        place,
        (owned, theirs),
        [whole_spec(owned.shape)] * 2,
        [whole_spec(shape)],
        [(shape, BF16)],
        (1,),
    )[0]


def leave_kernel(place, *refs):
    out = refs[-1]
    rows = refs[0].shape[0]
    count = out.shape[0] // rows
    block = out.shape[1] // COLUMNS
    for layer in range(2):

        @pl.when(place[0] == layer)
        def _():
            start = count * layer if len(refs) > count + 1 else 0
            for by, held in enumerate(refs[start : start + count]):
                source = (place[2] + count - by) % count
                for at in range(COLUMNS):
                    target = spot(place[1] ^ block_mask(at, layer), block)
                    out[spot(source, rows), target] = held[:, block * at : block * (at + 1)]


def rows_out(values, core, tensor, count, *others):
    length, width = values.shape
    rows = length // count
    blocks = hold(
        [
            lax.dynamic_slice(values, (((tensor + by) % count) * rows, 0), (rows, width))
            for by in range(count)
        ],
        *others,
    )
    pairs = lambda by: [(core * count + i, core * count + (i + by) % count) for i in range(count)]
    return [blocks[0]] + [
        lax.ppermute(blocks[by], ("section", "tensor"), pairs(by)) for by in range(1, count)
    ]


def leave_rows(place, first, second=()):
    rows, width = first[0].shape
    count = len(first)
    shape = (rows * count, width)
    out = placed_call(
        leave_kernel,
        place,
        (*first, *second),
        [whole_spec((rows, width))] * (count + len(second)),
        [whole_spec(shape)],
        [(shape, BF16)],
        (1,),
    )[0]
    return out.reshape(count, rows, width)


def assemble_kernel(layer, pieces, place, keep, theirs, *refs):
    blocks, outs = refs[:pieces], refs[pieces:]
    rows = keep.shape[0] // COLUMNS

    def put(target, size, read):
        start = 0
        for out in outs:
            part = out.shape[1] // 4
            out[target : target + size, read[0] * part : (read[0] + 1) * part] = read[1](
                start, start + part
            )
            start += part

    for mine, held in ((True, keep), (False, theirs)):

        @pl.when((place[0] == layer) == mine)
        def _():
            put(0, keep.shape[0], (0, lambda low, high: held[:, low:high]))

    own, from_x, from_y, far_low, far_high = blocks
    half = far_low.shape[0]
    for at, held in enumerate((own, from_x, from_y)):
        for slot in range(3):
            put(
                rows * at,
                rows,
                (slot + 1, lambda low, high: held[rows * slot : rows * (slot + 1), low:high]),
            )
    step = rows // 2
    for chunk in range(6):
        held, start = (far_low, chunk * step) if chunk < 3 else (far_high, chunk * step - half)
        put(
            3 * rows + (chunk % 2) * step,
            step,
            (chunk // 2 + 1, lambda low, high: held[start : start + step, low:high]),
        )


def gathered_kernel(layer, place, keep, theirs, block, *outs):
    rows = keep.shape[0]
    start = 0
    for out in outs:
        part = out.shape[1] // 4
        for mine, held in ((True, keep), (False, theirs)):

            @pl.when((place[0] == layer) == mine)
            def _():
                out[:, :part] = held[:, start : start + part]

        for slot in range(3):
            out[:, part * (slot + 1) : part * (slot + 2)] = block[
                rows * slot : rows * (slot + 1), start : start + part
            ]
        start += part


def assemble(layer, place, keep, theirs, blocks, parts):
    operands = (keep, theirs, *blocks)
    width, size = keep.shape
    shapes = [((width, 4 * part), BF16) for part in parts]
    if len(blocks) > 1:
        return placed_call(
            partial(assemble_kernel, layer, len(blocks)),
            place,
            operands,
            [whole_spec(item.shape) for item in operands],
            [whole_spec(shape) for shape, _ in shapes],
            shapes,
            (1,),
        )
    rows = width // COLUMNS
    by_row = lambda size: pl.BlockSpec((rows, size), lambda r, place: (r, 0))
    owner = lambda r, place: (place[1] ^ block_mask(r, place[0]), 0)
    return placed_call(
        partial(gathered_kernel, layer),
        place,
        operands,
        [by_row(size), by_row(size), pl.BlockSpec((3 * rows, size), owner)],
        [by_row(4 * part) for part in parts],
        shapes,
        (COLUMNS,),
    )


def add_low(*terms):
    total = terms[0].astype(F32)
    for term in terms[1:]:
        total = total + term.astype(F32)
    return total.astype(BF16)


def finish_kernel(place, *refs):
    sources, (g_in, g_out, g_up, g_down, attn, mlp, sems) = refs[:8], refs[8:]
    step = pl.program_id(0)
    rows = g_in.shape[1]
    lanes = g_out.shape[0] // 2
    hidden = g_down.shape[0] // 2
    core = place[0]

    @pl.when(step == 0)
    def _():
        for layer in range(2):

            @pl.when(core == layer)
            def _():
                own_attn, own_mlp, got_attn, got_mlp = sources[4 * layer : 4 * layer + 4]
                copies = [
                    pltpu.make_async_copy(own_attn, attn.at[layer], sems.at[0]),
                    pltpu.make_async_copy(got_attn, attn.at[1 - layer], sems.at[1]),
                    pltpu.make_async_copy(own_mlp, mlp.at[layer], sems.at[2]),
                    pltpu.make_async_copy(got_mlp, mlp.at[1 - layer], sems.at[3]),
                ]
                for copy in copies:
                    copy.start()
                for copy in copies:
                    copy.wait()

    for half in range(2):
        at = block_mask(place[1] ^ step, half)
        attn_rows = spot(at, rows)
        up_rows = spot(2 * at, rows)
        down_rows = spot(2 * at + 1, rows)
        for part in range(3):
            g_in[part, :, lanes * half : lanes * (half + 1)] = attn[
                half, attn_rows, lanes * part : lanes * (part + 1)
            ].astype(F32)
        g_out[lanes * half : lanes * (half + 1), :] = (
            attn[half, attn_rows, 3 * lanes :].astype(F32).T
        )
        g_up[:, hidden * half : hidden * (half + 1)] = mlp[half, up_rows, :].astype(F32)
        g_down[hidden * half : hidden * (half + 1), :] = mlp[half, down_rows, :].astype(F32).T


def finish(place, sources, lanes, hidden):
    width = sources[0].shape[0]
    rows = width // COLUMNS
    return placed_call(
        finish_kernel,
        place,
        sources,
        [pl.BlockSpec(memory_space=pl.ANY)] * 8,
        [
            pl.BlockSpec((3, rows, 2 * lanes), lambda b, place: (0, b, 0)),
            pl.BlockSpec((2 * lanes, rows), lambda b, place: (0, b)),
            pl.BlockSpec((rows, 2 * hidden), lambda b, place: (b, 0)),
            pl.BlockSpec((2 * hidden, rows), lambda b, place: (0, b)),
        ],
        [
            ((3, width, 2 * lanes), F32),
            ((2 * lanes, width), F32),
            ((width, 2 * hidden), F32),
            ((2 * hidden, width), F32),
        ],
        (COLUMNS,),
        [
            pltpu.VMEM((2, *sources[0].shape), BF16),
            pltpu.VMEM((2, *sources[1].shape), BF16),
            pltpu.SemaphoreType.DMA((4,)),
        ],
    )


class Flow:
    def __init__(self):
        self.table = {}
        self.at = 0

    def plan(self, at, action):
        self.table.setdefault(max(at, self.at), []).append(action)

    def point(self, token, *inputs):
        launched = []
        while self.table.get(self.at):
            launched += self.table[self.at].pop(0)(token)
        self.at += 1
        return hold(inputs, *launched) if launched else inputs

    def drain(self):
        while any(self.table.values()):
            at = min(key for key, actions in self.table.items() if actions)
            self.table[at].pop(0)(None)


def held(values, token):
    return values if token is None else hold(values, token)


def column_stage(links, state, token):
    far_low, far_high = held(state["far"], token)
    to_x = join_half(state["at_x"], far_low, 0)
    to_y = join_half(state["at_y"], far_high, 1)
    state["near"] = (links.near(to_x), links.other(to_y))
    return [to_x, to_y]


def slot_stage(links, states, total, token):
    count = links.count
    if "sum" in states[0]:
        sums = held(tuple(state["sum"] for state in states), token)
        size = sums[0].shape[1] // count
        slots = [
            jnp.concatenate([item[:, size * at : size * (at + 1)] for item in sums])
            for at in range(count)
        ]
    else:
        (state,) = states
        slots = total_slots(state["own"], *held(state["near"], token), count)
    total["slots"] = slots
    total["near"] = links.along(slots[2], -1)
    total["last"] = links.along(slots[3], 1)
    return slots[2:]


def arrive(state, token):
    (state["sum"],) = held((state["sum"],), token)
    return [state["sum"]]


def relay_stage(links, total, token):
    near, total["last"] = held((total["near"], total["last"]), token)
    relayed = add_low(total["slots"][1], near)
    total["near"] = links.along(relayed, -1)
    return [relayed]


def spread_stage(links, total, token):
    came = held((total["near"], total["last"]), token)
    own = add_low(total["slots"][0], *came)
    total["blocks"] = (own, links.near(own), links.other(own))
    return [own]


def far_stage(links, total, token):
    own, from_x, from_y = total["blocks"]
    from_x, from_y = held((from_x, from_y), token)
    total["blocks"] = (own, from_x, from_y, *links.relay(from_x, from_y))
    return []


def per_chip(
    inputs, segments, projection_in, projection_out, up_weight, down_weight, norm_gains, cotangent
):
    section = lax.axis_index("section")
    column = lax.axis_index("dp")
    tensor = lax.axis_index("tensor")
    count = lax.axis_size("tensor")
    width = inputs.shape[3]
    length = inputs.shape[2] * count
    lanes = projection_out.shape[1] // 2
    hidden = up_weight.shape[2] // 2

    place = jnp.stack([section, column, tensor]).astype(jnp.int32)
    keep_attn, keep_mlp, send_attn, send_mlp = make_slabs(
        place,
        projection_in[0].reshape(width, 6 * lanes),
        projection_out[0],
        up_weight[0],
        down_weight[0],
    )
    attn_slabs = (keep_attn, other_core(send_attn))
    mlp_slabs = (keep_mlp, other_core(send_mlp))
    gains_other = other_core(norm_gains[0])
    gains = [
        turn_blocks(
            jnp.where(section == layer, norm_gains[0], gains_other), section, column, 1
        )
        for layer in range(2)
    ]
    rows = width // COLUMNS
    piece = lambda slabs, layer: jnp.where(section == layer, slabs[0][:rows], slabs[1][:rows])
    attn_parts, mlp_parts = ((3 * lanes, lanes), (hidden, hidden))
    links = Links(count)
    everywhere = lambda values: lax.all_gather(values, "dp", axis=0, tiled=True)
    hop = lambda values: (links.along(values, 1), links.along(values, -1))
    segment = lax.dynamic_index_in_dim(segments[0], tensor, 0, keepdims=False)
    cosine, sine = rope_lanes(length, lanes)
    tables = (cosine, sine, segment[:, None], segment[None, :])

    block = min(512, hidden)
    a_first, a_last = hop(piece(attn_slabs, 0))
    (m_own,) = hold([piece(mlp_slabs, 0)], a_first, a_last, cosine, sine, *gains)
    a_second = links.along(a_first, 1)
    m_first, m_last = hop(m_own)
    a_z = jnp.concatenate([a_first, a_second, a_last])
    a_x, a_y = links.near(a_z), links.other(a_z)
    m_second = links.along(m_first, 1)
    got = send_rows(links, inputs[0], section, tensor, count, m_first, m_last)
    a_far = links.relay(a_x, a_y)
    (m_z,) = hold([jnp.concatenate([m_first, m_second, m_last])], *a_far)
    m_all = everywhere(m_z)
    w_in, w_out = assemble(0, place, *attn_slabs, (a_z, a_x, a_y, *a_far), attn_parts)
    got = hold(got, w_out)
    layer_in = enter_rows(place, got)
    (b_own,) = hold([piece(attn_slabs, 1)], *got)
    b_first, b_last = hop(b_own)
    (normed,) = row_call(norm_kernel, [layer_in], [gains[0]], [BF16])
    b_second = links.along(b_first, 1)
    (n_own,) = hold([piece(mlp_slabs, 1)], b_first, b_last)
    qkv, attended = attend_forward(normed, w_in, tables, lanes, 0, 2)
    b_second, b_last = hold((b_second, b_last), attended)
    n_first, n_last = hop(n_own)
    b_z = jnp.concatenate([b_first, b_second, b_last])
    b_all = everywhere(b_z)
    (normed_b,) = hold([normed], b_z, n_own)
    qkv, attended = attend_forward(normed_b, w_in, tables, lanes, 2, 2, (qkv, attended))
    n_first, n_last = hold((n_first, n_last), attended)
    n_second = links.along(n_first, 1)
    (attended_b,) = hold([attended], n_first)
    branch = outward(attended_b, w_out)
    branch = (branch, other_core(branch))
    (normed_mid,) = row_call(middle_kernel, [layer_in, *branch], [gains[0]], [BF16])
    m_all, n_second, n_last = hold((m_all, n_second, n_last), normed_mid)
    w_up, w_down = assemble(0, place, *mlp_slabs, (m_all,), mlp_parts)
    n_z = jnp.concatenate([n_first, n_second, n_last])
    n_all = everywhere(n_z)
    got = send_rows(links, cotangent[0], section, tensor, count, n_z)
    (normed_b,) = hold([normed_mid], n_z)
    hid, slope, mixed = hidden_forward(normed_b, w_up, w_down, block)
    mixed_b, *got = hold([mixed, *got])
    upstream = enter_rows(place, got)
    mixed = (mixed_b, other_core(mixed_b))
    result, normed_next = row_call(
        result_kernel, [layer_in, *branch, *mixed], [gains[0], gains[1]], [BF16, BF16]
    )
    entering = [layer_in, result]
    weights = [(w_in, w_out, w_up, w_down)]
    saved = [(branch, mixed, normed, normed_mid, qkv, attended, hid, slope)]
    b_all, upstream = hold((b_all, upstream), result)
    w_in, w_out = assemble(1, place, *attn_slabs, (b_all,), attn_parts)
    layer_in = result
    normed = normed_next
    left = [rows_out(entering[1], 0, tensor, count, w_in)]
    (normed_b,) = hold([normed], left[0][0])
    qkv, attended = attend_forward(normed_b, w_in, tables, lanes, 0, 4)
    attended_b, *left[0] = hold([attended, *left[0]])
    branch = outward(attended_b, w_out)
    branch = (branch, other_core(branch))
    (normed_mid,) = row_call(middle_kernel, [layer_in, *branch], [gains[1]], [BF16])
    (n_all,) = hold([n_all], normed_mid)
    w_up, w_down = assemble(1, place, *mlp_slabs, (n_all,), mlp_parts)
    hid, slope, mixed = hidden_forward(normed_mid, w_up, w_down, block)
    mixed = (mixed, other_core(mixed))
    result, _ = row_call(
        result_kernel, [layer_in, *branch, *mixed], [gains[1], gains[1]], [BF16, BF16]
    )
    weights.append((w_in, w_out, w_up, w_down))
    saved.append((branch, mixed, normed, normed_mid, qkv, attended, hid, slope))
    flow = Flow()

    def plan_totals(layer, states, steps):
        total = {}
        totals[layer].append(total)
        for at, stage in zip(steps, (slot_stage, relay_stage, spread_stage, far_stage)):
            item = (states, total) if stage is slot_stage else (total,)
            flow.plan(at, partial(stage, links, *item))

    totals = [[], []]
    gain_sums = [None, None]
    input_grads = [None, None]

    def send_grads(token):
        grads = jnp.where(section == 0, *input_grads)
        size = grads.shape[0] // count
        blocks = [
            lax.dynamic_slice_in_dim(grads, ((tensor + by) % count) * size, size, 0)
            for by in range(count)
        ]
        left.append([blocks[0]] + [links.along(blocks[by], by) for by in range(1, count)])
        return []

    running = {"hops": [("tensor", 1), ("tensor", 2), ("dp", 1), ("dp", 2)]}

    def gain_start(token):
        running["sum"] = unturn(jnp.concatenate(gain_sums), section, column)
        running["sent"] = swap_gains()
        return []

    def swap_gains():
        axis, by = running["hops"].pop(0)
        pairs = [(i, i ^ by) for i in range(lax.axis_size(axis))]
        return lax.ppermute(running["sum"], axis, pairs)

    def gain_hop(token):
        running["sum"] = running["sum"] + running["sent"]
        if running["hops"]:
            running["sent"] = swap_gains()
        return []

    def reduction(parts):
        if len(parts) == 1:
            return {"sum": lax.psum_scatter(parts[0], "dp", scatter_dimension=0, tiled=True)}
        own, at_x, at_y, far_low, far_high = parts
        far = (links.other(far_low), links.near(far_high))
        return {"own": own, "at_x": at_x, "at_y": at_y, "far": far}

    for layer in (1, 0):
        layer_in = entering[layer]
        gain = gains[layer]
        w_in, w_out, w_up, w_down = weights[layer]
        branch, mixed, normed, normed_mid, qkv, attended, hid, slope = saved[layer]
        mixed_grad, part_three = row_call(
            mixed_back_kernel, [*mixed, upstream], [gain], [BF16], 1
        )
        (mixed_grad,) = flow.point(mixed_grad, mixed_grad)
        heights = (2 * rows, 2 * rows, 2 * rows, rows, rows) if layer == 0 else (2 * width,)
        *parts, mid_low = hidden_backward(
            place, mixed_grad, normed_mid, w_up, w_down, hid, slope, block, heights
        )
        mlp = reduction(parts)
        (mid_low,) = flow.point(mid_low, mid_low)
        mid_other = other_core(mid_low)
        branch_grad, middle_grad, part_two = row_call(
            middle_back_kernel,
            [layer_in, *branch, upstream, mid_low, mid_other],
            [gain],
            [BF16, F32],
            2,
        )
        if layer == 0:
            flow.plan(7, partial(column_stage, links, mlp))
        (branch_grad,) = flow.point(branch_grad, branch_grad)
        heights = (rows, rows, rows, rows // 2, rows // 2) if layer == 0 else (width,)
        shared = (normed, qkv, attended, w_in, w_out, tables, lanes, heights)
        if layer:
            leaving = rows_out(result, 1, tensor, count, branch_grad)
            (branch_grad,) = hold([branch_grad], leaving[0])
            parts = attend_backward(place, branch_grad, *shared, 0, 2)
            branch_grad, *leaving = hold([branch_grad, *leaving], parts[-1])
            left.append(leaving)
            *parts, normed_low = attend_backward(place, branch_grad, *shared, 2, 2, parts)
        else:
            *parts, normed_low = attend_backward(place, branch_grad, *shared, 0, 4)
        attn = reduction(parts)
        if layer:
            flow.plan(6, partial(arrive, mlp))
            plan_totals(1, [mlp, attn], (7, 8, 12, 15))
        else:
            flow.plan(9, partial(column_stage, links, attn))
            plan_totals(0, [mlp], (10, 13, 18, 22))
            plan_totals(0, [attn], (15, 17, 21, 24))
            flow.plan(11, gain_start)
            for at in (14, 16, 19, 23):
                flow.plan(at, gain_hop)
            flow.plan(20, send_grads)
        (normed_low,) = flow.point(normed_low, normed_low)
        normed_other = other_core(normed_low)
        grad, part_zero = row_call(
            input_back_kernel, [layer_in, middle_grad, normed_low, normed_other], [gain], [BF16], 1
        )
        if layer == 0:
            layer_store = leave_rows(place, left[0], left[1])
            grad = hold([grad], layer_store)[0]
        (grad,) = flow.point(grad, grad)
        gain_sums[layer] = jnp.sum(
            jnp.concatenate([part_zero, part_two, part_three]), axis=1
        )
        input_grads[layer] = grad
        upstream = grad
    flow.drain()
    grad_store = leave_rows(place, left[2])
    gain_total = running["sum"]
    gain_total = jnp.where(section == 0, gain_total[:4], gain_total[4:])
    (both_parts,) = totals[1]
    own, from_x, from_y, far_low, far_high = both_parts["blocks"]
    far_rows = jnp.concatenate([far_low, far_high])
    upper = (own, from_x, from_y, far_rows)
    sums = [
        tuple(jnp.concatenate(total["blocks"]) for total in reversed(totals[0])),
        (
            jnp.concatenate([item[2 * rows :] for item in upper]),
            jnp.concatenate([item[: 2 * rows] for item in upper]),
        ),
    ]
    sources = []
    for layer in range(2):
        got = [lax.ppermute(item, "section", [(1 - layer, layer)]) for item in sums[layer]]
        sources += [*sums[layer], *got]
    in_grad, out_grad, up_grad, down_grad = finish(place, sources, lanes, hidden)
    return (
        layer_store[None, None],
        grad_store[None, None],
        in_grad.transpose(1, 0, 2)[None],
        out_grad[None],
        up_grad[None],
        down_grad[None],
        gain_total[None],
    )


def one_pack_per_chip(mesh):
    return mesh.shape["section"] == 2 and mesh.shape["tensor"] == 4 and mesh.shape["dp"] == 4


def solution(mesh):
    placed = (
        P("dp", None, "tensor", None),
        P("dp", None, None),
        P("section", None, None, "tensor"),
        P("section", "tensor", None),
        P("section", None, "tensor"),
        P("section", "tensor", None),
        P("section", None, None),
        P("dp", None, "tensor", None),
    )
    body = per_chip if one_pack_per_chip(mesh) else per_device
    return jax.shard_map(
        body,
        mesh=mesh,
        in_specs=placed,
        out_specs=(
            P("section", "dp", None, "tensor", None),
            P("section", "dp", None, "tensor", None),
            P("section", None, None, "tensor"),
            P("section", "tensor", None),
            P("section", None, "tensor"),
            P("section", "tensor", None),
            P("section", None, None),
        ),
        check_vma=False,
    )
```

```python
from functools import partial
import math

import jax
import jax.numpy as jnp
from jax import lax
from jax.experimental import pallas as pl
from jax.experimental.pallas import tpu as pltpu
from jax.sharding import PartitionSpec as P

HEAD_DIM = 64
QBLOCK = 512


EPSILON = 1e-05
ROTARY_BASE = 10000.0
NEGATIVE = -1e30


def from_behind(shard, axis, by):
    length = lax.axis_size(axis)
    pairs = [(i, i + by) for i in range(length) if 0 <= i + by < length]
    return lax.ppermute(shard, axis, pairs)


def rms_parts(values, gain):
    inverse = lax.rsqrt(jnp.mean(values * values, axis=-1, keepdims=True) + EPSILON)
    return (values * inverse * gain, inverse)


def rms_back(values, inverse, gain, upstream):
    normed = values * inverse
    scaled = upstream * gain
    back = inverse * (scaled - normed * jnp.mean(scaled * normed, axis=-1, keepdims=True))
    return (back, jnp.sum(upstream * normed, axis=0))


def rotary_tables(length):
    half = HEAD_DIM // 2
    freqs = ROTARY_BASE ** (-2.0 * jnp.arange(half, dtype=jnp.float32) / HEAD_DIM)
    angles = jnp.arange(length, dtype=jnp.float32)[:, None] * freqs[None, :]
    return (jnp.cos(angles)[:, None, :], jnp.sin(angles)[:, None, :])


def rotate(values, cosine, sine):
    half = values.shape[-1] // 2
    first = values[..., :half]
    second = values[..., half:]
    return jnp.concatenate(
        [first * cosine - second * sine, second * cosine + first * sine], axis=-1
    )


def unrotate(upstream, cosine, sine):
    half = upstream.shape[-1] // 2
    first = upstream[..., :half]
    second = upstream[..., half:]
    return jnp.concatenate(
        [first * cosine + second * sine, second * cosine - first * sine], axis=-1
    )


def times_transposed(left, right):
    return lax.dot_general(
        left, right, (((1,), (1,)), ((), ())), preferred_element_type=jnp.float32
    )


def transposed_times(left, right):
    return lax.dot_general(
        left, right, (((0,), (0,)), ((), ())), preferred_element_type=jnp.float32
    )


def split_heads(projected, inner, cosine, sine):
    length = projected.shape[0]
    heads = inner // HEAD_DIM
    queries = rotate(projected[:, :inner].reshape(length, heads, HEAD_DIM), cosine, sine).astype(
        jnp.bfloat16
    )
    keys = rotate(
        projected[:, inner : 2 * inner].reshape(length, heads, HEAD_DIM), cosine, sine
    ).astype(jnp.bfloat16)
    values = projected[:, 2 * inner :].reshape(length, heads, HEAD_DIM).astype(jnp.bfloat16)
    return (queries, keys, values)


def block_scores(query_block, keys, segment_block, position_block, segment, position):
    scale = 1.0 / math.sqrt(HEAD_DIM)
    scores = (
        jnp.einsum("qhd,khd->hqk", query_block, keys, preferred_element_type=jnp.float32) * scale
    )
    allowed = (segment_block[:, None] == segment[None, :]) & (
        position_block[:, None] >= position[None, :]
    )
    return jnp.where(allowed[None], scores, NEGATIVE)


def attend(queries, keys, values, segment):
    length, heads, width = queries.shape
    blocks = length // QBLOCK
    position = jnp.arange(length, dtype=jnp.int32)

    def one_block(pieces):
        query_block, segment_block, position_block = pieces
        scores = block_scores(query_block, keys, segment_block, position_block, segment, position)
        largest = jnp.max(scores, axis=-1, keepdims=True)
        exponent = jnp.exp(scores - largest)
        totals = jnp.sum(exponent, axis=-1, keepdims=True)
        probs = (exponent / totals).astype(jnp.bfloat16)
        mixed = jnp.einsum("hqk,khd->qhd", probs, values, preferred_element_type=jnp.float32)
        return (
            mixed.reshape(QBLOCK, heads * width).astype(jnp.bfloat16),
            (largest + jnp.log(totals))[..., 0],
        )

    attended, logsum = lax.map(
        one_block,
        (
            queries.reshape(blocks, QBLOCK, heads, width),
            segment.reshape(blocks, QBLOCK),
            position.reshape(blocks, QBLOCK),
        ),
    )
    return (attended.reshape(length, heads * width), logsum)


def attend_back(queries, keys, values, segment, logsum, upstream):
    length, heads, width = queries.shape
    blocks = length // QBLOCK
    scale = 1.0 / math.sqrt(width)
    position = jnp.arange(length, dtype=jnp.int32)

    def one_block(carry, pieces):
        key_grad, value_grad = carry
        query_block, segment_block, position_block, logsum_block, upstream_block = pieces
        scores = block_scores(query_block, keys, segment_block, position_block, segment, position)
        probs = jnp.exp(scores - logsum_block[:, :, None])
        upstream_heads = upstream_block.reshape(QBLOCK, heads, width)
        prob_grad = jnp.einsum(
            "qhd,khd->hqk", upstream_heads, values, preferred_element_type=jnp.float32
        )
        score_grad = (
            probs * (prob_grad - jnp.sum(probs * prob_grad, axis=-1, keepdims=True))
        ).astype(jnp.bfloat16)
        query_grad = (
            jnp.einsum("hqk,khd->qhd", score_grad, keys, preferred_element_type=jnp.float32) * scale
        )
        key_grad = (
            key_grad
            + jnp.einsum(
                "hqk,qhd->khd", score_grad, query_block, preferred_element_type=jnp.float32
            )
            * scale
        )
        value_grad = value_grad + jnp.einsum(
            "hqk,qhd->khd",
            probs.astype(jnp.bfloat16),
            upstream_heads,
            preferred_element_type=jnp.float32,
        )
        return ((key_grad, value_grad), query_grad)

    zeros = jnp.zeros((length, heads, width), jnp.float32)
    carried, query_grad = lax.scan(
        one_block,
        (zeros, zeros),
        (
            queries.reshape(blocks, QBLOCK, heads, width),
            segment.reshape(blocks, QBLOCK),
            position.reshape(blocks, QBLOCK),
            logsum,
            upstream.reshape(blocks, QBLOCK, heads * width),
        ),
    )
    return (query_grad.reshape(length, heads, width), carried[0], carried[1])


def layer_forward(layer_in, segment, params):
    weight_in, weight_out, weight_up, weight_down, gain_table = params
    inner = weight_out.shape[0]
    inputs_float = layer_in.astype(jnp.float32)
    normed, _ = rms_parts(inputs_float, gain_table[0])
    normed_full = lax.all_gather(normed.astype(jnp.bfloat16), "tensor", axis=0, tiled=True)
    cosine, sine = rotary_tables(normed_full.shape[0])
    projected = jnp.dot(normed_full, weight_in, preferred_element_type=jnp.float32)
    queries, keys, values = split_heads(projected, inner, cosine, sine)
    attended, logsum = attend(queries, keys, values, segment)
    branch = lax.psum_scatter(
        jnp.dot(attended, weight_out, preferred_element_type=jnp.float32).astype(jnp.bfloat16),
        "tensor",
        scatter_dimension=0,
        tiled=True,
    ).astype(jnp.float32)
    branch_normed, _ = rms_parts(branch, gain_table[1])
    middle = inputs_float + branch_normed
    normed_mid, _ = rms_parts(middle, gain_table[2])
    mid_rows = lax.all_gather(normed_mid.astype(jnp.bfloat16), "tensor", axis=0, tiled=True)
    hidden = jax.nn.gelu(
        jnp.dot(mid_rows, weight_up, preferred_element_type=jnp.float32), approximate=False
    ).astype(jnp.bfloat16)
    mixed = lax.psum_scatter(
        jnp.dot(hidden, weight_down, preferred_element_type=jnp.float32).astype(jnp.bfloat16),
        "tensor",
        scatter_dimension=0,
        tiled=True,
    ).astype(jnp.float32)
    mixed_normed, _ = rms_parts(mixed, gain_table[3])
    return (middle + mixed_normed, (branch, mixed, attended, logsum, normed_full, mid_rows))


def layer_backward(layer_in, segment, params, kept, upstream):
    weight_in, weight_out, weight_up, weight_down, gain_table = params
    inner = weight_out.shape[0]
    branch, mixed, attended, logsum, normed_full, mid_rows = kept
    inputs_float = layer_in.astype(jnp.float32)
    _, in_inverse = rms_parts(inputs_float, gain_table[0])
    branch_normed, branch_inverse = rms_parts(branch, gain_table[1])
    middle = inputs_float + branch_normed
    _, mid_inverse = rms_parts(middle, gain_table[2])
    _, mixed_inverse = rms_parts(mixed, gain_table[3])
    mixed_grad, gain_three = rms_back(mixed, mixed_inverse, gain_table[3], upstream)
    mixed_rows = lax.all_gather(mixed_grad.astype(jnp.bfloat16), "tensor", axis=0, tiled=True)
    preact = jnp.dot(mid_rows, weight_up, preferred_element_type=jnp.float32)
    hidden, gelu_back = jax.vjp(partial(jax.nn.gelu, approximate=False), preact)
    hidden = hidden.astype(jnp.bfloat16)
    down_part = transposed_times(hidden, mixed_rows)
    preact_grad = gelu_back(times_transposed(mixed_rows, weight_down))[0].astype(jnp.bfloat16)
    up_part = transposed_times(mid_rows, preact_grad)
    mid_grad = lax.psum_scatter(
        times_transposed(preact_grad, weight_up).astype(jnp.bfloat16),
        "tensor",
        scatter_dimension=0,
        tiled=True,
    ).astype(jnp.float32)
    middle_back, gain_two = rms_back(middle, mid_inverse, gain_table[2], mid_grad)
    middle_grad = upstream + middle_back
    branch_grad, gain_one = rms_back(branch, branch_inverse, gain_table[1], middle_grad)
    branch_full = lax.all_gather(branch_grad.astype(jnp.bfloat16), "tensor", axis=0, tiled=True)
    out_part = transposed_times(attended, branch_full)
    attended_grad = times_transposed(branch_full, weight_out).astype(jnp.bfloat16)
    length = normed_full.shape[0]
    cosine, sine = rotary_tables(length)
    projected = jnp.dot(normed_full, weight_in, preferred_element_type=jnp.float32)
    queries, keys, values = split_heads(projected, inner, cosine, sine)
    query_grad, key_grad, value_grad = attend_back(
        queries, keys, values, segment, logsum, attended_grad
    )
    projected_grad = jnp.concatenate(
        [
            unrotate(query_grad, cosine, sine).reshape(length, inner),
            unrotate(key_grad, cosine, sine).reshape(length, inner),
            value_grad.reshape(length, inner),
        ],
        axis=1,
    ).astype(jnp.bfloat16)
    in_part = transposed_times(normed_full, projected_grad)
    normed_grad = lax.psum_scatter(
        times_transposed(projected_grad, weight_in).astype(jnp.bfloat16),
        "tensor",
        scatter_dimension=0,
        tiled=True,
    ).astype(jnp.float32)
    input_back, gain_zero = rms_back(inputs_float, in_inverse, gain_table[0], normed_grad)
    gain_parts = jnp.stack([gain_zero, gain_one, gain_two, gain_three])
    return (middle_grad + input_back, (in_part, out_part, up_part, down_part), gain_parts)


def take_slot(buffer, slot):
    return lax.dynamic_index_in_dim(buffer, slot, 0, keepdims=False)


def put_slot(buffer, slot, value, valid):
    merged = jnp.where(valid, value, take_slot(buffer, slot))
    return lax.dynamic_update_index_in_dim(buffer, merged, slot, 0)


def per_device(
    inputs, segments, projection_in, projection_out, up_weight, down_weight, norm_gains, cotangent
):
    section = lax.axis_index("section")
    micro = inputs.shape[1]
    rows = inputs.shape[2]
    width = inputs.shape[3]
    inner = projection_out.shape[1]
    up_use, down_use = (up_weight[0], down_weight[0])
    params = (
        projection_in[0].reshape(width, 3 * inner),
        projection_out[0],
        up_use,
        down_use,
        norm_gains[0],
    )
    received = jnp.zeros((rows, width), jnp.bfloat16)
    stored_inputs = jnp.zeros((micro, rows, width), jnp.bfloat16)
    layer_store = jnp.zeros((micro, rows, width), jnp.bfloat16)
    saved = None
    for period in range(micro + 1):
        index = period - section
        valid = (index >= 0) & (index < micro)
        slot = jnp.clip(index, 0, micro - 1)
        own_rows = take_slot(inputs[0], slot)
        layer_in = jnp.where(section == 0, own_rows, received)
        segment = take_slot(segments[0], slot)
        result, kept = layer_forward(layer_in, segment, params)
        result_low = result.astype(jnp.bfloat16)
        if saved is None:
            saved = jax.tree.map(lambda item: jnp.zeros((micro,) + item.shape, item.dtype), kept)
        saved = jax.tree.map(lambda buffer, item: put_slot(buffer, slot, item, valid), saved, kept)
        stored_inputs = put_slot(stored_inputs, slot, layer_in, valid)
        layer_store = put_slot(layer_store, slot, result_low, valid)
        if period < micro:
            received = from_behind(result_low, "section", 1)
    grad_back = jnp.zeros((rows, width), jnp.bfloat16)
    grad_store = jnp.zeros((micro, rows, width), jnp.bfloat16)
    total_in = jnp.zeros((width, 3 * inner), jnp.float32)
    total_out = jnp.zeros((inner, width), jnp.float32)
    total_up = jnp.zeros(up_use.shape, jnp.float32)
    total_down = jnp.zeros(down_use.shape, jnp.float32)
    total_gain = jnp.zeros((4, width), jnp.float32)
    for period in range(micro + 1):
        index = period - (1 - section)
        valid = (index >= 0) & (index < micro)
        slot = jnp.clip(index, 0, micro - 1)
        own_grad = take_slot(cotangent[0], slot)
        upstream = jnp.where(section == 1, own_grad, grad_back).astype(jnp.float32)
        kept = jax.tree.map(lambda buffer: take_slot(buffer, slot), saved)
        layer_in = take_slot(stored_inputs, slot)
        segment = take_slot(segments[0], slot)
        input_grad, weight_parts, gain_parts = layer_backward(
            layer_in, segment, params, kept, upstream
        )
        total_in = total_in + jnp.where(valid, weight_parts[0], 0.0)
        total_out = total_out + jnp.where(valid, weight_parts[1], 0.0)
        total_up = total_up + jnp.where(valid, weight_parts[2], 0.0)
        total_down = total_down + jnp.where(valid, weight_parts[3], 0.0)
        total_gain = total_gain + jnp.where(valid, gain_parts, 0.0)
        grad_low = input_grad.astype(jnp.bfloat16)
        grad_store = put_slot(grad_store, slot, grad_low, valid)
        if period < micro:
            grad_back = from_behind(grad_low, "section", -1)
    total_in, total_out, total_up, total_down = (
        lax.psum(total_in.astype(jnp.bfloat16), "dp").astype(jnp.float32),
        lax.psum(total_out.astype(jnp.bfloat16), "dp").astype(jnp.float32),
        lax.psum(total_up.astype(jnp.bfloat16), "dp").astype(jnp.float32),
        lax.psum(total_down.astype(jnp.bfloat16), "dp").astype(jnp.float32),
    )
    total_gain = lax.psum(total_gain, ("dp", "tensor"))
    return (
        layer_store[None, None],
        grad_store[None, None],
        total_in.reshape(1, width, 3, inner),
        total_out[None],
        total_up[None],
        total_down[None],
        total_gain[None],
    )


BF16 = jnp.bfloat16
F32 = jnp.float32
QROWS = 256
ROW_BLOCK = 256
COLUMNS = 4
ROOMY = pltpu.CompilerParams(vmem_limit_bytes=40 * 1024 * 1024)
WINDOW = 512
BYTES_PER_MICRO = 3400000
COLUMN_DEPTH = 3
TENSOR_DEPTH = 3


def cost(micros):
    return pl.CostEstimate(
        flops=int(micros * 1e9), bytes_accessed=int(micros * BYTES_PER_MICRO), transcendentals=0
    )


def rope_lanes(length, lanes):
    half = HEAD_DIM // 2
    lane = jnp.arange(lanes, dtype=jnp.int32)
    freqs = ROTARY_BASE ** (-2.0 * jnp.arange(half, dtype=F32) / HEAD_DIM)
    angles = jnp.arange(length, dtype=F32)[:, None] * freqs[None, :]
    repeat = lanes // half
    cosine = jnp.tile(jnp.cos(angles), (1, repeat))
    sine = jnp.tile(jnp.sin(angles), (1, repeat))
    first = (lane % HEAD_DIM) < half
    return (cosine, jnp.where(first[None, :], -sine, sine))


def partner(values):
    lanes = values.shape[-1]
    half = HEAD_DIM // 2
    lane = lax.broadcasted_iota(jnp.int32, values.shape, 1)
    return jnp.where(
        (lane % HEAD_DIM) < half,
        pltpu.roll(values, lanes - half, 1),
        pltpu.roll(values, half, 1),
    )


def head_lanes(shape, head):
    lane = lax.broadcasted_iota(jnp.int32, shape, 1)
    return (lane // HEAD_DIM) == head


def nt(left, right):
    return lax.dot_general(left, right, (((1,), (1,)), ((), ())), preferred_element_type=F32)


def nn(left, right):
    return lax.dot_general(left, right, (((1,), (0,)), ((), ())), preferred_element_type=F32)


def allowed_keys(row0, rows, key0, keys, seg_col, seg_row):
    query_at = row0 + lax.broadcasted_iota(jnp.int32, (rows, keys), 0)
    key_at = key0 + lax.broadcasted_iota(jnp.int32, (rows, keys), 1)
    same = seg_col[row0 : row0 + rows, :] == seg_row[:, key0 : key0 + keys]
    return same & (query_at >= key_at)


def windows(length):
    rows = min(QROWS, length)
    for row0 in range(0, length, rows):
        key0 = max(0, row0 - WINDOW)
        yield row0, rows, key0, row0 + rows - key0


def attend_kernel(normed, weight, cosine, sine, seg_col, seg_row, qkv, mixed):
    length = normed.shape[0]
    lanes = mixed.shape[1]
    projected = nn(normed[...], weight[...])
    for part in range(2):
        raw = projected[:, part * lanes : (part + 1) * lanes]
        turned = raw * cosine[...] + partner(raw) * sine[...]
        qkv[:, part * lanes : (part + 1) * lanes] = turned.astype(BF16)
    qkv[:, 2 * lanes :] = projected[:, 2 * lanes :].astype(BF16)
    scale = 1.0 / math.sqrt(HEAD_DIM)
    for row0, rows, key0, keys in windows(length):
        keep = allowed_keys(row0, rows, key0, keys, seg_col, seg_row)
        query = qkv[row0 : row0 + rows, :lanes].astype(F32) * scale
        key = qkv[key0 : key0 + keys, lanes : 2 * lanes]
        value = qkv[key0 : key0 + keys, 2 * lanes :]
        total = jnp.zeros((rows, lanes), F32)
        for head in range(lanes // HEAD_DIM):
            mine = head_lanes((rows, lanes), head)
            scores = nt(jnp.where(mine, query, 0.0).astype(BF16), key)
            scores = jnp.where(keep, scores, NEGATIVE)
            largest = jnp.max(scores, axis=-1, keepdims=True)
            exponent = jnp.exp(scores - largest)
            inverse = 1.0 / jnp.sum(exponent, axis=-1, keepdims=True)
            probs = (exponent * inverse).astype(BF16)
            total = jnp.where(mine, nn(probs, value), total)
        mixed[row0 : row0 + rows, :] = total.astype(BF16)


def attend_forward(normed, weight, tables, lanes, first, count, kept=()):
    length, width = normed.shape
    pieces = weight.shape[1] // (3 * lanes)
    whole = lambda shape: pl.BlockSpec(shape, lambda j: (0, 0))

    def kernel(*refs):
        attend_kernel(*refs[:6], *refs[6 + len(kept) :])

    return pl.pallas_call(
        kernel,
        grid=(count,),
        in_specs=[
            whole((length, width)),
            pl.BlockSpec((width, 3 * lanes), lambda j: (0, first + j)),
            whole((length, lanes)),
            whole((length, lanes)),
            whole((length, 1)),
            whole((1, length)),
        ]
        + [pl.BlockSpec(memory_space=pl.ANY)] * len(kept),
        out_specs=[
            pl.BlockSpec((length, 3 * lanes), lambda j: (0, first + j)),
            pl.BlockSpec((length, lanes), lambda j: (0, first + j)),
        ],
        out_shape=[
            jax.ShapeDtypeStruct((length, pieces * 3 * lanes), BF16),
            jax.ShapeDtypeStruct((length, pieces * lanes), BF16),
        ],
        input_output_aliases={6 + at: at for at in range(len(kept))},
        compiler_params=ROOMY,
        cost_estimate=cost(13),
    )(normed, weight, *tables, *kept)


def tn(left, right):
    return lax.dot_general(left, right, (((0,), (0,)), ((), ())), preferred_element_type=F32)


def attend_back_kernel(
    carried,
    place,
    branch_grad,
    normed,
    qkv,
    attended,
    w_in,
    w_out,
    cosine,
    sine,
    seg_col,
    seg_row,
    *refs,
):
    before, refs = refs[:carried], refs[carried:]
    outs, (normed_grad, grads, key_acc, value_acc, total) = refs[:-5], refs[-5:]
    step = pl.program_id(0)
    length = qkv.shape[0]
    lanes = attended.shape[1]
    scale = 1.0 / math.sqrt(HEAD_DIM)

    @pl.when(step == 0)
    def _():
        total[...] = before[-1][...] if carried else jnp.zeros_like(total)

    key_acc[...] = jnp.zeros_like(key_acc)
    value_acc[...] = jnp.zeros_like(value_acc)
    for row0, rows, key0, keys in windows(length):
        keep = allowed_keys(row0, rows, key0, keys, seg_col, seg_row)
        query = qkv[row0 : row0 + rows, :lanes].astype(F32) * scale
        above = nn(branch_grad[row0 : row0 + rows, :], w_out[...]).astype(BF16).astype(F32)
        key = qkv[key0 : key0 + keys, lanes : 2 * lanes]
        value = qkv[key0 : key0 + keys, 2 * lanes :]
        query_grad = jnp.zeros((rows, lanes), F32)
        key_sum = jnp.zeros((lanes, keys), F32)
        value_sum = jnp.zeros((lanes, keys), F32)
        for head in range(lanes // HEAD_DIM):
            mine = head_lanes((rows, lanes), head)
            query_mine = jnp.where(mine, query, 0.0)
            above_mine = jnp.where(mine, above, 0.0)
            scores = jnp.where(keep, nt(query_mine.astype(BF16), key), NEGATIVE)
            largest = jnp.max(scores, axis=-1, keepdims=True)
            exponent = jnp.exp(scores - largest)
            probs = exponent * (1.0 / jnp.sum(exponent, axis=-1, keepdims=True))
            prob_grad = nt(above_mine.astype(BF16), value)
            centre = jnp.sum(probs * prob_grad, axis=-1, keepdims=True)
            score_grad = (probs * (prob_grad - centre)).astype(BF16)
            query_grad = jnp.where(mine, nn(score_grad, key), query_grad)
            key_sum = key_sum + nn(query_mine.T.astype(BF16), score_grad)
            value_sum = value_sum + nn(above_mine.T.astype(BF16), probs.astype(BF16))
        key_acc[:, key0 : key0 + keys] += key_sum
        value_acc[:, key0 : key0 + keys] += value_sum
        query_grad = query_grad * scale
        near, far = (cosine[row0 : row0 + rows, :], sine[row0 : row0 + rows, :])
        grads[row0 : row0 + rows, :lanes] = (query_grad * near - partner(query_grad) * far).astype(
            BF16
        )
    key_grad = key_acc[...].T
    grads[:, lanes : 2 * lanes] = (key_grad * cosine[...] - partner(key_grad) * sine[...]).astype(
        BF16
    )
    grads[:, 2 * lanes :] = value_acc[...].T.astype(BF16)
    width = normed.shape[1]
    block = width // COLUMNS
    targets = [(out, slice(0, out.shape[0])) for out in outs]
    if len(outs) == 1:
        owners = [place[1] ^ block_mask(at, place[0]) for at in range(COLUMNS)]
        targets = [(outs[0], spot(owner, block)) for owner in owners]
    low = 0
    for out, rows in targets:
        high = low + (block if len(outs) == 1 else out.shape[0])
        out[rows, : 3 * lanes] = tn(normed[:, low:high], grads[...]).astype(BF16)
        out[rows, 3 * lanes :] = tn(branch_grad[:, low:high], attended[...]).astype(BF16)
        low = high
    for row0 in range(0, length, QROWS):
        total[row0 : row0 + QROWS, :] += nt(grads[row0 : row0 + QROWS, :], w_in[...])

    @pl.when(step == pl.num_programs(0) - 1)
    def _():
        normed_grad[...] = total[...].astype(normed_grad.dtype)


def attend_backward(
    place,
    branch_grad,
    normed,
    qkv,
    attended,
    w_in,
    w_out,
    tables,
    lanes,
    heights,
    first,
    count,
    kept=(),
):
    length, width = normed.shape
    pieces = attended.shape[1] // lanes
    last = first + count == pieces
    whole = lambda shape: pl.BlockSpec(shape, lambda j, place: (0, 0))
    by_piece = lambda rows, size: pl.BlockSpec((rows, size), lambda j, place: (0, first + j))
    aliases = {11 + at: at for at in range(len(heights))} if kept else {}
    specs = [pl.BlockSpec(memory_space=pl.ANY)] * len(heights) + [whole((length, width))]
    return placed_call(
        partial(attend_back_kernel, len(kept)),
        place,
        (branch_grad, normed, qkv, attended, w_in, w_out, *tables, *kept),
        [
            whole((length, width)),
            whole((length, width)),
            by_piece(length, 3 * lanes),
            by_piece(length, lanes),
            by_piece(width, 3 * lanes),
            by_piece(width, lanes),
            whole((length, lanes)),
            whole((length, lanes)),
            whole((length, 1)),
            whole((1, length)),
        ]
        + (specs if kept else []),
        [by_piece(rows, 4 * lanes) for rows in heights] + [whole((length, width))],
        [((rows, 4 * lanes * pieces), BF16) for rows in heights]
        + [((length, width), BF16 if last else F32)],
        (count,),
        [
            pltpu.VMEM((length, 3 * lanes), BF16),
            pltpu.VMEM((lanes, length), F32),
            pltpu.VMEM((lanes, length), F32),
            pltpu.VMEM((length, width), F32),
        ],
        aliases,
    )


def outward_kernel(values, weight, out):
    out[...] = nt(values[...], weight[...]).astype(BF16)


def outward(values, weight):
    length, inner = values.shape
    width = weight.shape[0]
    return pl.pallas_call(
        outward_kernel,
        grid=(length // QROWS,),
        in_specs=[
            pl.BlockSpec((QROWS, inner), lambda j: (j, 0)),
            pl.BlockSpec((width, inner), lambda j: (0, 0)),
        ],
        out_specs=pl.BlockSpec((QROWS, width), lambda j: (j, 0)),
        out_shape=jax.ShapeDtypeStruct((length, width), BF16),
        compiler_params=ROOMY,
        cost_estimate=cost(5),
    )(values, weight)


def hidden_kernel(rows_ref, w_up, w_down, hidden, slope, mixed, total):
    step = pl.program_id(0)

    @pl.when(step == 0)
    def _():
        total[...] = jnp.zeros_like(total)

    for row0 in range(0, rows_ref.shape[0], QROWS):
        rows = slice(row0, row0 + QROWS)
        preact = nn(rows_ref[rows, :], w_up[...])
        cumulative = 0.5 + 0.5 * lax.erf(preact * (1.0 / math.sqrt(2.0)))
        density = jnp.exp(preact * preact * -0.5) * (1.0 / math.sqrt(2.0 * math.pi))
        hidden[rows, :] = (preact * cumulative).astype(BF16)
        slope[rows, :] = (cumulative + preact * density).astype(BF16)
        total[rows, :] += nt(hidden[rows, :], w_down[...])

    @pl.when(step == pl.num_programs(0) - 1)
    def _():
        mixed[...] = total[...].astype(BF16)


def hidden_forward(rows, w_up, w_down, block):
    length, width = rows.shape
    size = w_up.shape[1]
    whole = pl.BlockSpec((length, width), lambda j: (0, 0))
    return pl.pallas_call(
        hidden_kernel,
        grid=(size // block,),
        in_specs=[whole] + [pl.BlockSpec((width, block), lambda j: (0, j))] * 2,
        out_specs=[pl.BlockSpec((length, block), lambda j: (0, j))] * 2 + [whole],
        out_shape=[jax.ShapeDtypeStruct((length, size), BF16)] * 2
        + [jax.ShapeDtypeStruct((length, width), BF16)],
        scratch_shapes=[pltpu.VMEM((length, width), F32)],
        compiler_params=ROOMY,
        cost_estimate=cost(19),
    )(rows, w_up, w_down)


def hidden_back_kernel(
    place,
    mixed_grad,
    normed_mid,
    w_up,
    w_down,
    hidden,
    slope,
    *refs,
):
    outs, (mid_grad, preact_grad, total) = refs[:-3], refs[-3:]
    step = pl.program_id(0)

    @pl.when(step == 0)
    def _():
        total[...] = jnp.zeros_like(total)

    for row0 in range(0, mixed_grad.shape[0], QROWS):
        rows = slice(row0, row0 + QROWS)
        back = nn(mixed_grad[rows, :], w_down[...]) * slope[rows, :].astype(F32)
        preact_grad[rows, :] = back.astype(BF16)
        total[rows, :] += nt(preact_grad[rows, :], w_up[...])
    block = mixed_grad.shape[1] // COLUMNS
    for at in range(COLUMNS):
        features = slice(block * at, block * (at + 1))
        if len(outs) == 1:
            owner = place[1] ^ block_mask(at, place[0])
            up, down = outs[0].at[spot(2 * owner, block)], outs[0].at[spot(2 * owner + 1, block)]
        elif at < 3:
            up, down = outs[at].at[:block], outs[at].at[block:]
        else:
            up, down = outs[3:]
        up[...] = tn(normed_mid[:, features], preact_grad[...]).astype(BF16)
        down[...] = tn(mixed_grad[:, features], hidden[...]).astype(BF16)

    @pl.when(step == pl.num_programs(0) - 1)
    def _():
        mid_grad[...] = total[...].astype(BF16)


def hidden_backward(place, mixed_grad, normed_mid, w_up, w_down, hidden, slope, size, heights):
    length, width = mixed_grad.shape
    total = hidden.shape[1]
    whole = pl.BlockSpec((length, width), lambda j, place: (0, 0))
    column = lambda rows: pl.BlockSpec((rows, size), lambda j, place: (0, j))
    return placed_call(
        hidden_back_kernel,
        place,
        (mixed_grad, normed_mid, w_up, w_down, hidden, slope),
        [whole, whole, column(width), column(width), column(length), column(length)],
        [column(rows) for rows in heights] + [whole],
        [((rows, total), BF16) for rows in heights] + [((length, width), BF16)],
        (total // size,),
        [pltpu.VMEM((length, size), BF16), pltpu.VMEM((length, width), F32)],
    )


def rms_row(values):
    return lax.rsqrt(jnp.mean(values * values, axis=-1, keepdims=True) + EPSILON)


def both(left, right):
    block = left.shape[1] // COLUMNS
    turned = [right[:, block * at : block * (at + 1)].astype(F32) for at in (0, 2, 1, 3)]
    return left[...].astype(F32) + jnp.concatenate(turned, axis=1)


def back_row(values, gain, upstream):
    inverse = rms_row(values)
    normed = values * inverse
    scaled = upstream * gain
    back = inverse * (scaled - normed * jnp.mean(scaled * normed, axis=-1, keepdims=True))
    product = upstream * normed
    return back, jnp.sum(product.reshape(-1, 8, product.shape[1]), axis=0)


def gather_gain(out, parts):
    @pl.when(pl.program_id(0) == 0)
    def _():
        out[...] = jnp.zeros_like(out)

    for at, part in enumerate(parts):
        out[at] += part


def row_call(kernel, arrays, tables, outs, gains=0):
    length, width = arrays[0].shape
    by_row = pl.BlockSpec((ROW_BLOCK, width), lambda i: (i, 0))
    out_specs = [by_row] * len(outs)
    out_shape = [jax.ShapeDtypeStruct((length, width), kind) for kind in outs]
    if gains:
        out_specs.append(pl.BlockSpec((gains, 8, width), lambda i: (0, 0, 0)))
        out_shape.append(jax.ShapeDtypeStruct((gains, 8, width), F32))
    return pl.pallas_call(
        kernel,
        grid=(length // ROW_BLOCK,),
        in_specs=[by_row] * len(arrays)
        + [pl.BlockSpec(table.shape, lambda i: (0, 0)) for table in tables],
        out_specs=out_specs,
        out_shape=out_shape,
        compiler_params=ROOMY,
        cost_estimate=cost(6),
    )(*arrays, *tables)


def norm_kernel(values, gain, normed):
    rows = values[...].astype(F32)
    normed[...] = (rows * rms_row(rows) * gain[0:1, :]).astype(BF16)


def middle_row(layer_in, low, other, gain):
    branch = both(low, other)
    return layer_in[...].astype(F32) + branch * rms_row(branch) * gain[1:2, :], branch


def middle_kernel(layer_in, low, other, gain, normed_mid):
    middle, _ = middle_row(layer_in, low, other, gain)
    normed_mid[...] = (middle * rms_row(middle) * gain[2:3, :]).astype(BF16)


def result_kernel(layer_in, low, other, mixed_low, mixed_other, gain, follow, result, normed):
    middle, _ = middle_row(layer_in, low, other, gain)
    mixed = both(mixed_low, mixed_other)
    result[...] = (middle + mixed * rms_row(mixed) * gain[3:4, :]).astype(BF16)
    rows = result[...].astype(F32)
    normed[...] = (rows * rms_row(rows) * follow[0:1, :]).astype(BF16)


def mixed_back_kernel(mixed_low, mixed_other, upstream, gain, mixed_grad, gains):
    back, part = back_row(
        both(mixed_low, mixed_other), gain[3:4, :], upstream[...].astype(F32)
    )
    mixed_grad[...] = back.astype(BF16)
    gather_gain(gains, [part])


def middle_back_kernel(
    layer_in, low, other, upstream, mid_low, mid_other, gain, branch_grad, middle_grad, gains
):
    middle, branch = middle_row(layer_in, low, other, gain)
    back, part_two = back_row(middle, gain[2:3, :], both(mid_low, mid_other))
    total = upstream[...].astype(F32) + back
    middle_grad[...] = total
    back, part_one = back_row(branch, gain[1:2, :], total)
    branch_grad[...] = back.astype(BF16)
    gather_gain(gains, [part_one, part_two])


def input_back_kernel(layer_in, middle_grad, low, other, gain, grad, gains):
    back, part = back_row(layer_in[...].astype(F32), gain[0:1, :], both(low, other))
    grad[...] = (middle_grad[...] + back).astype(BF16)
    gather_gain(gains, [part])


def join_kernel(near, arrived, out):
    out[...] = (near[...].astype(F32) + arrived[...].astype(F32)).astype(BF16)


def join_half(near, arrived, half):
    rows, size = arrived.shape
    return pl.pallas_call(
        join_kernel,
        grid=(4,),
        in_specs=[
            pl.BlockSpec((rows, size // 4), lambda j: (half, j)),
            pl.BlockSpec((rows, size // 4), lambda j: (0, j)),
        ],
        out_specs=pl.BlockSpec((rows, size // 4), lambda j: (half, j)),
        out_shape=jax.ShapeDtypeStruct(near.shape, BF16),
        input_output_aliases={0: 0},
        compiler_params=ROOMY,
        cost_estimate=cost(3.7),
    )(near, arrived)


def total_kernel(own, from_x, from_y, *slots):
    size = own.shape[1] // len(slots)
    for at, slot in enumerate(slots):
        part = slice(size * at, size * (at + 1))
        slot[...] = (
            own[:, part].astype(F32) + from_x[:, part].astype(F32) + from_y[:, part].astype(F32)
        ).astype(BF16)


def total_slots(own, from_x, from_y, count):
    rows, size = own.shape
    step = rows // 4
    by_row = lambda size: pl.BlockSpec((step, size), lambda i: (i, 0))
    return pl.pallas_call(
        total_kernel,
        grid=(4,),
        in_specs=[by_row(size)] * 3,
        out_specs=[by_row(size // count)] * count,
        out_shape=[jax.ShapeDtypeStruct((rows, size // count), BF16)] * count,
        compiler_params=ROOMY,
        cost_estimate=cost(3),
    )(own, from_x, from_y)


def ring(length, by):
    return [(i, (i + by) % length) for i in range(length)]


def other_core(values):
    return lax.ppermute(values, "section", [(0, 1), (1, 0)])


def block_mask(at, section):
    return at ^ (3 * section * ((at ^ (at >> 1)) & 1))


def turn_blocks(values, section, column, axis):
    size = values.shape[axis] // COLUMNS
    blocks = [
        lax.dynamic_slice_in_dim(
            values, (column ^ block_mask(block, section)) * size, size, axis
        )
        for block in range(COLUMNS)
    ]
    return jnp.concatenate(blocks, axis=axis)


def unturn(values, section, column):
    size = values.shape[1] // COLUMNS
    blocks = []
    for block in range(COLUMNS):
        at = block_mask(column ^ block, section)
        blocks.append(lax.dynamic_slice_in_dim(values, at * size, size, 1))
    return jnp.concatenate(blocks, axis=1)


class Channel:
    def __init__(self, depth):
        self.depth = depth
        self.sent = []

    def send(self, values, axes, pairs):
        if len(self.sent) >= self.depth:
            (values,) = hold([values], self.sent[-self.depth])
        got = lax.ppermute(values, axes, pairs)
        self.sent.append(got)
        return got


class Links:
    def __init__(self, count):
        self.count = count
        self.columns = Channel(COLUMN_DEPTH)
        self.tensor = Channel(TENSOR_DEPTH)

    def across(self, values, masks):
        pairs = [
            (core * COLUMNS + at, core * COLUMNS + (at ^ masks[core]))
            for core in range(2)
            for at in range(COLUMNS)
        ]
        return self.columns.send(values, ("section", "dp"), pairs)

    def near(self, values):
        return self.across(values, (1, 2))

    def other(self, values):
        return self.across(values, (2, 1))

    def along(self, values, by):
        return self.tensor.send(values, "tensor", ring(self.count, by % self.count))

    def relay(self, first, second):
        half = first.shape[0] // 2
        return self.other(first[:half]), self.near(second[half:])


def spot(index, size):
    return pl.ds(pl.multiple_of(index * size, size), size)


def placed_call(
    kernel, place, operands, in_specs, out_specs, shapes, grid, scratch=(), aliases=None
):
    return pl.pallas_call(
        kernel,
        grid_spec=pltpu.PrefetchScalarGridSpec(
            num_scalar_prefetch=1,
            grid=grid,
            in_specs=in_specs,
            out_specs=out_specs,
            scratch_shapes=scratch,
        ),
        out_shape=[jax.ShapeDtypeStruct(shape, kind) for shape, kind in shapes],
        input_output_aliases=aliases or {},
        compiler_params=ROOMY,
        cost_estimate=cost(6),
    )(place, *operands)


def whole_spec(shape):
    return pl.BlockSpec(shape, lambda *_: (0,) * len(shape))


def slab_kernel(place, *refs):
    (keep_attn, keep_mlp, send_attn, send_mlp) = refs[8:]
    lanes = refs[1].shape[0] // 2
    hidden = refs[3].shape[0] // 2
    for sources, attn, mlp, core in (
        (refs[:4], keep_attn, keep_mlp, place[0]),
        (refs[4:8], send_attn, send_mlp, 1 - place[0]),
    ):
        w_in, w_out, w_up, w_down = sources
        for part in range(3):
            attn[:, lanes * part : lanes * (part + 1)] = w_in[:, spot(2 * part + core, lanes)]
        attn[:, 3 * lanes :] = w_out[spot(core, lanes), :].T
        mlp[:, :hidden] = w_up[:, spot(core, hidden)]
        mlp[:, hidden:] = w_down[spot(core, hidden), :].T


def make_slabs(place, w_in, w_out, w_up, w_down):
    width = w_in.shape[0]
    rows = width // COLUMNS
    lanes, hidden = (w_out.shape[0] // 2, w_down.shape[0] // 2)
    at = lambda r, place: place[1] ^ block_mask(r, place[0])
    other = lambda r, place: place[1] ^ block_mask(r, 1 - place[0])
    by_row = lambda size, which: pl.BlockSpec((rows, size), lambda r, p: (which(r, p), 0))
    by_column = lambda size, which: pl.BlockSpec((size, rows), lambda r, p: (0, which(r, p)))
    result = lambda size: pl.BlockSpec((rows, size), lambda r, place: (r, 0))
    sizes = (4 * lanes, 2 * hidden, 4 * lanes, 2 * hidden)
    return placed_call(
        slab_kernel,
        place,
        (w_in, w_out, w_up, w_down) * 2,
        [
            make(size, which)
            for which in (at, other)
            for make, size in (
                (by_row, 6 * lanes),
                (by_column, 2 * lanes),
                (by_row, 2 * hidden),
                (by_column, 2 * hidden),
            )
        ],
        [result(size) for size in sizes],
        [((width, size), BF16) for size in sizes],
        (COLUMNS,),
    )


def enter_kernel(place, owned, theirs, out):
    count = 4
    half = owned.shape[0] // count
    block = out.shape[1] // COLUMNS
    for by in range(count):
        source = (place[2] + count - by) % count
        for held, core in ((owned, place[0]), (theirs, 1 - place[0])):
            for at in range(COLUMNS):
                out[spot(2 * source + core, half), block * at : block * (at + 1)] = held[
                    half * by : half * (by + 1), spot(place[1] ^ block_mask(at, place[0]), block)
                ]


def hold(values, *others):
    return lax.optimization_barrier((*values, *others))[: len(values)]


def send_rows(links, blocks, section, tensor, count, *others):
    _, rows, width = blocks.shape
    half = rows // 2
    mine = lambda pack: lax.dynamic_slice(blocks, (pack, section * half, 0), (1, half, width))[0]
    sent = hold([mine((tensor + by) % count) for by in range(count)], *others)
    return [sent[0]] + [links.along(sent[by], by) for by in range(1, count)]


def enter_rows(place, got):
    owned = jnp.concatenate(got)
    theirs = other_core(owned)
    shape = (2 * owned.shape[0], owned.shape[1])
    return placed_call(
        enter_kernel,
        place,
        (owned, theirs),
        [whole_spec(owned.shape)] * 2,
        [whole_spec(shape)],
        [(shape, BF16)],
        (1,),
    )[0]


def leave_kernel(place, *refs):
    out = refs[-1]
    rows = refs[0].shape[0]
    count = out.shape[0] // rows
    block = out.shape[1] // COLUMNS
    for layer in range(2):

        @pl.when(place[0] == layer)
        def _():
            start = count * layer if len(refs) > count + 1 else 0
            for by, held in enumerate(refs[start : start + count]):
                source = (place[2] + count - by) % count
                for at in range(COLUMNS):
                    target = spot(place[1] ^ block_mask(at, layer), block)
                    out[spot(source, rows), target] = held[:, block * at : block * (at + 1)]


def rows_out(values, core, tensor, count, *others):
    length, width = values.shape
    rows = length // count
    blocks = hold(
        [
            lax.dynamic_slice(values, (((tensor + by) % count) * rows, 0), (rows, width))
            for by in range(count)
        ],
        *others,
    )
    pairs = lambda by: [(core * count + i, core * count + (i + by) % count) for i in range(count)]
    return [blocks[0]] + [
        lax.ppermute(blocks[by], ("section", "tensor"), pairs(by)) for by in range(1, count)
    ]


def leave_rows(place, first, second=()):
    rows, width = first[0].shape
    count = len(first)
    shape = (rows * count, width)
    out = placed_call(
        leave_kernel,
        place,
        (*first, *second),
        [whole_spec((rows, width))] * (count + len(second)),
        [whole_spec(shape)],
        [(shape, BF16)],
        (1,),
    )[0]
    return out.reshape(count, rows, width)


def assemble_kernel(layer, pieces, place, keep, theirs, *refs):
    blocks, outs = refs[:pieces], refs[pieces:]
    rows = keep.shape[0] // COLUMNS

    def put(target, size, read):
        start = 0
        for out in outs:
            part = out.shape[1] // 4
            out[target : target + size, read[0] * part : (read[0] + 1) * part] = read[1](
                start, start + part
            )
            start += part

    for mine, held in ((True, keep), (False, theirs)):

        @pl.when((place[0] == layer) == mine)
        def _():
            put(0, keep.shape[0], (0, lambda low, high: held[:, low:high]))

    own, from_x, from_y, far_low, far_high = blocks
    half = far_low.shape[0]
    for at, held in enumerate((own, from_x, from_y)):
        for slot in range(3):
            put(
                rows * at,
                rows,
                (slot + 1, lambda low, high: held[rows * slot : rows * (slot + 1), low:high]),
            )
    step = rows // 2
    for chunk in range(6):
        held, start = (far_low, chunk * step) if chunk < 3 else (far_high, chunk * step - half)
        put(
            3 * rows + (chunk % 2) * step,
            step,
            (chunk // 2 + 1, lambda low, high: held[start : start + step, low:high]),
        )


def gathered_kernel(layer, place, keep, theirs, block, *outs):
    rows = keep.shape[0]
    start = 0
    for out in outs:
        part = out.shape[1] // 4
        for mine, held in ((True, keep), (False, theirs)):

            @pl.when((place[0] == layer) == mine)
            def _():
                out[:, :part] = held[:, start : start + part]

        for slot in range(3):
            out[:, part * (slot + 1) : part * (slot + 2)] = block[
                rows * slot : rows * (slot + 1), start : start + part
            ]
        start += part


def assemble(layer, place, keep, theirs, blocks, parts):
    operands = (keep, theirs, *blocks)
    width, size = keep.shape
    shapes = [((width, 4 * part), BF16) for part in parts]
    if len(blocks) > 1:
        return placed_call(
            partial(assemble_kernel, layer, len(blocks)),
            place,
            operands,
            [whole_spec(item.shape) for item in operands],
            [whole_spec(shape) for shape, _ in shapes],
            shapes,
            (1,),
        )
    rows = width // COLUMNS
    by_row = lambda size: pl.BlockSpec((rows, size), lambda r, place: (r, 0))
    owner = lambda r, place: (place[1] ^ block_mask(r, place[0]), 0)
    return placed_call(
        partial(gathered_kernel, layer),
        place,
        operands,
        [by_row(size), by_row(size), pl.BlockSpec((3 * rows, size), owner)],
        [by_row(4 * part) for part in parts],
        shapes,
        (COLUMNS,),
    )


def add_low(*terms):
    total = terms[0].astype(F32)
    for term in terms[1:]:
        total = total + term.astype(F32)
    return total.astype(BF16)


def finish_kernel(place, *refs):
    sources, (g_in, g_out, g_up, g_down, attn, mlp, sems) = refs[:8], refs[8:]
    step = pl.program_id(0)
    rows = g_in.shape[1]
    lanes = g_out.shape[0] // 2
    hidden = g_down.shape[0] // 2
    core = place[0]

    @pl.when(step == 0)
    def _():
        for layer in range(2):

            @pl.when(core == layer)
            def _():
                own_attn, own_mlp, got_attn, got_mlp = sources[4 * layer : 4 * layer + 4]
                copies = [
                    pltpu.make_async_copy(own_attn, attn.at[layer], sems.at[0]),
                    pltpu.make_async_copy(got_attn, attn.at[1 - layer], sems.at[1]),
                    pltpu.make_async_copy(own_mlp, mlp.at[layer], sems.at[2]),
                    pltpu.make_async_copy(got_mlp, mlp.at[1 - layer], sems.at[3]),
                ]
                for copy in copies:
                    copy.start()
                for copy in copies:
                    copy.wait()

    for half in range(2):
        at = block_mask(place[1] ^ step, half)
        attn_rows = spot(at, rows)
        up_rows = spot(2 * at, rows)
        down_rows = spot(2 * at + 1, rows)
        for part in range(3):
            g_in[part, :, lanes * half : lanes * (half + 1)] = attn[
                half, attn_rows, lanes * part : lanes * (part + 1)
            ].astype(F32)
        g_out[lanes * half : lanes * (half + 1), :] = (
            attn[half, attn_rows, 3 * lanes :].astype(F32).T
        )
        g_up[:, hidden * half : hidden * (half + 1)] = mlp[half, up_rows, :].astype(F32)
        g_down[hidden * half : hidden * (half + 1), :] = mlp[half, down_rows, :].astype(F32).T


def finish(place, sources, lanes, hidden):
    width = sources[0].shape[0]
    rows = width // COLUMNS
    return placed_call(
        finish_kernel,
        place,
        sources,
        [pl.BlockSpec(memory_space=pl.ANY)] * 8,
        [
            pl.BlockSpec((3, rows, 2 * lanes), lambda b, place: (0, b, 0)),
            pl.BlockSpec((2 * lanes, rows), lambda b, place: (0, b)),
            pl.BlockSpec((rows, 2 * hidden), lambda b, place: (b, 0)),
            pl.BlockSpec((2 * hidden, rows), lambda b, place: (0, b)),
        ],
        [
            ((3, width, 2 * lanes), F32),
            ((2 * lanes, width), F32),
            ((width, 2 * hidden), F32),
            ((2 * hidden, width), F32),
        ],
        (COLUMNS,),
        [
            pltpu.VMEM((2, *sources[0].shape), BF16),
            pltpu.VMEM((2, *sources[1].shape), BF16),
            pltpu.SemaphoreType.DMA((4,)),
        ],
    )


class Flow:
    def __init__(self):
        self.table = {}
        self.at = 0

    def plan(self, at, action):
        self.table.setdefault(max(at, self.at), []).append(action)

    def point(self, token, *inputs):
        launched = []
        while self.table.get(self.at):
            launched += self.table[self.at].pop(0)(token)
        self.at += 1
        return hold(inputs, *launched) if launched else inputs

    def drain(self):
        while any(self.table.values()):
            at = min(key for key, actions in self.table.items() if actions)
            self.table[at].pop(0)(None)


def held(values, token):
    return values if token is None else hold(values, token)


def column_stage(links, state, token):
    far_low, far_high = held(state["far"], token)
    to_x = join_half(state["at_x"], far_low, 0)
    to_y = join_half(state["at_y"], far_high, 1)
    state["near"] = (links.near(to_x), links.other(to_y))
    return [to_x, to_y]


def slot_stage(links, states, total, token):
    count = links.count
    if "sum" in states[0]:
        sums = held(tuple(state["sum"] for state in states), token)
        size = sums[0].shape[1] // count
        slots = [
            jnp.concatenate([item[:, size * at : size * (at + 1)] for item in sums])
            for at in range(count)
        ]
    else:
        (state,) = states
        slots = total_slots(state["own"], *held(state["near"], token), count)
    total["slots"] = slots
    total["near"] = links.along(slots[2], -1)
    total["last"] = links.along(slots[3], 1)
    return slots[2:]


def arrive(state, token):
    (state["sum"],) = held((state["sum"],), token)
    return [state["sum"]]


def relay_stage(links, total, token):
    near, total["last"] = held((total["near"], total["last"]), token)
    relayed = add_low(total["slots"][1], near)
    total["near"] = links.along(relayed, -1)
    return [relayed]


def spread_stage(links, total, token):
    came = held((total["near"], total["last"]), token)
    own = add_low(total["slots"][0], *came)
    total["blocks"] = (own, links.near(own), links.other(own))
    return [own]


def far_stage(links, total, token):
    own, from_x, from_y = total["blocks"]
    from_x, from_y = held((from_x, from_y), token)
    total["blocks"] = (own, from_x, from_y, *links.relay(from_x, from_y))
    return []


def per_chip(
    inputs, segments, projection_in, projection_out, up_weight, down_weight, norm_gains, cotangent
):
    section = lax.axis_index("section")
    column = lax.axis_index("dp")
    tensor = lax.axis_index("tensor")
    count = lax.axis_size("tensor")
    width = inputs.shape[3]
    length = inputs.shape[2] * count
    lanes = projection_out.shape[1] // 2
    hidden = up_weight.shape[2] // 2

    place = jnp.stack([section, column, tensor]).astype(jnp.int32)
    keep_attn, keep_mlp, send_attn, send_mlp = make_slabs(
        place,
        projection_in[0].reshape(width, 6 * lanes),
        projection_out[0],
        up_weight[0],
        down_weight[0],
    )
    attn_slabs = (keep_attn, other_core(send_attn))
    mlp_slabs = (keep_mlp, other_core(send_mlp))
    gains_other = other_core(norm_gains[0])
    gains = [
        turn_blocks(
            jnp.where(section == layer, norm_gains[0], gains_other), section, column, 1
        )
        for layer in range(2)
    ]
    rows = width // COLUMNS
    piece = lambda slabs, layer: jnp.where(section == layer, slabs[0][:rows], slabs[1][:rows])
    attn_parts, mlp_parts = ((3 * lanes, lanes), (hidden, hidden))
    links = Links(count)
    everywhere = lambda values: lax.all_gather(values, "dp", axis=0, tiled=True)
    hop = lambda values: (links.along(values, 1), links.along(values, -1))
    segment = lax.dynamic_index_in_dim(segments[0], tensor, 0, keepdims=False)
    cosine, sine = rope_lanes(length, lanes)
    tables = (cosine, sine, segment[:, None], segment[None, :])

    block = min(512, hidden)
    a_first, a_last = hop(piece(attn_slabs, 0))
    (m_own,) = hold([piece(mlp_slabs, 0)], a_first, a_last, cosine, sine, *gains)
    a_second = links.along(a_first, 1)
    m_first, m_last = hop(m_own)
    a_z = jnp.concatenate([a_first, a_second, a_last])
    a_x, a_y = links.near(a_z), links.other(a_z)
    m_second = links.along(m_first, 1)
    got = send_rows(links, inputs[0], section, tensor, count, m_first, m_last)
    a_far = links.relay(a_x, a_y)
    (m_z,) = hold([jnp.concatenate([m_first, m_second, m_last])], *a_far)
    m_all = everywhere(m_z)
    w_in, w_out = assemble(0, place, *attn_slabs, (a_z, a_x, a_y, *a_far), attn_parts)
    got = hold(got, w_out)
    layer_in = enter_rows(place, got)
    (b_own,) = hold([piece(attn_slabs, 1)], *got)
    b_first, b_last = hop(b_own)
    (normed,) = row_call(norm_kernel, [layer_in], [gains[0]], [BF16])
    b_second = links.along(b_first, 1)
    (n_own,) = hold([piece(mlp_slabs, 1)], b_first, b_last)
    qkv, attended = attend_forward(normed, w_in, tables, lanes, 0, 2)
    b_second, b_last = hold((b_second, b_last), attended)
    n_first, n_last = hop(n_own)
    b_z = jnp.concatenate([b_first, b_second, b_last])
    b_all = everywhere(b_z)
    (normed_b,) = hold([normed], b_z, n_own)
    qkv, attended = attend_forward(normed_b, w_in, tables, lanes, 2, 2, (qkv, attended))
    n_first, n_last = hold((n_first, n_last), attended)
    n_second = links.along(n_first, 1)
    (attended_b,) = hold([attended], n_first)
    branch = outward(attended_b, w_out)
    branch = (branch, other_core(branch))
    (normed_mid,) = row_call(middle_kernel, [layer_in, *branch], [gains[0]], [BF16])
    m_all, n_second, n_last = hold((m_all, n_second, n_last), normed_mid)
    w_up, w_down = assemble(0, place, *mlp_slabs, (m_all,), mlp_parts)
    n_z = jnp.concatenate([n_first, n_second, n_last])
    n_all = everywhere(n_z)
    got = send_rows(links, cotangent[0], section, tensor, count, n_z)
    (normed_b,) = hold([normed_mid], n_z)
    hid, slope, mixed = hidden_forward(normed_b, w_up, w_down, block)
    mixed_b, *got = hold([mixed, *got])
    upstream = enter_rows(place, got)
    mixed = (mixed_b, other_core(mixed_b))
    result, normed_next = row_call(
        result_kernel, [layer_in, *branch, *mixed], [gains[0], gains[1]], [BF16, BF16]
    )
    entering = [layer_in, result]
    weights = [(w_in, w_out, w_up, w_down)]
    saved = [(branch, mixed, normed, normed_mid, qkv, attended, hid, slope)]
    b_all, upstream = hold((b_all, upstream), result)
    w_in, w_out = assemble(1, place, *attn_slabs, (b_all,), attn_parts)
    layer_in = result
    normed = normed_next
    left = [rows_out(entering[1], 0, tensor, count, w_in)]
    (normed_b,) = hold([normed], left[0][0])
    qkv, attended = attend_forward(normed_b, w_in, tables, lanes, 0, 4)
    attended_b, *left[0] = hold([attended, *left[0]])
    branch = outward(attended_b, w_out)
    branch = (branch, other_core(branch))
    (normed_mid,) = row_call(middle_kernel, [layer_in, *branch], [gains[1]], [BF16])
    (n_all,) = hold([n_all], normed_mid)
    w_up, w_down = assemble(1, place, *mlp_slabs, (n_all,), mlp_parts)
    hid, slope, mixed = hidden_forward(normed_mid, w_up, w_down, block)
    mixed = (mixed, other_core(mixed))
    result, _ = row_call(
        result_kernel, [layer_in, *branch, *mixed], [gains[1], gains[1]], [BF16, BF16]
    )
    weights.append((w_in, w_out, w_up, w_down))
    saved.append((branch, mixed, normed, normed_mid, qkv, attended, hid, slope))
    flow = Flow()

    def plan_totals(layer, states, steps):
        total = {}
        totals[layer].append(total)
        for at, stage in zip(steps, (slot_stage, relay_stage, spread_stage, far_stage)):
            item = (states, total) if stage is slot_stage else (total,)
            flow.plan(at, partial(stage, links, *item))

    totals = [[], []]
    gain_sums = [None, None]
    input_grads = [None, None]

    def send_grads(token):
        grads = jnp.where(section == 0, *input_grads)
        size = grads.shape[0] // count
        blocks = [
            lax.dynamic_slice_in_dim(grads, ((tensor + by) % count) * size, size, 0)
            for by in range(count)
        ]
        left.append([blocks[0]] + [links.along(blocks[by], by) for by in range(1, count)])
        return []

    running = {"hops": [("tensor", 1), ("tensor", 2), ("dp", 1), ("dp", 2)]}

    def gain_start(token):
        running["sum"] = unturn(jnp.concatenate(gain_sums), section, column)
        running["sent"] = swap_gains()
        return []

    def swap_gains():
        axis, by = running["hops"].pop(0)
        pairs = [(i, i ^ by) for i in range(lax.axis_size(axis))]
        return lax.ppermute(running["sum"], axis, pairs)

    def gain_hop(token):
        running["sum"] = running["sum"] + running["sent"]
        if running["hops"]:
            running["sent"] = swap_gains()
        return []

    def reduction(parts):
        if len(parts) == 1:
            return {"sum": lax.psum_scatter(parts[0], "dp", scatter_dimension=0, tiled=True)}
        own, at_x, at_y, far_low, far_high = parts
        far = (links.other(far_low), links.near(far_high))
        return {"own": own, "at_x": at_x, "at_y": at_y, "far": far}

    for layer in (1, 0):
        layer_in = entering[layer]
        gain = gains[layer]
        w_in, w_out, w_up, w_down = weights[layer]
        branch, mixed, normed, normed_mid, qkv, attended, hid, slope = saved[layer]
        mixed_grad, part_three = row_call(
            mixed_back_kernel, [*mixed, upstream], [gain], [BF16], 1
        )
        (mixed_grad,) = flow.point(mixed_grad, mixed_grad)
        heights = (2 * rows, 2 * rows, 2 * rows, rows, rows) if layer == 0 else (2 * width,)
        *parts, mid_low = hidden_backward(
            place, mixed_grad, normed_mid, w_up, w_down, hid, slope, block, heights
        )
        mlp = reduction(parts)
        (mid_low,) = flow.point(mid_low, mid_low)
        mid_other = other_core(mid_low)
        branch_grad, middle_grad, part_two = row_call(
            middle_back_kernel,
            [layer_in, *branch, upstream, mid_low, mid_other],
            [gain],
            [BF16, F32],
            2,
        )
        if layer == 0:
            flow.plan(7, partial(column_stage, links, mlp))
        (branch_grad,) = flow.point(branch_grad, branch_grad)
        heights = (rows, rows, rows, rows // 2, rows // 2) if layer == 0 else (width,)
        shared = (normed, qkv, attended, w_in, w_out, tables, lanes, heights)
        if layer:
            leaving = rows_out(result, 1, tensor, count, branch_grad)
            (branch_grad,) = hold([branch_grad], leaving[0])
            parts = attend_backward(place, branch_grad, *shared, 0, 2)
            branch_grad, *leaving = hold([branch_grad, *leaving], parts[-1])
            left.append(leaving)
            *parts, normed_low = attend_backward(place, branch_grad, *shared, 2, 2, parts)
        else:
            *parts, normed_low = attend_backward(place, branch_grad, *shared, 0, 4)
        attn = reduction(parts)
        if layer:
            flow.plan(6, partial(arrive, mlp))
            plan_totals(1, [mlp, attn], (7, 8, 12, 15))
        else:
            flow.plan(9, partial(column_stage, links, attn))
            plan_totals(0, [mlp], (10, 13, 18, 22))
            plan_totals(0, [attn], (15, 17, 21, 24))
            flow.plan(11, gain_start)
            for at in (14, 16, 19, 23):
                flow.plan(at, gain_hop)
            flow.plan(20, send_grads)
        (normed_low,) = flow.point(normed_low, normed_low)
        normed_other = other_core(normed_low)
        grad, part_zero = row_call(
            input_back_kernel, [layer_in, middle_grad, normed_low, normed_other], [gain], [BF16], 1
        )
        if layer == 0:
            layer_store = leave_rows(place, left[0], left[1])
            grad = hold([grad], layer_store)[0]
        (grad,) = flow.point(grad, grad)
        gain_sums[layer] = jnp.sum(
            jnp.concatenate([part_zero, part_two, part_three]), axis=1
        )
        input_grads[layer] = grad
        upstream = grad
    flow.drain()
    grad_store = leave_rows(place, left[2])
    gain_total = running["sum"]
    gain_total = jnp.where(section == 0, gain_total[:4], gain_total[4:])
    (both_parts,) = totals[1]
    own, from_x, from_y, far_low, far_high = both_parts["blocks"]
    far_rows = jnp.concatenate([far_low, far_high])
    upper = (own, from_x, from_y, far_rows)
    sums = [
        tuple(jnp.concatenate(total["blocks"]) for total in reversed(totals[0])),
        (
            jnp.concatenate([item[2 * rows :] for item in upper]),
            jnp.concatenate([item[: 2 * rows] for item in upper]),
        ),
    ]
    sources = []
    for layer in range(2):
        got = [lax.ppermute(item, "section", [(1 - layer, layer)]) for item in sums[layer]]
        sources += [*sums[layer], *got]
    in_grad, out_grad, up_grad, down_grad = finish(place, sources, lanes, hidden)
    return (
        layer_store[None, None],
        grad_store[None, None],
        in_grad.transpose(1, 0, 2)[None],
        out_grad[None],
        up_grad[None],
        down_grad[None],
        gain_total[None],
    )


def one_pack_per_chip(mesh):
    return mesh.shape["section"] == 2 and mesh.shape["tensor"] == 4 and mesh.shape["dp"] == 4


def solution(mesh):
    placed = (
        P("dp", None, "tensor", None),
        P("dp", None, None),
        P("section", None, None, "tensor"),
        P("section", "tensor", None),
        P("section", None, "tensor"),
        P("section", "tensor", None),
        P("section", None, None),
        P("dp", None, "tensor", None),
    )
    body = per_chip if one_pack_per_chip(mesh) else per_device
    return jax.shard_map(
        body,
        mesh=mesh,
        in_specs=placed,
        out_specs=(
            P("section", "dp", None, "tensor", None),
            P("section", "dp", None, "tensor", None),
            P("section", None, None, "tensor"),
            P("section", "tensor", None),
            P("section", None, "tensor"),
            P("section", "tensor", None),
            P("section", None, None),
        ),
        check_vma=False,
    )
```
